32 devices in a mesh: dp: 4 (over x, core), ctx: 8 (over z, y).
Axes of the slice: x: 2, y: 2, z: 4, core: 2. Of those that a mesh axis runs over, the one named last changes fastest.
Arguments:
- queries: bfloat16 [4, 2048, 1024], P('dp', 'ctx'), may hold values from -4.5 to 4.5
- keys: bfloat16 [4, 2048, 1024], P('dp', 'ctx'), may hold values from -4.5 to 4.5
- values: bfloat16 [4, 2048, 1024], P('dp', 'ctx'), may hold values from -6 to 6
- out_grad: bfloat16 [4, 2048, 2048], P('dp', 'ctx'), may hold values from -6 to 6
- chosen: int32 [4, 8], P('dp'), may hold values from -1 to 15, as said below
- proj: bfloat16 [1024, 2048], P('ctx', 'dp'), may hold values from -0.1875 to 0.1875
Outputs:
- attn_out: bfloat16 [4, 2048, 2048], P('dp', 'ctx')
- q_grad: bfloat16 [4, 2048, 1024], P('dp', 'ctx')
- k_grad: bfloat16 [4, 2048, 1024], P('dp', 'ctx')
- v_grad: bfloat16 [4, 2048, 1024], P('dp', 'ctx')
- proj_grad: float32 [1024, 2048], P('ctx', 'dp')
The draws below stay inside these ranges and needn't reach their ends.
Inputs may be any that keep to these rules, and one draw needn't show every extreme that they name: chosen[d, c] is -1 or the index pos // 128 of one of the blocks that ctx index c stores (position spans c and 15 - c, of 1 block each); every sequence has one or more entries that are not -1.
All inputs are finite; a program needn't handle non-finite values.
Results may differ from the reference program's by a relative error of at most 0.023.
Values may be sent and summed in bfloat16 or wider, within the bound.
A program may use at most 192 MiB of HBM per device.

```python
import math
import jax
import jax.numpy as jnp
from jax import lax

DH = 128
DOUT = 2048
BLOCK = 128
SPAN_BLOCKS = 1
HEADS = 8
HD = 1024
TOK_DEV = 256
SEQ = 2048
SLOTS = 1024
N_DP = 4
N_CTX = 8


def base_field(key, salt):
    inner = jax.random.fold_in(key, salt)
    field = jnp.clip(jax.random.normal(inner, (N_DP, SEQ, HD)), -4.5, 4.5)
    return field


def draw_queries(key, part):
    field = base_field(key, 1)
    return field.astype(jnp.bfloat16)


def draw_keys(key, part):
    field = base_field(key, 2)
    return field.astype(jnp.bfloat16)


def draw_chosen(key, part):
    ctx_ids = jnp.arange(N_CTX, dtype=jnp.int32)[None, :]
    pick = jax.random.randint(jax.random.fold_in(key, 11), (N_DP, N_CTX), 0, 2 * SPAN_BLOCKS)
    span_id = jnp.where(pick < SPAN_BLOCKS, ctx_ids, 2 * N_CTX - 1 - ctx_ids)
    block_id = span_id * SPAN_BLOCKS + pick % SPAN_BLOCKS
    active = jax.random.randint(jax.random.fold_in(key, 12), (N_DP, N_CTX), 0, 5) < 3
    forced = jax.random.randint(jax.random.fold_in(key, 13), (N_DP, 1), 0, N_CTX)
    active = active | (ctx_ids == forced)
    return jnp.where(active, block_id, -1).astype(jnp.int32)


def with_spikes(drawn, stream_key, source, target, blocks, factor):
    def block_of(position):
        return (jnp.arange(drawn.shape[position]) // (drawn.shape[position] // blocks)).reshape((-1,) + (1,) * (drawn.ndim - 1 - position))

    first = jax.random.permutation(stream_key, blocks)[block_of(target)]
    second = (block_of(target) + blocks // 2) % blocks
    return jnp.where((block_of(source) == first) | (block_of(source) == second), factor * drawn, drawn)


def shard_levels(own_key, extent, pieces, low, top_value):
    loudness, own = 1.0, jax.random.fold_in(own_key, 6)
    for axis_at, parts in pieces:
        draws = jnp.exp(jax.random.uniform(jax.random.fold_in(own, axis_at), (parts,), jnp.float32, low / len(pieces), top_value / len(pieces)))
        loudness = loudness * jnp.repeat(draws, extent[axis_at] // parts).reshape([-1 if axis == axis_at else 1 for axis in range(len(extent))])
    return loudness


def noise(own_key, dims, spread, reach, shards=(), held_as=jnp.bfloat16):
    loudness = shard_levels(own_key, dims, shards, -0.22, 0.18) if shards else 1.0
    drawn = jax.random.normal(own_key, dims, jnp.float32) * spread * loudness
    return jnp.minimum(jnp.maximum(drawn, -reach), reach).astype(held_as)


def heavy_noise(own_key, dims, width, limit, cuts, heavy, kind=jnp.bfloat16):
    drawn = width * jax.random.normal(own_key, dims, jnp.float32)
    if cuts:
        drawn = drawn * shard_levels(own_key, dims, cuts, -0.22, 0.18)
    return jnp.clip(with_spikes(drawn, jax.random.fold_in(own_key, 3), *heavy), -limit, limit).astype(kind)


def setup_inputs(seed: int = 0) -> dict:
    key_of = jax.random.split(jax.random.key(seed), 7)
    queries = draw_queries(jax.random.fold_in(key_of[6], 71), 0)
    keys = draw_keys(jax.random.fold_in(key_of[6], 71), 0)
    values = noise(key_of[2], (N_DP, SEQ, HD), 1.0, 6.0, ((0, 4), (1, 8)))
    out_grad = heavy_noise(key_of[3], (N_DP, SEQ, DOUT), 1.0, 6.0, ((0, 4), (1, 8)), (0, 2, 4, 2.0))
    chosen = draw_chosen(jax.random.fold_in(key_of[6], 71), 0)
    proj = noise(key_of[5], (HD, DOUT), HD ** -0.5, 0.1875, ((0, 8), (1, 4)))
    return dict(queries=queries, keys=keys, values=values, out_grad=out_grad, chosen=chosen, proj=proj)


def slot_rows(picked):
    half_rows = TOK_DEV // 2
    ctx_ids = jnp.arange(N_CTX, dtype=jnp.int32)
    live_pick = picked >= 0
    safe_pick = jnp.where(live_pick, picked, 0).astype(jnp.int32)
    first_pos = safe_pick * BLOCK
    span_id = first_pos // half_rows
    local_row = jnp.where(span_id == ctx_ids, first_pos % half_rows, half_rows + first_pos % half_rows)
    local_row = jnp.where(live_pick, local_row, 0).astype(jnp.int32)
    offsets = jnp.arange(BLOCK, dtype=jnp.int32)
    src_rows = (ctx_ids[:, None] * TOK_DEV + local_row[:, None] + offsets[None, :]).reshape(SLOTS).astype(jnp.int32)
    slot_pos = (safe_pick[:, None] * BLOCK + offsets[None, :]).reshape(SLOTS).astype(jnp.int32)
    slot_live = jnp.repeat(live_pick, BLOCK)
    return (src_rows, slot_pos, slot_live)

def head_probs(head_q, head_k, allowed):
    scores = jnp.dot(head_q, head_k.T, preferred_element_type=jnp.float32) * (1.0 / math.sqrt(DH))
    masked = jnp.where(allowed, scores, -1e+30)
    row_max = lax.optimization_barrier(jnp.max(masked, axis=1, keepdims=True))
    exp_terms = jnp.where(allowed, jnp.exp(masked - row_max), 0.0)
    return exp_terms / lax.optimization_barrier(jnp.sum(exp_terms, axis=1, keepdims=True))

def head_forward(head_q, head_k, head_v, allowed):
    attn_prob = head_probs(head_q, head_k, allowed)
    return jnp.dot(attn_prob.astype(jnp.bfloat16), head_v, preferred_element_type=jnp.float32).astype(jnp.bfloat16)

def head_backward(head_q, head_k, head_v, head_a, head_g, allowed):
    attn_prob = head_probs(head_q, head_k, allowed)
    prob_b = attn_prob.astype(jnp.bfloat16)
    row_delta = lax.optimization_barrier(jnp.sum(head_g.astype(jnp.float32) * head_a.astype(jnp.float32), axis=1, keepdims=True))
    prob_grad = jnp.dot(head_g, head_v.T, preferred_element_type=jnp.float32)
    score_grad = (attn_prob * (prob_grad - row_delta)).astype(jnp.bfloat16)
    score_scale = 1.0 / math.sqrt(DH)
    grad_q = (jnp.dot(score_grad, head_k, preferred_element_type=jnp.float32) * score_scale).astype(jnp.bfloat16)
    grad_k = (jnp.dot(score_grad.T, head_q, preferred_element_type=jnp.float32) * score_scale).astype(jnp.bfloat16)
    grad_v = jnp.dot(prob_b.T, head_g, preferred_element_type=jnp.float32).astype(jnp.bfloat16)
    return (grad_q, grad_k, grad_v)

def split_heads(block_rows):
    return block_rows.reshape(SLOTS, HEADS, DH).transpose(1, 0, 2)

def join_heads(block_rows):
    return block_rows.transpose(1, 0, 2).reshape(SLOTS, HD)

def one_sequence(seq_query, seq_key, seq_value, seq_grad, picked, proj):
    src_rows, slot_pos, slot_live = slot_rows(picked)
    live_col = slot_live[:, None]
    zero_bf = jnp.zeros((), jnp.bfloat16)
    query_slots = jnp.where(live_col, seq_query[src_rows], zero_bf)
    key_slots = jnp.where(live_col, seq_key[src_rows], zero_bf)
    value_slots = jnp.where(live_col, seq_value[src_rows], zero_bf)
    grad_slots = jnp.where(live_col, seq_grad[src_rows], zero_bf)
    slot_ids = jnp.arange(SLOTS, dtype=jnp.int32)
    allowed = live_col & slot_live[None, :] & (slot_pos[None, :] <= slot_pos[:, None]) | (slot_ids[:, None] == slot_ids[None, :])
    heads_q = split_heads(query_slots)
    heads_k = split_heads(key_slots)
    heads_v = split_heads(value_slots)

    def forward_one(triple):
        return head_forward(triple[0], triple[1], triple[2], allowed)
    attn_heads = lax.map(forward_one, (heads_q, heads_k, heads_v))
    attn = join_heads(attn_heads)
    mixed = jnp.dot(attn, proj, preferred_element_type=jnp.float32).astype(jnp.bfloat16)
    attn_grad = jnp.dot(grad_slots, proj.T, preferred_element_type=jnp.float32).astype(jnp.bfloat16)
    weight_term = jnp.dot(attn.T, grad_slots, preferred_element_type=jnp.float32)

    def backward_one(group):
        return head_backward(group[0], group[1], group[2], group[3], group[4], allowed)
    grad_q, grad_k, grad_v = lax.map(backward_one, (heads_q, heads_k, heads_v, attn_heads, split_heads(attn_grad)))
    out_rows = jnp.zeros((SEQ, DOUT), jnp.bfloat16).at[src_rows].set(mixed)
    blank = jnp.zeros((SEQ, HD), jnp.bfloat16)
    q_rows = blank.at[src_rows].set(join_heads(grad_q))
    k_rows = blank.at[src_rows].set(join_heads(grad_k))
    v_rows = blank.at[src_rows].set(join_heads(grad_v))
    return ((out_rows, q_rows, k_rows, v_rows), weight_term)

def reference(queries, keys, values, out_grad, chosen, proj):

    def scan_step(total, inputs):
        results, weight_term = one_sequence(inputs[0], inputs[1], inputs[2], inputs[3], inputs[4], proj)
        return (total + weight_term, results)
    total, stacked = lax.scan(scan_step, jnp.zeros((HD, DOUT), jnp.float32), (queries, keys, values, out_grad, chosen))
    return (stacked[0], stacked[1], stacked[2], stacked[3], total)
```

```python
import functools
import math

import jax
import jax.numpy as jnp
from jax import lax
from jax.experimental import pallas as pl
from jax.experimental.pallas import tpu as pltpu
from jax.sharding import PartitionSpec as P

BLOCK = 128
FAR = 1 << 30


def dot_nt(a, b):
    return lax.dot_general(a, b, (((1,), (1,)), ((), ())), preferred_element_type=jnp.float32)


def dot_nn(a, b):
    return lax.dot_general(a, b, (((1,), (0,)), ((), ())), preferred_element_type=jnp.float32)


def transposed(a):
    return a.astype(jnp.float32).T.astype(a.dtype)


def block_marks(picked, me, count):
    entry = picked[0, me]
    spans = count // 2
    index = jnp.maximum(entry, 0)
    local = jnp.where(index // spans == me, index % spans, spans + index % spans)
    local = jnp.where(entry >= 0, local, -1)
    return [jnp.where(local == j, 1.0, 0.0) for j in range(count)]


def place_kernel(
    n, dn, count, picked, mix, dq, dkv, w, out, q_out, k_out, v_out, w_out,
    mix_v, dq_v, dkv_v, out_v, q_v, k_v, v_v, in_s, out_s,
):
    loads = [
        pltpu.make_async_copy(mix, mix_v, in_s.at[0]),
        pltpu.make_async_copy(dq, dq_v, in_s.at[1]),
        pltpu.make_async_copy(dkv, dkv_v, in_s.at[2]),
    ]
    for copy in loads:
        copy.start()
    stores = [pltpu.make_async_copy(w, w_out, out_s.at[4])]
    stores[0].start()
    marks = block_marks(picked, lax.axis_index("ctx"), count)
    block, dh, dc = dq.shape[1], dq.shape[2], mix.shape[2]

    def spread(dst, cols, value):
        value = value.astype(jnp.float32)
        for j, mark in enumerate(marks):
            dst[j * block:(j + 1) * block, cols] = (value * mark).astype(dst.dtype)

    def put(src, dst, sem):
        copy = pltpu.make_async_copy(src, dst, sem)
        copy.start()
        stores.append(copy)

    loads[0].wait()
    for d in range(dn):
        spread(out_v, slice(d * dc, (d + 1) * dc), mix_v[d])
    put(out_v, out, out_s.at[0])
    loads[1].wait()
    for h in range(n):
        spread(q_v, slice(h * dh, (h + 1) * dh), dq_v[h])
    put(q_v, q_out, out_s.at[1])
    loads[2].wait()
    for t, (dst, ref) in enumerate(((k_v, k_out), (v_v, v_out))):
        for h in range(n):
            spread(dst, slice(h * dh, (h + 1) * dh), dkv_v[h, t])
        put(dst, ref, out_s.at[2 + t])
    for copy in stores:
        copy.wait()


scope = jax.named_scope


def kernel(
    n, dn, scale,
    picked, q_hbm, k_hbm, v_hbm, g_hbm, proj,
    dq_r, dkv_r, w_out, mix_r,
    q_in, k_in, v_in, g_in, qkv, g, kpos, qkv_r, g_r, proj_r, agp_s, agp_r, ag_s, ag_r, attn_s, attn_r, attn_d, attn_t,
    p_s, k_t, v_t, dq_s, dkv_s, dk_acc, dv_acc, w_s, w_y, w_x, w_m, w_p, mix_s,
    qkv_ss, qkv_rs, g_ss, g_rs, proj_ss, proj_rs, fwd_ss, pass_ss, agp_ss, agp_rs, ag_ss, ag_rs,
    attn_ss, attn_rs, ad_ss, ad_rs, ad_fs, dq_ss, dq_rs, dkv_ss, dkv_rs, w_ss, wy_rs, wx_rs, wm_rs, wp_rs, mix_ss, mix_rs,
    loc,
):
    me = lax.axis_index("ctx")
    md = lax.axis_index("dp")
    bf16 = jnp.bfloat16
    block, dh = qkv.shape[2], qkv.shape[3]
    dc = proj.shape[1]
    slots = n * block
    width = 2 * block
    rows = n // 2
    half = rows // 2

    def ctx_copy(src, dst, ss, rs, peer):
        return pltpu.make_async_remote_copy(
            src_ref=src, dst_ref=dst, send_sem=ss, recv_sem=rs,
            device_id={"ctx": peer}, device_id_type=pl.DeviceIdType.MESH)

    def dp_copy(src, dst, ss, rs, peer):
        return pltpu.make_async_remote_copy(
            src_ref=src, dst_ref=dst, send_sem=ss, recv_sem=rs,
            device_id={"dp": peer}, device_id_type=pl.DeviceIdType.MESH)

    ctx_peers = [lax.rem(me + s, n) for s in range(1, n)]
    dp_peers = [lax.rem(md + s, dn) for s in range(1, dn)]

    barrier = pltpu.get_barrier_semaphore()
    for peer in ctx_peers:
        pl.semaphore_signal(barrier, inc=1, device_id={"ctx": peer}, device_id_type=pl.DeviceIdType.MESH)
    for peer in dp_peers:
        pl.semaphore_signal(barrier, inc=1, device_id={"dp": peer}, device_id_type=pl.DeviceIdType.MESH)

    own_proj = pltpu.make_async_copy(proj, proj_r.at[me], loc.at[2])
    loads = [
        pltpu.make_async_copy(src, dst, loc.at[6 + t])
        for t, (src, dst) in enumerate(((g_hbm, g_in), (q_hbm, q_in), (k_hbm, k_in), (v_hbm, v_in)))]
    for copy in loads:
        copy.start()
    own_proj.start()
    marks = block_marks(picked, me, q_in.shape[0] // block)

    def chosen_rows(ref, low, high):
        total = None
        for j, mark in enumerate(marks):
            term = ref[j * block:(j + 1) * block, low:high].astype(jnp.float32) * mark
            total = term if total is None else total + term
        return total.astype(bf16)

    row = me // 2
    side = lax.rem(me, 2)
    pair = me + 1 - 2 * side
    own_base = (row // half) * half
    far_base = half - own_base

    def near(s):
        return own_base + lax.rem(row + s, half)

    def across(s):
        return far_base + lax.rem(row + s, half)

    mates = [near(s) for s in range(1, half)]
    partner = across(0)
    mate_partners = [across(s) for s in range(1, half)]

    with scope("A_load"):
        loads[0].wait()
        for j in range(dn):
            g[j] = chosen_rows(g_in, j * dc, (j + 1) * dc)
        g_r[md] = g[md]
        for t, ref in enumerate((q_in, k_in, v_in)):
            loads[1 + t].wait()
            for h in range(n):
                qkv[h, t] = chosen_rows(ref, h * dh, (h + 1) * dh)
        qkv_r[me] = qkv[me]
    with scope("B_barrier"):
        pl.semaphore_wait(barrier, n - 1 + dn - 1)
    sends = []

    def go(copy):
        copy.start()
        sends.append(copy)

    for a in [partner] + mates:
        peer = 2 * a + side
        go(ctx_copy(proj, proj_r.at[me], proj_ss.at[peer], proj_rs.at[me], peer))
    go(ctx_copy(proj, proj_r.at[me], proj_ss.at[pair], proj_rs.at[me], pair))
    for peer in dp_peers:
        go(dp_copy(g.at[peer], g_r.at[md], g_ss.at[peer], g_rs.at[md], peer))

    def send_qkv(peers):
        for peer in peers:
            go(ctx_copy(qkv.at[peer], qkv_r.at[me], qkv_ss.at[peer], qkv_rs.at[me], peer))

    far_heads = [2 * across(s) + (side if t == 0 else 1 - side) for s in range(half) for t in range(2)]
    near_heads = [2 * a + (side if t == 0 else 1 - side) for a in mates for t in range(2)] + [pair]
    early_far = len(far_heads) // 2
    send_qkv(far_heads[:early_far])

    down = lax.broadcasted_iota(jnp.int32, (block, block), 0)
    for j in range(n):
        entry = picked[0, j]
        kpos[j * block:(j + 1) * block] = down + jnp.where(entry >= 0, entry * block, FAR)

    def ctx_arrived(buf, ss, rs, peer):
        ctx_copy(buf.at[peer], buf.at[peer], ss.at[peer], rs.at[peer], peer).wait_recv()

    def dp_arrived(buf, ss, rs, peer):
        dp_copy(buf.at[peer], buf.at[peer], ss.at[peer], rs.at[peer], peer).wait_recv()

    def proj_arrived(h):
        ctx_arrived(proj_r, proj_ss, proj_rs, h)

    def pass_pair(h):
        go(ctx_copy(proj_r.at[h], proj_r.at[h], fwd_ss.at[h], proj_rs.at[h], pair))

    with scope("C_waitmate"):
        for a in mates:
            proj_arrived(2 * a + side)
            pass_pair(2 * a + side)
    with scope("D_waitpartner"):
        ph = 2 * partner + side
        proj_arrived(ph)
        for a in mates:
            peer = 2 * a + side
            go(ctx_copy(proj_r.at[ph], proj_r.at[ph], pass_ss.at[peer], proj_rs.at[ph], peer))
        pass_pair(ph)
    send_qkv(far_heads[early_far:] + near_heads)
    own_proj.wait()
    with scope("E_waitg"):
        for peer in dp_peers:
            dp_arrived(g_r, g_ss, g_rs, peer)

    def part(h):
        out = dot_nt(g_r[...].reshape(dn * block, dc), proj_r[h]).astype(bf16)
        agp_s[h] = out.reshape(dn, block, dh)
        for peer in dp_peers:
            go(dp_copy(agp_s.at[h, peer], agp_r.at[h, md], agp_ss.at[h, peer], agp_rs.at[h, md], peer))

    def finish(h):
        total = agp_s[h, md].astype(jnp.float32)
        for peer in dp_peers:
            dp_copy(agp_r.at[h, peer], agp_r.at[h, peer], agp_ss.at[h, peer], agp_rs.at[h, peer], peer).wait_recv()
            total = total + agp_r[h, peer].astype(jnp.float32)
        ag_s[h] = total.astype(bf16)
        if h is me:
            ag_r[me] = ag_s[me]
        else:
            go(ctx_copy(ag_s.at[h], ag_r.at[me], ag_ss.at[h], ag_rs.at[me], h))

    first = [2 * partner + side] + [2 * a + side for a in mates]
    second = [2 * a + side for a in mate_partners]
    cross = [2 * a + 1 - side for a in mates + [partner]]
    heads = [(h, False) for h in first] + [(me, False), (pair, True)]
    heads += [(h, True) for h in cross] + [(h, True) for h in second]
    heads += [(2 * a + 1 - side, True) for a in mate_partners]
    lag = 2
    for k, (h, pending) in enumerate(heads):
        if pending:
            with scope("F_waitproj"):
                proj_arrived(h)
        if any(h is other for other in second):
            pass_pair(h)
        with scope("G_part"):
            part(h)
        if k >= lag:
            with scope("H_finish"):
                finish(heads[k - lag][0])
    for h, _ in heads[-lag:]:
        with scope("H_finish"):
            finish(h)

    with scope("I_waitqkv"):
        for peer in ctx_peers:
            ctx_arrived(qkv_r, qkv_ss, qkv_rs, peer)
    k_t[...] = transposed(qkv_r[:, 1].reshape(slots, dh))
    v_t[...] = transposed(qkv_r[:, 2].reshape(slots, dh))

    def ordered(k):
        late = k // half
        return far_base * (1 - late) + own_base * late + lax.rem(row + k + late, half)

    def send_pair(i, src, dst, ss, rs, own_sem):
        for t in range(2):
            peer = 2 * i + t

            @pl.when(peer != me)
            def _():
                ctx_copy(src.at[peer], dst.at[me], ss.at[peer], rs.at[me], peer).start()

            @pl.when(peer == me)
            def _():
                pltpu.make_async_copy(src.at[peer], dst.at[peer], own_sem).start()

    def forward(k, carry):
        i = ordered(k)
        q = qkv_r[pl.ds(2 * i, 2), 0].reshape(width, dh)
        keys = qkv_r[:, 1].reshape(slots, dh)
        scores = dot_nt(keys, q) * scale
        key_pos = kpos[...]
        key_pos = jnp.concatenate([key_pos, key_pos], axis=1)
        same = lax.broadcasted_iota(jnp.int32, (slots, width), 0) == (
            lax.broadcasted_iota(jnp.int32, (slots, width), 1) + i * width)
        lane = lax.broadcasted_iota(jnp.int32, (1, width), 1)
        first, second = picked[0, 2 * i], picked[0, 2 * i + 1]
        first = jnp.where(first >= 0, first * block, -FAR)
        second = jnp.where(second >= 0, (second - 1) * block, -FAR)
        query_pos = lane + jnp.where(lane < block, first, second)
        scores = jnp.where((key_pos <= query_pos) | same, scores, -1e30)
        e = jnp.exp(scores - jnp.max(scores, axis=0, keepdims=True))
        p = (e * (1.0 / jnp.sum(e, axis=0, keepdims=True))).astype(bf16)
        p_s[i] = p
        a_t = dot_nn(v_t[...], p)
        attn_t[i] = a_t.astype(bf16)
        attn_s[pl.ds(2 * i, 2)] = a_t.T.astype(bf16).reshape(2, block, dh)
        send_pair(i, attn_s, attn_r, attn_ss, attn_rs, loc.at[3])
        return carry

    with scope("J_forward"):
        lax.fori_loop(0, rows, forward, 0)

    dk_acc[...] = jnp.zeros_like(dk_acc)
    dv_acc[...] = jnp.zeros_like(dv_acc)

    def backward(k, carry):
        i = ordered(k)
        with scope("K_waitag"):
            for t in range(2):
                peer = 2 * i + t

                @pl.when(peer != me)
                def _():
                    ctx_arrived(ag_r, ag_ss, ag_rs, peer)
        q = qkv_r[pl.ds(2 * i, 2), 0].reshape(width, dh)
        v = qkv_r[:, 2].reshape(slots, dh)
        da = ag_r[pl.ds(2 * i, 2)].reshape(width, dh)
        delta = jnp.sum(da.astype(jnp.float32).T * attn_t[i].astype(jnp.float32), axis=0, keepdims=True)
        p = p_s[i]
        ds = (p.astype(jnp.float32) * (dot_nt(v, da) - delta)).astype(bf16)
        dq_t = dot_nn(k_t[...], ds) * scale
        dq_s[pl.ds(2 * i, 2)] = dq_t.T.astype(bf16).reshape(2, block, dh)
        send_pair(i, dq_s, dq_r, dq_ss, dq_rs, loc.at[4])
        dk_acc[...] += dot_nn(ds, q)
        dv_acc[...] += dot_nn(p, da)
        return carry

    twin = md + 1 - 2 * lax.rem(md, 2)
    dp_far = [lax.rem(md + 2 * s, dn) for s in range(1, dn // 2)]
    groups = [pl.ds(2 * far_base, rows), pl.ds(2 * own_base, rows)]
    own_attn = []

    def spread_attn(t):
        part_of = groups[t]
        for peer in dp_far + [twin]:
            go(dp_copy(attn_r.at[part_of], attn_d.at[md, part_of], ad_ss.at[t, peer], ad_rs.at[t, md], peer))
        copy = pltpu.make_async_copy(attn_r.at[part_of], attn_d.at[md, part_of], loc.at[t])
        copy.start()
        own_attn.append(copy)

    def group_arrived(t, peer):
        view = attn_d.at[peer, groups[t]]
        dp_copy(view, view, ad_ss.at[t, peer], ad_rs.at[t, peer], peer).wait_recv()

    early = rows - 1
    with scope("L_backward"):
        lax.fori_loop(0, early, backward, 0)
    with scope("M_waitattn"):
        for h in far_heads:
            ctx_arrived(attn_r, attn_ss, attn_rs, h)
        spread_attn(0)
    with scope("L_backward"):
        lax.fori_loop(early, rows, backward, 0)

    dkv_s[:, 0] = (dk_acc[...] * scale).astype(bf16).reshape(n, block, dh)
    dkv_s[:, 1] = dv_acc[...].astype(bf16).reshape(n, block, dh)
    for peer in far_heads + near_heads:
        go(ctx_copy(dkv_s.at[peer], dkv_r.at[me], dkv_ss.at[peer], dkv_rs.at[me], peer))
    own_dkv = pltpu.make_async_copy(dkv_s.at[me], dkv_r.at[me], loc.at[5])
    own_dkv.start()

    with scope("M_waitattn"):
        for h in near_heads:
            ctx_arrived(attn_r, attn_ss, attn_rs, h)
        pltpu.make_async_copy(attn_s.at[me], attn_r.at[me], loc.at[3]).wait()
        spread_attn(1)

    with scope("N_waitspread"):
        for t in range(2):
            for peer in dp_far:
                group_arrived(t, peer)
                view = attn_d.at[peer, groups[t]]
                go(dp_copy(view, view, ad_fs.at[t, peer], ad_rs.at[t, peer], twin))
        for t in range(2):
            for peer in [twin] + [lax.rem(twin + 2 * s, dn) for s in range(1, dn // 2)]:
                group_arrived(t, peer)
        for copy in own_attn:
            copy.wait()

    def weight(h):
        heads_of = attn_d[:, h].reshape(dn * block, dh)
        return dot_nn(transposed(heads_of), g_r[...].reshape(dn * block, dc))

    orders = mate_partners + [partner] + mates + [row]
    with scope("P_weight"):
        for a in orders:
            h = 2 * a + 1 - side
            w_s[h] = weight(h).astype(bf16)
            go(ctx_copy(w_s.at[h], w_y.at[a], w_ss.at[h], wy_rs.at[a], pair))

    def mix_step(j, carry):
        rows_of = jnp.concatenate(
            [attn_d[pl.ds(2 * j, 2), h].reshape(width, dh) for h in range(n)], axis=1)
        out = dot_nn(rows_of, proj_r[...].reshape(n * dh, dc))
        mix_s[pl.ds(2 * j, 2)] = out.astype(bf16).reshape(2, block, dc)
        return carry

    with scope("Q_mix"):
        lax.fori_loop(0, dn // 2, mix_step, 0)
    for peer in dp_peers:
        go(dp_copy(mix_s.at[peer], mix_r.at[md], mix_ss.at[peer], mix_rs.at[md], peer))
    own_mix = pltpu.make_async_copy(mix_s.at[md], mix_r.at[md], loc.at[2])
    own_mix.start()

    def both_sides(a):
        total = weight(2 * a + side)
        with scope("R_waitside"):
            ctx_copy(w_y.at[a], w_y.at[a], w_ss.at[me], wy_rs.at[a], pair).wait_recv()
        return total + w_y[a].astype(jnp.float32)

    def send_w(a, total, dst, rs, peer_row):
        h = 2 * a + side
        w_s[h] = total.astype(bf16)
        go(ctx_copy(w_s.at[h], dst, w_ss.at[h], rs, 2 * peer_row + side))

    for a, mate in zip(mate_partners, mates):
        send_w(a, both_sides(a), w_x.at[row], wx_rs.at[row], mate)
    total = both_sides(partner)
    with scope("S_waitcross"):
        for a in mates:
            ctx_copy(w_x.at[a], w_x.at[a], w_ss.at[me], wx_rs.at[a], pair).wait_recv()
            total = total + w_x[a].astype(jnp.float32)
    send_w(partner, total, w_p, wp_rs.at[0], partner)
    for a in mates:
        send_w(a, both_sides(a), w_m.at[row], wm_rs.at[row], a)
    w_out[...] = both_sides(row)

    with scope("T_waitdq"):
        pltpu.make_async_copy(dq_s.at[me], dq_r.at[me], loc.at[4]).wait()
        for peer in ctx_peers:
            ctx_arrived(dq_r, dq_ss, dq_rs, peer)
    with scope("U_waitdkv"):
        own_dkv.wait()
        for peer in ctx_peers:
            ctx_arrived(dkv_r, dkv_ss, dkv_rs, peer)
    with scope("V_waitmix"):
        own_mix.wait()
        for peer in dp_peers:
            dp_arrived(mix_r, mix_ss, mix_rs, peer)
    with scope("W_waitmates"):
        for a in mates:
            ctx_copy(w_m.at[a], w_m.at[a], w_ss.at[me], wm_rs.at[a], pair).wait_recv()
            w_out[...] += w_m[a].astype(jnp.float32)
    with scope("X_waitpartner"):
        ctx_copy(w_p, w_p, w_ss.at[me], wp_rs.at[0], pair).wait_recv()
        w_out[...] += w_p[...].astype(jnp.float32)

    with scope("Y_waitsend"):
        for copy in sends:
            copy.wait_send()
        for peer in ctx_peers:
            ctx_copy(attn_s.at[peer], attn_r.at[me], attn_ss.at[peer], attn_rs.at[me], peer).wait_send()
            ctx_copy(dq_s.at[peer], dq_r.at[me], dq_ss.at[peer], dq_rs.at[me], peer).wait_send()


def shards(queries, keys, values, out_grad, chosen, proj):
    n = lax.axis_size("ctx")
    dn = lax.axis_size("dp")
    tokens = queries.shape[1]
    hd = queries.shape[2]
    dh = hd // n
    dc = proj.shape[1]
    slots = n * BLOCK
    width = 2 * BLOCK
    rows = n // 2
    bf16, f32 = jnp.bfloat16, jnp.float32
    sem = pltpu.SemaphoreType.DMA
    vm = pltpu.VMEM
    blocks = (n, BLOCK, dh)
    sheets = (rows, dh, dc)
    scratch = [
        vm((tokens, hd), bf16), vm((tokens, hd), bf16), vm((tokens, hd), bf16), vm((tokens, dn * dc), bf16),
        vm((n, 3, BLOCK, dh), bf16), vm((dn, BLOCK, dc), bf16), vm((slots, BLOCK), jnp.int32),
        vm((n, 3, BLOCK, dh), bf16), vm((dn, BLOCK, dc), bf16), vm((n, dh, dc), bf16),
        vm((n, dn, BLOCK, dh), bf16), vm((n, dn, BLOCK, dh), bf16), vm(blocks, bf16), vm(blocks, bf16),
        vm(blocks, bf16), vm(blocks, bf16), vm((dn,) + blocks, bf16), vm((rows, dh, width), bf16),
        vm((rows, slots, width), bf16), vm((dh, slots), bf16), vm((dh, slots), bf16),
        vm(blocks, bf16), vm((n, 2, BLOCK, dh), bf16), vm((slots, dh), f32), vm((slots, dh), f32),
        vm((n, dh, dc), bf16), vm(sheets, bf16), vm(sheets, bf16), vm(sheets, bf16), vm((dh, dc), bf16),
        vm((dn, BLOCK, dc), bf16),
    ]
    c, d = sem((n,)), sem((dn,))
    e = sem((n, dn))
    f = sem((2, dn))
    sems = [
        c, c, d, d, c, c, c, c, e, e, c, c,
        c, c, f, f, f, c, c, c, c, c, c, c, c, sem((1,)), d, d,
        sem((10,)),
    ]
    vmem = pl.BlockSpec(memory_space=pltpu.VMEM)
    smem = pl.BlockSpec(memory_space=pltpu.SMEM)
    hbm = pl.BlockSpec(memory_space=pl.ANY)
    dq, dkv, weight_grad, mixed = pl.pallas_call(
        functools.partial(kernel, n, dn, 1.0 / math.sqrt(dh)),
        out_shape=(
            jax.ShapeDtypeStruct(blocks, bf16),
            jax.ShapeDtypeStruct((n, 2, BLOCK, dh), bf16),
            jax.ShapeDtypeStruct((dh, dc), f32),
            jax.ShapeDtypeStruct((dn, BLOCK, dc), bf16),
        ),
        in_specs=[smem] + [hbm] * 5,
        out_specs=[hbm, hbm, vmem, hbm],
        scratch_shapes=scratch + sems,
        compiler_params=pltpu.CompilerParams(
            collective_id=0, has_side_effects=True, vmem_limit_bytes=60 * 1024 * 1024),
    )(chosen, queries[0], keys[0], values[0], out_grad[0], proj)

    wide = (tokens, dn * dc)
    thin = (tokens, hd)
    out, q_grad, k_grad, v_grad, proj_grad = pl.pallas_call(
        functools.partial(place_kernel, n, dn, tokens // BLOCK),
        out_shape=(
            jax.ShapeDtypeStruct(wide, bf16), jax.ShapeDtypeStruct(thin, bf16), jax.ShapeDtypeStruct(thin, bf16),
            jax.ShapeDtypeStruct(thin, bf16), jax.ShapeDtypeStruct((dh, dc), f32)),
        in_specs=[smem] + [hbm] * 3 + [vmem],
        out_specs=[hbm] * 5,
        scratch_shapes=[
            vm((dn, BLOCK, dc), bf16), vm(blocks, bf16), vm((n, 2, BLOCK, dh), bf16),
            vm(wide, bf16), vm(thin, bf16), vm(thin, bf16), vm(thin, bf16), sem((3,)), sem((5,))],
    )(chosen, mixed, dq, dkv, weight_grad)
    return out[None], q_grad[None], k_grad[None], v_grad[None], proj_grad


def solution(mesh):
    rows = P("dp", "ctx", None)
    return jax.shard_map(
        shards,
        mesh=mesh,
        in_specs=(rows, rows, rows, rows, P("dp", None), P("ctx", "dp")),
        out_specs=(rows, rows, rows, rows, P("ctx", "dp")),
        check_vma=False,
    )
```

```python
import functools
import math

import jax
import jax.numpy as jnp
from jax import lax
from jax.experimental import pallas as pl
from jax.experimental.pallas import tpu as pltpu
from jax.sharding import PartitionSpec as P

BLOCK = 128
FAR = 1 << 30
MIB = 1024 * 1024
SPARE = 8 * MIB

scope = jax.named_scope


def dot_nt(a, b):
    return lax.dot_general(a, b, (((1,), (1,)), ((), ())), preferred_element_type=jnp.float32)


def dot_nn(a, b):
    return lax.dot_general(a, b, (((1,), (0,)), ((), ())), preferred_element_type=jnp.float32)


def transposed(a):
    return a.astype(jnp.float32).T.astype(a.dtype)


def local_block(picked, me, count):
    entry = picked[0, me]
    spans = count // 2
    index = jnp.maximum(entry, 0)
    local = jnp.where(index // spans == me, index % spans, spans + index % spans)
    return entry, local


def block_marks(picked, me, count):
    entry, local = local_block(picked, me, count)
    local = jnp.where(entry >= 0, local, -1)
    return [jnp.where(local == j, 1.0, 0.0) for j in range(count)]


def place_kernel(n, dn, count, picked, mix, dq, dkv, w, out, q_out, k_out, v_out, w_out, zero, sems, w_sem):
    block, dh, dc = dq.shape[1], dq.shape[2], mix.shape[2]
    entry, local = local_block(picked, lax.axis_index("ctx"), count)
    local = jnp.where(entry >= 0, local, -1)
    w_copy = pltpu.make_async_copy(w, w_out, w_sem.at[0])
    w_copy.start()
    zero[...] = jnp.zeros_like(zero)
    outs = (out, q_out, k_out, v_out)
    for j in range(count):
        rows = pl.ds(j * block, block)

        @pl.when(local == j)
        def _():
            for d in range(dn):
                pltpu.make_async_copy(mix.at[d], out.at[rows, pl.ds(d * dc, dc)], sems.at[j, 0]).start()
            for h in range(n):
                cols = pl.ds(h * dh, dh)
                pltpu.make_async_copy(dq.at[h], q_out.at[rows, cols], sems.at[j, 1]).start()
                pltpu.make_async_copy(dkv.at[h, 0], k_out.at[rows, cols], sems.at[j, 2]).start()
                pltpu.make_async_copy(dkv.at[h, 1], v_out.at[rows, cols], sems.at[j, 3]).start()

        @pl.when(local != j)
        def _():
            for t, dst in enumerate(outs):
                pltpu.make_async_copy(zero.at[:, pl.ds(0, dst.shape[1])], dst.at[rows], sems.at[j, t]).start()

    for j in range(count):
        for t, dst in enumerate(outs):
            view = dst.at[pl.ds(j * block, block)]
            pltpu.make_async_copy(view, view, sems.at[j, t]).wait()
    w_copy.wait()


def kernel(
    n, dn, scale,
    picked, q_hbm, k_hbm, v_hbm, g_hbm, proj,
    dq_r, dkv_r, w_out, mix_r,
    qkv_in, g_in, qkv, g, kpos, qkv_r, g_r, proj_r, agp_s, agp_r, ag_s, ag_r,
    attn_s, attn_r, attn_y, attn_d, attn_e, attn_t,
    p_s, k_t, v_t, dq_s, dkv_s, dk_acc, dv_acc, w_s, w_x, w_m, w_p, mix_s,
    ss, rs, proj_rs, agp_rs, ag_rs, ad_rs, ae_rs, loc,
):
    me = lax.axis_index("ctx")
    md = lax.axis_index("dp")
    bf16 = jnp.bfloat16
    block, dh = qkv.shape[2], qkv.shape[3]
    dc = proj.shape[1]
    slots = n * block
    width = 2 * block
    rows = n // 2
    half = rows // 2
    s_proj, s_g, s_qkv, s_agp, s_ag, s_gp, s_attn, s_dq, s_dkv, s_ad, s_ap, s_ae, s_w, s_mix, s_pass = (
        ss.at[k] for k in range(15))
    r_g, r_qkv, r_gp, r_attn0, r_attn1, r_dq, r_dkv, r_ap, r_wx, r_wm, r_wp, r_mix = (rs.at[k] for k in range(12))

    def ctx_copy(src, dst, send, recv, peer):
        return pltpu.make_async_remote_copy(
            src_ref=src, dst_ref=dst, send_sem=send, recv_sem=recv,
            device_id={"ctx": peer}, device_id_type=pl.DeviceIdType.MESH)

    def dp_copy(src, dst, send, recv, peer):
        return pltpu.make_async_remote_copy(
            src_ref=src, dst_ref=dst, send_sem=send, recv_sem=recv,
            device_id={"dp": peer}, device_id_type=pl.DeviceIdType.MESH)

    ctx_peers = [lax.rem(me + s, n) for s in range(1, n)]
    dp_peers = [lax.rem(md + s, dn) for s in range(1, dn)]

    barrier = pltpu.get_barrier_semaphore()
    for peer in ctx_peers:
        pl.semaphore_signal(barrier, inc=1, device_id={"ctx": peer}, device_id_type=pl.DeviceIdType.MESH)
    for peer in dp_peers:
        pl.semaphore_signal(barrier, inc=1, device_id={"dp": peer}, device_id_type=pl.DeviceIdType.MESH)

    row = me // 2
    side = lax.rem(me, 2)
    other = 1 - side
    pair = me + 1 - 2 * side
    own_base = (row // half) * half
    far_base = half - own_base

    def near(s):
        return own_base + lax.rem(row + s, half)

    def across(s):
        return far_base + lax.rem(row + s, half)

    mates = [near(s) for s in range(1, half)]
    partner = across(0)
    mate_partners = [across(s) for s in range(1, half)]

    own_proj = pltpu.make_async_copy(proj, proj_r.at[side, row], loc.at[0])
    g_load = pltpu.make_async_copy(g_hbm, g_in, loc.at[1])
    g_load.start()
    for t, src in enumerate((q_hbm, k_hbm, v_hbm)):
        pltpu.make_async_copy(src, qkv_in.at[t], loc.at[2]).start()
    own_proj.start()
    marks = block_marks(picked, me, qkv_in.shape[1] // block)

    def chosen_rows(load):
        total = None
        for j, mark in enumerate(marks):
            term = load(slice(j * block, (j + 1) * block)).astype(jnp.float32) * mark
            total = term if total is None else total + term
        return total.astype(bf16)

    def arrived(view, recv):
        ctx_copy(view, view, s_proj, recv, pair).wait_recv()

    def sent(view, send):
        ctx_copy(view, view, send, r_g, pair).wait_send()

    with scope("A_load"):
        g_load.wait()
        for j in range(dn):
            g[j] = chosen_rows(lambda r: g_in[r, j * dc:(j + 1) * dc])
        g_r[side, md] = g[md]
        pltpu.make_async_copy(qkv_in, qkv_in, loc.at[2]).wait()
        for t in range(3):
            for h in range(n):
                qkv[h, t] = chosen_rows(lambda r: qkv_in[t, r, h * dh:(h + 1) * dh])
        qkv_r[me] = qkv[me]
    with scope("B_barrier"):
        pl.semaphore_wait(barrier, n - 1 + dn - 1)

    own_block = proj_r.at[side, row]
    for peer in [2 * a + side for a in [partner] + mates] + [pair]:
        ctx_copy(proj, own_block, s_proj, proj_rs.at[side, row], peer).start()
    for peer in dp_peers:
        dp_copy(g.at[peer], g_r.at[side, md], s_g, r_g, peer).start()

    def send_qkv(peers):
        for peer in peers:
            ctx_copy(qkv.at[peer], qkv_r.at[me], s_qkv, r_qkv, peer).start()

    send_qkv([2 * a + side for a in [partner] + mate_partners])

    down = lax.broadcasted_iota(jnp.int32, (block, block), 0)
    for j in range(n):
        entry = picked[0, j]
        kpos[j * block:(j + 1) * block] = down + jnp.where(entry >= 0, entry * block, FAR)

    def proj_arrived(a, s):
        arrived(proj_r.at[s, a], proj_rs.at[s, a])

    def pass_on(a, peer):
        ctx_copy(proj_r.at[side, a], proj_r.at[side, a], s_pass, proj_rs.at[side, a], peer).start()

    with scope("C_waitmate"):
        for a in mates:
            proj_arrived(a, side)
            pass_on(a, pair)
    with scope("D_waitpartner"):
        proj_arrived(partner, side)
        for a in mates:
            pass_on(partner, 2 * a + side)
        pass_on(partner, pair)
    send_qkv([2 * a + side for a in mates])
    own_proj.wait()
    with scope("E_waitg"):
        arrived(g_r.at[side, pl.ds(0, dn - 1)], r_g)

    def part(a, s):
        h = 2 * a + s
        out = dot_nt(g_r[side].reshape(dn * block, dc), proj_r[s, a]).astype(bf16)
        agp_s[h] = out.reshape(dn, block, dh)
        for peer in dp_peers:
            dp_copy(agp_s.at[h, peer], agp_r.at[h, md], s_agp, agp_rs.at[h], peer).start()

    def finish(a, s):
        h = 2 * a + s
        arrived(agp_r.at[h, pl.ds(0, dn - 1)], agp_rs.at[h])
        total = agp_s[h, md].astype(jnp.float32)
        for peer in dp_peers:
            total = total + agp_r[h, peer].astype(jnp.float32)
        if a is row and s is side:
            ag_r[me] = total.astype(bf16)
        else:
            ag_s[h] = total.astype(bf16)
            ctx_copy(ag_s.at[h], ag_r.at[me], s_ag, ag_rs.at[row], h).start()

    with scope("G_part"):
        first = [(partner, side)] + [(a, side) for a in mates] + [(row, side)]
        for a, s in first:
            part(a, s)
    with scope("F_waitsecond"):
        for a in mate_partners:
            proj_arrived(a, side)
            pass_on(a, pair)
    send_qkv([2 * a + other for a in [partner] + mate_partners + mates] + [pair])
    rest = [(a, side) for a in mate_partners]
    rest += [(row, other)] + [(a, other) for a in mates + [partner] + mate_partners]
    waiting = first
    for a, s in rest:
        if s is other:
            with scope("F_waitproj"):
                proj_arrived(a, s)
        with scope("G_part"):
            part(a, s)
        with scope("H_finish"):
            finish(*waiting[0])
        waiting = waiting[1:] + [(a, s)]
    with scope("H_finish"):
        for a, s in waiting:
            finish(a, s)
    ctx_copy(g_r.at[side], g_r.at[side], s_gp, r_gp, pair).start()

    with scope("I_waitqkv"):
        arrived(qkv_r.at[pl.ds(0, n - 1)], r_qkv)
    k_t[...] = transposed(qkv_r[:, 1].reshape(slots, dh))
    v_t[...] = transposed(qkv_r[:, 2].reshape(slots, dh))

    def ordered(k):
        late = k // half
        return far_base * (1 - late) + own_base * late + lax.rem(row + k + late, half)

    def forward(k, carry):
        i = ordered(k)
        q = qkv_r[pl.ds(2 * i, 2), 0].reshape(width, dh)
        keys = qkv_r[:, 1].reshape(slots, dh)
        scores = dot_nt(keys, q) * scale
        key_pos = kpos[...]
        key_pos = jnp.concatenate([key_pos, key_pos], axis=1)
        same = lax.broadcasted_iota(jnp.int32, (slots, width), 0) == (
            lax.broadcasted_iota(jnp.int32, (slots, width), 1) + i * width)
        lane = lax.broadcasted_iota(jnp.int32, (1, width), 1)
        one, two = picked[0, 2 * i], picked[0, 2 * i + 1]
        one = jnp.where(one >= 0, one * block, -FAR)
        two = jnp.where(two >= 0, (two - 1) * block, -FAR)
        query_pos = lane + jnp.where(lane < block, one, two)
        scores = jnp.where((key_pos <= query_pos) | same, scores, -1e30)
        e = jnp.exp(scores - jnp.max(scores, axis=0, keepdims=True))
        p = (e * (1.0 / jnp.sum(e, axis=0, keepdims=True))).astype(bf16)
        p_s[i] = p
        a_t = dot_nn(v_t[...], p)
        attn_t[i] = a_t.astype(bf16)
        attn_s[i] = a_t.T.astype(bf16)

        @pl.when(k < half)
        def _():
            ctx_copy(attn_s.at[i], attn_r.at[row], s_attn, r_attn0, 2 * i + side).start()

        @pl.when((k >= half) & (k < rows - 1))
        def _():
            ctx_copy(attn_s.at[i], attn_r.at[row], s_attn, r_attn1, 2 * i + side).start()

        @pl.when(k == rows - 1)
        def _():
            pltpu.make_async_copy(attn_s.at[i], attn_r.at[i], loc.at[3]).start()

        return carry

    with scope("J_forward"):
        lax.fori_loop(0, rows, forward, 0)

    dk_acc[...] = jnp.zeros_like(dk_acc)
    dv_acc[...] = jnp.zeros_like(dv_acc)

    def backward(k, carry):
        i = ordered(k)
        with scope("K_waitag"):
            @pl.when(k < rows - 1)
            def _():
                arrived(ag_r.at[pl.ds(2 * i, 2)], ag_rs.at[i])

            @pl.when(k == rows - 1)
            def _():
                arrived(ag_r.at[pair], ag_rs.at[row])

        q = qkv_r[pl.ds(2 * i, 2), 0].reshape(width, dh)
        v = qkv_r[:, 2].reshape(slots, dh)
        da = ag_r[pl.ds(2 * i, 2)].reshape(width, dh)
        delta = jnp.sum(da.astype(jnp.float32).T * attn_t[i].astype(jnp.float32), axis=0, keepdims=True)
        p = p_s[i]
        ds = (p.astype(jnp.float32) * (dot_nt(v, da) - delta)).astype(bf16)
        dq_t = dot_nn(k_t[...], ds) * scale
        dq_s[pl.ds(2 * i, 2)] = dq_t.T.astype(bf16).reshape(2, block, dh)
        for t in range(2):
            peer = 2 * i + t

            @pl.when(peer != me)
            def _():
                ctx_copy(dq_s.at[peer], dq_r.at[me], s_dq, r_dq, peer).start()

            @pl.when(peer == me)
            def _():
                pltpu.make_async_copy(dq_s.at[peer], dq_r.at[peer], loc.at[4]).start()

        dk_acc[...] += dot_nn(ds, q)
        dv_acc[...] += dot_nn(p, da)
        return carry

    with scope("L_backward"):
        lax.fori_loop(0, rows, backward, 0)

    dkv_s[:, 0] = (dk_acc[...] * scale).astype(bf16).reshape(n, block, dh)
    dkv_s[:, 1] = dv_acc[...].astype(bf16).reshape(n, block, dh)
    for peer in [2 * a + s for a in [partner] + mate_partners + mates for s in (side, other)] + [pair]:
        ctx_copy(dkv_s.at[peer], dkv_r.at[me], s_dkv, r_dkv, peer).start()
    own_dkv = pltpu.make_async_copy(dkv_s.at[me], dkv_r.at[me], loc.at[5])
    own_dkv.start()

    twin = md + 1 - 2 * lax.rem(md, 2)
    dp_far = [lax.rem(md + 2 * s, dn) for s in range(1, dn // 2)]

    def spread(src, dst_of, send, recv, own_sem):
        for s, peer in enumerate(dp_far):
            dp_copy(src, dst_of(md), send, recv.at[1 + s], peer).start()
        dp_copy(src, dst_of(md), send, recv.at[0], twin).start()
        copy = pltpu.make_async_copy(src, dst_of(md), own_sem)
        copy.start()
        return copy

    def hand_over(dst_of, send, recv):
        for s in range(1, dn // 2):
            peer = lax.rem(md + dn - 2 * s, dn)
            arrived(dst_of(peer), recv.at[s])
            dp_copy(dst_of(peer), dst_of(peer), send, recv.at[0], twin).start()

    groups = [pl.ds(far_base, half), pl.ds(own_base, half)]
    with scope("M_waitattn"):
        arrived(attn_r.at[groups[0]], r_attn0)
    own_far = spread(attn_r.at[groups[0]], lambda d: attn_d.at[0, d, pl.ds(0, half)], s_ad, ad_rs.at[0], loc.at[6])
    with scope("M_waitattn"):
        if half > 1:
            arrived(attn_r.at[pl.ds(0, half - 1)], r_attn1)
        pltpu.make_async_copy(attn_s.at[row], attn_r.at[row], loc.at[3]).wait()
    own_near = spread(attn_r.at[groups[1]], lambda d: attn_d.at[1, d, pl.ds(0, half)], s_ad, ad_rs.at[1], loc.at[7])
    ctx_copy(attn_r.at[:, pl.ds(pl.multiple_of(other * block, block), block)], attn_y, s_ap, r_ap, pair).start()
    with scope("N_handover0"):
        hand_over(lambda d: attn_d.at[0, d, pl.ds(0, half)], s_ad, ad_rs.at[0])
    with scope("N_waitpair"):
        arrived(attn_y, r_ap)
    own_ae = spread(attn_y, lambda d: attn_e.at[d], s_ae, ae_rs, loc.at[8])
    with scope("N_handover1"):
        hand_over(lambda d: attn_d.at[1, d, pl.ds(0, half)], s_ad, ad_rs.at[1])
    with scope("N_waitspread"):
        own_far.wait()
        own_near.wait()
        for t in range(2):
            arrived(attn_d.at[t, pl.ds(0, dn // 2)], ad_rs.at[t, 0])
        arrived(g_r.at[other], r_gp)

    def weight(t, a):
        total = None
        for b in range(2):
            heads_of = attn_d[t, :, lax.rem(a, half), b * block:(b + 1) * block].reshape(dn * block, dh)
            term = dot_nn(transposed(heads_of), g_r[b].reshape(dn * block, dc))
            total = term if total is None else total + term
        return total

    def send_w(slot, value, dst, recv, peer_row):
        w_s[slot] = value.astype(bf16)
        ctx_copy(w_s.at[slot], dst, s_w, recv, 2 * peer_row + side).start()

    with scope("P_weight"):
        for k, a in enumerate(mate_partners):
            send_w(k, weight(0, a), w_x.at[row], r_wx, mates[k])
        crossing = weight(0, partner)
        for k, a in enumerate(mates):
            send_w(half - 1 + k, weight(1, a), w_m.at[row], r_wm, a)
        w_out[...] = weight(1, row)

    def cross_sum(total):
        if mates:
            arrived(w_x.at[pl.ds(0, half - 1)], r_wx)
        for a in mates:
            total = total + w_x[a].astype(jnp.float32)
        send_w(rows - 2, total, w_p, r_wp, partner)

    with scope("O_handover"):
        hand_over(lambda d: attn_e.at[d], s_ae, ae_rs)
        own_ae.wait()
        arrived(attn_e.at[pl.ds(0, dn // 2)], ae_rs.at[0])

    mine = pl.ds(pl.multiple_of(side * block, block), block)

    def mix_step(j, carry):
        def two(ref, *at):
            return ref[at].reshape(width, dh)

        d = pl.ds(2 * j, 2)
        t_of = [row // half if a // half else 1 - row // half for a in range(rows)]
        here = jnp.concatenate([two(attn_d, t_of[a], d, a % half, mine) for a in range(rows)], axis=1)
        there = jnp.concatenate([two(attn_e, d, a) for a in range(rows)], axis=1)
        out = dot_nn(here, proj_r[side].reshape(rows * dh, dc)) + dot_nn(there, proj_r[other].reshape(rows * dh, dc))
        mix_s[d] = out.astype(bf16).reshape(2, block, dc)
        return carry

    with scope("Q_mix"):
        lax.fori_loop(0, dn // 2, mix_step, 0)
    for peer in dp_peers:
        dp_copy(mix_s.at[peer], mix_r.at[md], s_mix, r_mix, peer).start()
    own_mix = pltpu.make_async_copy(mix_s.at[md], mix_r.at[md], loc.at[9])
    own_mix.start()

    with scope("S_waitcross"):
        cross_sum(crossing)

    with scope("T_waitdq"):
        pltpu.make_async_copy(dq_s.at[me], dq_r.at[me], loc.at[4]).wait()
        arrived(dq_r.at[pl.ds(0, n - 1)], r_dq)
    with scope("U_waitdkv"):
        own_dkv.wait()
        arrived(dkv_r.at[pl.ds(0, n - 1)], r_dkv)
    with scope("W_waitmates"):
        if mates:
            arrived(w_m.at[pl.ds(0, half - 1)], r_wm)
        for a in mates:
            w_out[...] += w_m[a].astype(jnp.float32)
    with scope("X_waitpartner"):
        arrived(w_p, r_wp)
        w_out[...] += w_p[...].astype(jnp.float32)
    with scope("V_waitmix"):
        own_mix.wait()
        arrived(mix_r.at[pl.ds(0, dn - 1)], r_mix)

    with scope("Y_waitsend"):
        blocks = pl.ds(0, n - 1)
        others = pl.ds(0, dn - 1)
        sent(qkv_r.at[pl.ds(0, n - 1)], s_qkv)
        sent(proj_r.at[0, pl.ds(0, half + 1)], s_proj)
        passed = rows + half - 2
        sent(proj_r.at[:, pl.ds(0, passed // 2)] if passed % 2 == 0 else proj_r.at[0, pl.ds(0, passed)], s_pass)
        sent(g.at[others], s_g)
        sent(agp_s.at[:, others], s_agp)
        sent(ag_s.at[blocks], s_ag)
        sent(g_r.at[0], s_gp)
        sent(attn_s.at[pl.ds(0, rows - 1)], s_attn)
        sent(dq_s.at[blocks], s_dq)
        sent(dkv_s.at[blocks], s_dkv)
        sent(attn_d.at[:, others], s_ad)
        sent(attn_y, s_ap)
        sent(attn_e.at[others], s_ae)
        sent(w_s.at[pl.ds(0, rows - 1)], s_w)
        sent(mix_s.at[others], s_mix)


def shards(queries, keys, values, out_grad, chosen, proj):
    n = lax.axis_size("ctx")
    dn = lax.axis_size("dp")
    tokens = queries.shape[1]
    hd = queries.shape[2]
    dh = hd // n
    dc = proj.shape[1]
    slots = n * BLOCK
    width = 2 * BLOCK
    rows = n // 2
    half = rows // 2
    bf16, f32 = jnp.bfloat16, jnp.float32
    sem = pltpu.SemaphoreType.DMA
    blocks = (n, BLOCK, dh)
    pairs = (rows, width, dh)
    sheets = (rows, dh, dc)
    buffers = [
        ((3, tokens, hd), bf16), ((tokens, dn * dc), bf16), ((n, 3, BLOCK, dh), bf16), ((dn, BLOCK, dc), bf16),
        ((slots, BLOCK), jnp.int32), ((n, 3, BLOCK, dh), bf16), ((2, dn, BLOCK, dc), bf16), ((2,) + sheets, bf16),
        ((n, dn, BLOCK, dh), bf16), ((n, dn, BLOCK, dh), bf16), (blocks, bf16), (blocks, bf16),
        (pairs, bf16), (pairs, bf16), ((rows, BLOCK, dh), bf16), ((2, dn, half, width, dh), bf16),
        ((dn, rows, BLOCK, dh), bf16), ((rows, dh, width), bf16),
        ((rows, slots, width), bf16), ((dh, slots), bf16), ((dh, slots), bf16),
        (blocks, bf16), ((n, 2, BLOCK, dh), bf16), ((slots, dh), f32), ((slots, dh), f32),
        (sheets, bf16), (sheets, bf16), (sheets, bf16), ((dh, dc), bf16), ((dn, BLOCK, dc), bf16),
    ]
    held = sum(math.prod(shape) * jnp.dtype(kind).itemsize for shape, kind in buffers)
    sems = [sem((15,)), sem((12,)), sem((2, rows)), sem((n,)), sem((rows,)), sem((2, dn // 2)), sem((dn // 2,)), sem((10,))]
    vmem = pl.BlockSpec(memory_space=pltpu.VMEM)
    smem = pl.BlockSpec(memory_space=pltpu.SMEM)
    free = pl.BlockSpec(memory_space=pl.ANY)
    hbm = pl.BlockSpec(memory_space=pltpu.HBM)
    dq, dkv, weight_grad, mixed = pl.pallas_call(
        functools.partial(kernel, n, dn, 1.0 / math.sqrt(dh)),
        out_shape=(
            jax.ShapeDtypeStruct(blocks, bf16),
            jax.ShapeDtypeStruct((n, 2, BLOCK, dh), bf16),
            jax.ShapeDtypeStruct((dh, dc), f32),
            jax.ShapeDtypeStruct((dn, BLOCK, dc), bf16),
        ),
        in_specs=[smem] + [hbm] * 5,
        out_specs=[free, free, vmem, free],
        scratch_shapes=[pltpu.VMEM(shape, kind) for shape, kind in buffers] + sems,
        compiler_params=pltpu.CompilerParams(
            collective_id=0, has_side_effects=True, vmem_limit_bytes=min(held + SPARE, 60 * MIB)),
    )(chosen, *[pltpu.with_memory_space_constraint(x, pltpu.HBM) for x in (queries[0], keys[0], values[0], out_grad[0], proj)])

    wide = (tokens, dn * dc)
    thin = (tokens, hd)
    count = tokens // BLOCK
    out, q_grad, k_grad, v_grad, proj_grad = pl.pallas_call(
        functools.partial(place_kernel, n, dn, count),
        out_shape=(
            jax.ShapeDtypeStruct(wide, bf16), jax.ShapeDtypeStruct(thin, bf16), jax.ShapeDtypeStruct(thin, bf16),
            jax.ShapeDtypeStruct(thin, bf16), jax.ShapeDtypeStruct((dh, dc), f32)),
        in_specs=[smem] + [free] * 4,
        out_specs=[hbm] * 5,
        scratch_shapes=[pltpu.VMEM((BLOCK, max(dn * dc, hd)), bf16), sem((count, 4)), sem((1,))],
        compiler_params=pltpu.CompilerParams(vmem_limit_bytes=8 * MIB),
    )(chosen, mixed, dq, dkv, weight_grad)
    return out[None], q_grad[None], k_grad[None], v_grad[None], proj_grad


def solution(mesh):
    rows = P("dp", "ctx", None)
    return jax.shard_map(
        shards,
        mesh=mesh,
        in_specs=(rows, rows, rows, rows, P("dp", None), P("ctx", "dp")),
        out_specs=(rows, rows, rows, rows, P("ctx", "dp")),
        check_vma=False,
    )
```

```python
import functools
import math

import jax
import jax.numpy as jnp
from jax import lax
from jax.experimental import pallas as pl
from jax.experimental.pallas import tpu as pltpu
from jax.sharding import PartitionSpec as P

BLOCK = 128
FAR = 1 << 30
MIB = 1024 * 1024
SPARE = 8 * MIB

scope = jax.named_scope


def dot_nt(a, b):
    return lax.dot_general(a, b, (((1,), (1,)), ((), ())), preferred_element_type=jnp.float32)


def dot_nn(a, b):
    return lax.dot_general(a, b, (((1,), (0,)), ((), ())), preferred_element_type=jnp.float32)


def transposed(a):
    return a.astype(jnp.float32).T.astype(a.dtype)


def local_block(picked, me, count):
    entry = picked[0, me]
    spans = count // 2
    index = jnp.maximum(entry, 0)
    local = jnp.where(index // spans == me, index % spans, spans + index % spans)
    return entry, local


def block_marks(picked, me, count):
    entry, local = local_block(picked, me, count)
    local = jnp.where(entry >= 0, local, -1)
    return [jnp.where(local == j, 1.0, 0.0) for j in range(count)]


def place_kernel(n, dn, count, chosen, mix, dq, dkv, w, out, q_out, k_out, v_out, w_out, picked, zero, sems, w_sem):
    block, dh, dc = dq.shape[1], dq.shape[2], mix.shape[2]
    pick = pltpu.make_async_copy(chosen, picked, w_sem.at[1])
    pick.start()
    w_copy = pltpu.make_async_copy(w, w_out, w_sem.at[0])
    w_copy.start()
    zero[...] = jnp.zeros_like(zero)
    pick.wait()
    entry, local = local_block(picked, lax.axis_index("ctx"), count)
    local = jnp.where(entry >= 0, local, -1)
    outs = (out, q_out, k_out, v_out)
    for j in range(count):
        rows = pl.ds(j * block, block)

        @pl.when(local == j)
        def _():
            for d in range(dn):
                pltpu.make_async_copy(mix.at[d], out.at[rows, pl.ds(d * dc, dc)], sems.at[j, 0]).start()
            for h in range(n):
                cols = pl.ds(h * dh, dh)
                pltpu.make_async_copy(dq.at[h], q_out.at[rows, cols], sems.at[j, 1]).start()
                pltpu.make_async_copy(dkv.at[h, 0], k_out.at[rows, cols], sems.at[j, 2]).start()
                pltpu.make_async_copy(dkv.at[h, 1], v_out.at[rows, cols], sems.at[j, 3]).start()

        @pl.when(local != j)
        def _():
            for t, dst in enumerate(outs):
                pltpu.make_async_copy(zero.at[:, pl.ds(0, dst.shape[1])], dst.at[rows], sems.at[j, t]).start()

    for j in range(count):
        for t, dst in enumerate(outs):
            view = dst.at[pl.ds(j * block, block)]
            pltpu.make_async_copy(view, view, sems.at[j, t]).wait()
    w_copy.wait()


def kernel(
    n, dn, scale,
    chosen, q_hbm, k_hbm, v_hbm, g_hbm, proj,
    dq_r, dkv_r, w_out, mix_r,
    picked, qkv_in, g_in, qkv, g, kpos, qkv_r, g_r, proj_r, agp_s, agp_r, ag_s, ag_r,
    attn_s, attn_r, attn_y, attn_d, attn_e, attn_t,
    p_s, k_t, v_t, dq_s, dkv_s, dk_acc, dv_acc, w_s, w_x, w_m, w_p, mix_s,
    ss, rs, proj_rs, agp_rs, ag_rs, ad_rs, ae_rs, loc,
):
    me = lax.axis_index("ctx")
    md = lax.axis_index("dp")
    bf16 = jnp.bfloat16
    block, dh = qkv.shape[2], qkv.shape[3]
    dc = proj.shape[1]
    slots = n * block
    width = 2 * block
    rows = n // 2
    half = rows // 2
    s_proj, s_g, s_qkv, s_agp, s_ag, s_gp, s_attn, s_dq, s_dkv, s_ad, s_ap, s_ae, s_w, s_mix, s_pass = (
        ss.at[k] for k in range(15))
    r_g, r_qkv, r_gp, r_attn0, r_attn1, r_dq, r_dkv, r_ap, r_wx, r_wm, r_wp, r_mix = (rs.at[k] for k in range(12))

    def ctx_copy(src, dst, send, recv, peer):
        return pltpu.make_async_remote_copy(
            src_ref=src, dst_ref=dst, send_sem=send, recv_sem=recv,
            device_id={"ctx": peer}, device_id_type=pl.DeviceIdType.MESH)

    def dp_copy(src, dst, send, recv, peer):
        return pltpu.make_async_remote_copy(
            src_ref=src, dst_ref=dst, send_sem=send, recv_sem=recv,
            device_id={"dp": peer}, device_id_type=pl.DeviceIdType.MESH)

    ctx_peers = [lax.rem(me + s, n) for s in range(1, n)]
    dp_peers = [lax.rem(md + s, dn) for s in range(1, dn)]

    barrier = pltpu.get_barrier_semaphore()
    for peer in ctx_peers:
        pl.semaphore_signal(barrier, inc=1, device_id={"ctx": peer}, device_id_type=pl.DeviceIdType.MESH)
    for peer in dp_peers:
        pl.semaphore_signal(barrier, inc=1, device_id={"dp": peer}, device_id_type=pl.DeviceIdType.MESH)

    row = me // 2
    side = lax.rem(me, 2)
    other = 1 - side
    pair = me + 1 - 2 * side
    own_base = (row // half) * half
    far_base = half - own_base

    def near(s):
        return own_base + lax.rem(row + s, half)

    def across(s):
        return far_base + lax.rem(row + s, half)

    mates = [near(s) for s in range(1, half)]
    partner = across(0)
    mate_partners = [across(s) for s in range(1, half)]

    pick = pltpu.make_async_copy(chosen, picked, loc.at[10])
    pick.start()
    own_proj = pltpu.make_async_copy(proj, proj_r.at[side, row], loc.at[0])
    g_load = pltpu.make_async_copy(g_hbm, g_in, loc.at[1])
    g_load.start()
    for t, src in enumerate((q_hbm, k_hbm, v_hbm)):
        pltpu.make_async_copy(src, qkv_in.at[t], loc.at[2]).start()
    own_proj.start()
    pick.wait()
    marks = block_marks(picked, me, qkv_in.shape[1] // block)

    def chosen_rows(load):
        total = None
        for j, mark in enumerate(marks):
            term = load(slice(j * block, (j + 1) * block)).astype(jnp.float32) * mark
            total = term if total is None else total + term
        return total.astype(bf16)

    def arrived(view, recv):
        ctx_copy(view, view, s_proj, recv, pair).wait_recv()

    def sent(view, send):
        ctx_copy(view, view, send, r_g, pair).wait_send()

    with scope("A_load"):
        g_load.wait()
        for j in range(dn):
            g[j] = chosen_rows(lambda r: g_in[r, j * dc:(j + 1) * dc])
        g_r[side, md] = g[md]
        pltpu.make_async_copy(qkv_in, qkv_in, loc.at[2]).wait()
        for t in range(3):
            for h in range(n):
                qkv[h, t] = chosen_rows(lambda r: qkv_in[t, r, h * dh:(h + 1) * dh])
        qkv_r[me] = qkv[me]
    with scope("B_barrier"):
        pl.semaphore_wait(barrier, n - 1 + dn - 1)

    own_block = proj_r.at[side, row]
    for peer in [2 * a + side for a in [partner] + mates] + [pair]:
        ctx_copy(proj, own_block, s_proj, proj_rs.at[side, row], peer).start()
    for peer in dp_peers:
        dp_copy(g.at[peer], g_r.at[side, md], s_g, r_g, peer).start()

    def send_qkv(peers):
        for peer in peers:
            ctx_copy(qkv.at[peer], qkv_r.at[me], s_qkv, r_qkv, peer).start()

    send_qkv([2 * a + side for a in [partner] + mate_partners])

    down = lax.broadcasted_iota(jnp.int32, (block, block), 0)
    for j in range(n):
        entry = picked[0, j]
        kpos[j * block:(j + 1) * block] = down + jnp.where(entry >= 0, entry * block, FAR)

    def proj_arrived(a, s):
        arrived(proj_r.at[s, a], proj_rs.at[s, a])

    def pass_on(a, peer):
        ctx_copy(proj_r.at[side, a], proj_r.at[side, a], s_pass, proj_rs.at[side, a], peer).start()

    with scope("C_waitmate"):
        for a in mates:
            proj_arrived(a, side)
            pass_on(a, pair)
    with scope("D_waitpartner"):
        proj_arrived(partner, side)
        for a in mates:
            pass_on(partner, 2 * a + side)
        pass_on(partner, pair)
    send_qkv([2 * a + side for a in mates])
    own_proj.wait()
    with scope("E_waitg"):
        arrived(g_r.at[side, pl.ds(0, dn - 1)], r_g)

    def part(a, s):
        h = 2 * a + s
        out = dot_nt(g_r[side].reshape(dn * block, dc), proj_r[s, a]).astype(bf16)
        agp_s[h] = out.reshape(dn, block, dh)
        for peer in dp_peers:
            dp_copy(agp_s.at[h, peer], agp_r.at[h, md], s_agp, agp_rs.at[h], peer).start()

    def finish(a, s):
        h = 2 * a + s
        arrived(agp_r.at[h, pl.ds(0, dn - 1)], agp_rs.at[h])
        total = agp_s[h, md].astype(jnp.float32)
        for peer in dp_peers:
            total = total + agp_r[h, peer].astype(jnp.float32)
        if a is row and s is side:
            ag_r[me] = total.astype(bf16)
        else:
            ag_s[h] = total.astype(bf16)
            ctx_copy(ag_s.at[h], ag_r.at[me], s_ag, ag_rs.at[row], h).start()

    with scope("G_part"):
        first = [(partner, side)] + [(a, side) for a in mates] + [(row, side)]
        for a, s in first:
            part(a, s)
    with scope("F_waitsecond"):
        for a in mate_partners:
            proj_arrived(a, side)
            pass_on(a, pair)
    send_qkv([2 * a + other for a in [partner] + mate_partners + mates] + [pair])
    rest = [(a, side) for a in mate_partners]
    rest += [(row, other)] + [(a, other) for a in mates + [partner]]
    last = [(a, other) for a in mate_partners]
    waiting = first
    for a, s in rest:
        if s is other:
            with scope("F_waitproj"):
                proj_arrived(a, s)
        with scope("G_part"):
            part(a, s)
        with scope("H_finish"):
            finish(*waiting[0])
        waiting = waiting[1:] + [(a, s)]
    with scope("H_finish"):
        for a, s in waiting:
            finish(a, s)
    ctx_copy(g_r.at[side], g_r.at[side], s_gp, r_gp, pair).start()

    with scope("I_waitqkv"):
        arrived(qkv_r.at[pl.ds(0, n - 1)], r_qkv)
    k_t[...] = transposed(qkv_r[:, 1].reshape(slots, dh))
    v_t[...] = transposed(qkv_r[:, 2].reshape(slots, dh))

    def ordered(k):
        late = k // half
        return far_base * (1 - late) + own_base * late + lax.rem(row + k + late, half)

    def forward(k, carry):
        i = ordered(k)
        q = qkv_r[pl.ds(2 * i, 2), 0].reshape(width, dh)
        keys = qkv_r[:, 1].reshape(slots, dh)
        scores = dot_nt(keys, q) * scale
        key_pos = kpos[...]
        key_pos = jnp.concatenate([key_pos, key_pos], axis=1)
        same = lax.broadcasted_iota(jnp.int32, (slots, width), 0) == (
            lax.broadcasted_iota(jnp.int32, (slots, width), 1) + i * width)
        lane = lax.broadcasted_iota(jnp.int32, (1, width), 1)
        one, two = picked[0, 2 * i], picked[0, 2 * i + 1]
        one = jnp.where(one >= 0, one * block, -FAR)
        two = jnp.where(two >= 0, (two - 1) * block, -FAR)
        query_pos = lane + jnp.where(lane < block, one, two)
        scores = jnp.where((key_pos <= query_pos) | same, scores, -1e30)
        e = jnp.exp(scores - jnp.max(scores, axis=0, keepdims=True))
        p = (e * (1.0 / jnp.sum(e, axis=0, keepdims=True))).astype(bf16)
        p_s[i] = p
        a_t = dot_nn(v_t[...], p)
        attn_t[i] = a_t.astype(bf16)
        attn_s[i] = a_t.T.astype(bf16)

        @pl.when(k < half)
        def _():
            ctx_copy(attn_s.at[i], attn_r.at[row], s_attn, r_attn0, 2 * i + side).start()

        @pl.when((k >= half) & (k < rows - 1))
        def _():
            ctx_copy(attn_s.at[i], attn_r.at[row], s_attn, r_attn1, 2 * i + side).start()

        @pl.when(k == rows - 1)
        def _():
            pltpu.make_async_copy(attn_s.at[i], attn_r.at[i], loc.at[3]).start()

        return carry

    with scope("J_forward"):
        lax.fori_loop(0, half, forward, 0)
    for a, s in last:
        with scope("F_waitproj"):
            proj_arrived(a, s)
        with scope("G_part"):
            part(a, s)
    with scope("J_forward"):
        lax.fori_loop(half, rows, forward, 0)
    for a, s in last:
        with scope("H_finish"):
            finish(a, s)

    dk_acc[...] = jnp.zeros_like(dk_acc)
    dv_acc[...] = jnp.zeros_like(dv_acc)

    def backward(k, carry):
        i = ordered(k)
        with scope("K_waitag"):
            @pl.when(k < rows - 1)
            def _():
                arrived(ag_r.at[pl.ds(2 * i, 2)], ag_rs.at[i])

            @pl.when(k == rows - 1)
            def _():
                arrived(ag_r.at[pair], ag_rs.at[row])

        q = qkv_r[pl.ds(2 * i, 2), 0].reshape(width, dh)
        v = qkv_r[:, 2].reshape(slots, dh)
        da = ag_r[pl.ds(2 * i, 2)].reshape(width, dh)
        delta = jnp.sum(da.astype(jnp.float32).T * attn_t[i].astype(jnp.float32), axis=0, keepdims=True)
        p = p_s[i]
        ds = (p.astype(jnp.float32) * (dot_nt(v, da) - delta)).astype(bf16)
        dq_t = dot_nn(k_t[...], ds) * scale
        dq_s[pl.ds(2 * i, 2)] = dq_t.T.astype(bf16).reshape(2, block, dh)
        for t in range(2):
            peer = 2 * i + t

            @pl.when(peer != me)
            def _():
                ctx_copy(dq_s.at[peer], dq_r.at[me], s_dq, r_dq, peer).start()

            @pl.when(peer == me)
            def _():
                pltpu.make_async_copy(dq_s.at[peer], dq_r.at[peer], loc.at[4]).start()

        dk_acc[...] += dot_nn(ds, q)
        dv_acc[...] += dot_nn(p, da)
        return carry

    with scope("L_backward"):
        lax.fori_loop(0, rows, backward, 0)

    dkv_s[:, 0] = (dk_acc[...] * scale).astype(bf16).reshape(n, block, dh)
    dkv_s[:, 1] = dv_acc[...].astype(bf16).reshape(n, block, dh)

    def send_dkv(peers):
        for peer in peers:
            ctx_copy(dkv_s.at[peer], dkv_r.at[me], s_dkv, r_dkv, peer).start()

    send_dkv([2 * a + side for a in [partner] + mate_partners + mates])
    own_dkv = pltpu.make_async_copy(dkv_s.at[me], dkv_r.at[me], loc.at[5])
    own_dkv.start()

    twin = md + 1 - 2 * lax.rem(md, 2)
    dp_far = [lax.rem(md + 2 * s, dn) for s in range(1, dn // 2)]

    def spread(src, dst_of, send, recv, own_sem):
        for s, peer in enumerate(dp_far):
            dp_copy(src, dst_of(md), send, recv.at[1 + s], peer).start()
        dp_copy(src, dst_of(md), send, recv.at[0], twin).start()
        copy = pltpu.make_async_copy(src, dst_of(md), own_sem)
        copy.start()
        return copy

    def hand_over(dst_of, send, recv):
        for s in range(1, dn // 2):
            peer = lax.rem(md + dn - 2 * s, dn)
            arrived(dst_of(peer), recv.at[s])
            dp_copy(dst_of(peer), dst_of(peer), send, recv.at[0], twin).start()

    groups = [pl.ds(far_base, half), pl.ds(own_base, half)]
    with scope("M_waitattn"):
        arrived(attn_r.at[groups[0]], r_attn0)
    own_far = spread(attn_r.at[groups[0]], lambda d: attn_d.at[0, d, pl.ds(0, half)], s_ad, ad_rs.at[0], loc.at[6])
    with scope("M_waitattn"):
        if half > 1:
            arrived(attn_r.at[pl.ds(0, half - 1)], r_attn1)
        pltpu.make_async_copy(attn_s.at[row], attn_r.at[row], loc.at[3]).wait()
    own_near = spread(attn_r.at[groups[1]], lambda d: attn_d.at[1, d, pl.ds(0, half)], s_ad, ad_rs.at[1], loc.at[7])
    ctx_copy(attn_r.at[:, pl.ds(pl.multiple_of(other * block, block), block)], attn_y, s_ap, r_ap, pair).start()
    send_dkv([2 * a + other for a in [partner] + mate_partners + mates] + [pair])
    with scope("N_handover0"):
        hand_over(lambda d: attn_d.at[0, d, pl.ds(0, half)], s_ad, ad_rs.at[0])
    with scope("N_handover1"):
        hand_over(lambda d: attn_d.at[1, d, pl.ds(0, half)], s_ad, ad_rs.at[1])
    with scope("N_waitspread"):
        own_far.wait()
        own_near.wait()
        for t in range(2):
            arrived(attn_d.at[t, pl.ds(0, dn // 2)], ad_rs.at[t, 0])
        arrived(g_r.at[other], r_gp)

    def weight(t, a):
        total = None
        for b in range(2):
            heads_of = attn_d[t, :, lax.rem(a, half), b * block:(b + 1) * block].reshape(dn * block, dh)
            term = dot_nn(transposed(heads_of), g_r[b].reshape(dn * block, dc))
            total = term if total is None else total + term
        return total

    def send_w(slot, value, dst, recv, peer_row):
        w_s[slot] = value.astype(bf16)
        ctx_copy(w_s.at[slot], dst, s_w, recv, 2 * peer_row + side).start()

    with scope("P_weight"):
        for k, a in enumerate(mate_partners):
            send_w(k, weight(0, a), w_x.at[row], r_wx, mates[k])
        crossing = weight(0, partner)
        for k, a in enumerate(mates):
            send_w(half - 1 + k, weight(1, a), w_m.at[row], r_wm, a)
        w_out[...] = weight(1, row)

    with scope("N_waitpair"):
        arrived(attn_y, r_ap)
    own_ae = spread(attn_y, lambda d: attn_e.at[d], s_ae, ae_rs, loc.at[8])

    def cross_sum(total):
        if mates:
            arrived(w_x.at[pl.ds(0, half - 1)], r_wx)
        for a in mates:
            total = total + w_x[a].astype(jnp.float32)
        send_w(rows - 2, total, w_p, r_wp, partner)

    with scope("O_handover"):
        hand_over(lambda d: attn_e.at[d], s_ae, ae_rs)
        own_ae.wait()
        arrived(attn_e.at[pl.ds(0, dn // 2)], ae_rs.at[0])

    mine = pl.ds(pl.multiple_of(side * block, block), block)

    def mix_step(j, carry):
        def two(ref, *at):
            return ref[at].reshape(width, dh)

        d = pl.ds(2 * j, 2)
        t_of = [row // half if a // half else 1 - row // half for a in range(rows)]
        here = jnp.concatenate([two(attn_d, t_of[a], d, a % half, mine) for a in range(rows)], axis=1)
        there = jnp.concatenate([two(attn_e, d, a) for a in range(rows)], axis=1)
        out = dot_nn(here, proj_r[side].reshape(rows * dh, dc)) + dot_nn(there, proj_r[other].reshape(rows * dh, dc))
        mix_s[d] = out.astype(bf16).reshape(2, block, dc)
        return carry

    with scope("Q_mix"):
        lax.fori_loop(0, dn // 2, mix_step, 0)
    for peer in dp_peers:
        dp_copy(mix_s.at[peer], mix_r.at[md], s_mix, r_mix, peer).start()
    own_mix = pltpu.make_async_copy(mix_s.at[md], mix_r.at[md], loc.at[9])
    own_mix.start()

    with scope("S_waitcross"):
        cross_sum(crossing)

    with scope("T_waitdq"):
        pltpu.make_async_copy(dq_s.at[me], dq_r.at[me], loc.at[4]).wait()
        arrived(dq_r.at[pl.ds(0, n - 1)], r_dq)
    with scope("U_waitdkv"):
        own_dkv.wait()
        arrived(dkv_r.at[pl.ds(0, n - 1)], r_dkv)
    with scope("W_waitmates"):
        if mates:
            arrived(w_m.at[pl.ds(0, half - 1)], r_wm)
        for a in mates:
            w_out[...] += w_m[a].astype(jnp.float32)
    with scope("X_waitpartner"):
        arrived(w_p, r_wp)
        w_out[...] += w_p[...].astype(jnp.float32)
    with scope("V_waitmix"):
        own_mix.wait()
        arrived(mix_r.at[pl.ds(0, dn - 1)], r_mix)

    with scope("Y_waitsend"):
        blocks = pl.ds(0, n - 1)
        others = pl.ds(0, dn - 1)
        sent(qkv_r.at[pl.ds(0, n - 1)], s_qkv)
        sent(proj_r.at[0, pl.ds(0, half + 1)], s_proj)
        passed = rows + half - 2
        sent(proj_r.at[:, pl.ds(0, passed // 2)] if passed % 2 == 0 else proj_r.at[0, pl.ds(0, passed)], s_pass)
        sent(g.at[others], s_g)
        sent(agp_s.at[:, others], s_agp)
        sent(ag_s.at[blocks], s_ag)
        sent(g_r.at[0], s_gp)
        sent(attn_s.at[pl.ds(0, rows - 1)], s_attn)
        sent(dq_s.at[blocks], s_dq)
        sent(dkv_s.at[blocks], s_dkv)
        sent(attn_d.at[:, others], s_ad)
        sent(attn_y, s_ap)
        sent(attn_e.at[others], s_ae)
        sent(w_s.at[pl.ds(0, rows - 1)], s_w)
        sent(mix_s.at[others], s_mix)


def shards(queries, keys, values, out_grad, chosen, proj):
    n = lax.axis_size("ctx")
    dn = lax.axis_size("dp")
    tokens = queries.shape[1]
    hd = queries.shape[2]
    dh = hd // n
    dc = proj.shape[1]
    slots = n * BLOCK
    width = 2 * BLOCK
    rows = n // 2
    half = rows // 2
    bf16, f32 = jnp.bfloat16, jnp.float32
    sem = pltpu.SemaphoreType.DMA
    blocks = (n, BLOCK, dh)
    pairs = (rows, width, dh)
    sheets = (rows, dh, dc)
    buffers = [
        ((3, tokens, hd), bf16), ((tokens, dn * dc), bf16), ((n, 3, BLOCK, dh), bf16), ((dn, BLOCK, dc), bf16),
        ((slots, BLOCK), jnp.int32), ((n, 3, BLOCK, dh), bf16), ((2, dn, BLOCK, dc), bf16), ((2,) + sheets, bf16),
        ((n, dn, BLOCK, dh), bf16), ((n, dn, BLOCK, dh), bf16), (blocks, bf16), (blocks, bf16),
        (pairs, bf16), (pairs, bf16), ((rows, BLOCK, dh), bf16), ((2, dn, half, width, dh), bf16),
        ((dn, rows, BLOCK, dh), bf16), ((rows, dh, width), bf16),
        ((rows, slots, width), bf16), ((dh, slots), bf16), ((dh, slots), bf16),
        (blocks, bf16), ((n, 2, BLOCK, dh), bf16), ((slots, dh), f32), ((slots, dh), f32),
        (sheets, bf16), (sheets, bf16), (sheets, bf16), ((dh, dc), bf16), ((dn, BLOCK, dc), bf16),
    ]
    held = sum(math.prod(shape) * jnp.dtype(kind).itemsize for shape, kind in buffers)
    sems = [sem((15,)), sem((12,)), sem((2, rows)), sem((n,)), sem((rows,)), sem((2, dn // 2)), sem((dn // 2,)), sem((11,))]
    vmem = pl.BlockSpec(memory_space=pltpu.VMEM)
    picks = pltpu.SMEM(chosen.shape, chosen.dtype)
    free = pl.BlockSpec(memory_space=pl.ANY)
    hbm = pl.BlockSpec(memory_space=pltpu.HBM)

    def kept(x):
        return pltpu.with_memory_space_constraint(x, pltpu.HBM)

    chosen = kept(chosen)
    dq, dkv, weight_grad, mixed = pl.pallas_call(
        functools.partial(kernel, n, dn, 1.0 / math.sqrt(dh)),
        out_shape=(
            jax.ShapeDtypeStruct(blocks, bf16),
            jax.ShapeDtypeStruct((n, 2, BLOCK, dh), bf16),
            jax.ShapeDtypeStruct((dh, dc), f32),
            jax.ShapeDtypeStruct((dn, BLOCK, dc), bf16),
        ),
        in_specs=[hbm] * 6,
        out_specs=[free, free, vmem, free],
        scratch_shapes=[picks] + [pltpu.VMEM(shape, kind) for shape, kind in buffers] + sems,
        compiler_params=pltpu.CompilerParams(
            collective_id=0, has_side_effects=True, vmem_limit_bytes=min(held + SPARE, 60 * MIB)),
    )(chosen, *[kept(x) for x in (queries[0], keys[0], values[0], out_grad[0], proj)])

    wide = (tokens, dn * dc)
    thin = (tokens, hd)
    count = tokens // BLOCK
    out, q_grad, k_grad, v_grad, proj_grad = pl.pallas_call(
        functools.partial(place_kernel, n, dn, count),
        out_shape=(
            jax.ShapeDtypeStruct(wide, bf16), jax.ShapeDtypeStruct(thin, bf16), jax.ShapeDtypeStruct(thin, bf16),
            jax.ShapeDtypeStruct(thin, bf16), jax.ShapeDtypeStruct((dh, dc), f32)),
        in_specs=[hbm] + [free] * 4,
        out_specs=[hbm] * 5,
        scratch_shapes=[picks, pltpu.VMEM((BLOCK, max(dn * dc, hd)), bf16), sem((count, 4)), sem((2,))],
        compiler_params=pltpu.CompilerParams(vmem_limit_bytes=8 * MIB),
    )(chosen, mixed, dq, dkv, weight_grad)
    return out[None], q_grad[None], k_grad[None], v_grad[None], proj_grad


def solution(mesh):
    rows = P("dp", "ctx", None)
    return jax.shard_map(
        shards,
        mesh=mesh,
        in_specs=(rows, rows, rows, rows, P("dp", None), P("ctx", "dp")),
        out_specs=(rows, rows, rows, rows, P("ctx", "dp")),
        check_vma=False,
    )
```

```python
import functools
import math

import jax
import jax.numpy as jnp
from jax import lax
from jax.experimental import pallas as pl
from jax.experimental.pallas import tpu as pltpu
from jax.sharding import PartitionSpec as P

BLOCK = 128
FAR = 1 << 30
MIB = 1024 * 1024
SPARE = 8 * MIB

scope = jax.named_scope


def dot_nt(a, b):
    return lax.dot_general(a, b, (((1,), (1,)), ((), ())), preferred_element_type=jnp.float32)


def dot_nn(a, b):
    return lax.dot_general(a, b, (((1,), (0,)), ((), ())), preferred_element_type=jnp.float32)


def transposed(a):
    return a.astype(jnp.float32).T.astype(a.dtype)


def local_block(picked, me, count):
    entry = picked[0, me]
    spans = count // 2
    index = jnp.maximum(entry, 0)
    local = jnp.where(index // spans == me, index % spans, spans + index % spans)
    return entry, local


def block_marks(picked, me, count):
    entry, local = local_block(picked, me, count)
    local = jnp.where(entry >= 0, local, -1)
    return [jnp.where(local == j, 1.0, 0.0) for j in range(count)]


def place_kernel(n, dn, count, chosen, mix, dq, dkv, w, out, q_out, k_out, v_out, w_out, picked, zero, sems, w_sem):
    block, dh, dc = dq.shape[1], dq.shape[2], mix.shape[2]
    pick = pltpu.make_async_copy(chosen, picked, w_sem.at[1])
    pick.start()
    w_copy = pltpu.make_async_copy(w, w_out, w_sem.at[0])
    w_copy.start()
    zero[...] = jnp.zeros_like(zero)
    pick.wait()
    entry, local = local_block(picked, lax.axis_index("ctx"), count)
    local = jnp.where(entry >= 0, local, -1)
    outs = (out, q_out, k_out, v_out)
    for j in range(count):
        rows = pl.ds(j * block, block)

        @pl.when(local == j)
        def _():
            for d in range(dn):
                pltpu.make_async_copy(mix.at[d], out.at[rows, pl.ds(d * dc, dc)], sems.at[j, 0]).start()
            for h in range(n):
                cols = pl.ds(h * dh, dh)
                pltpu.make_async_copy(dq.at[h], q_out.at[rows, cols], sems.at[j, 1]).start()
                pltpu.make_async_copy(dkv.at[h, 0], k_out.at[rows, cols], sems.at[j, 2]).start()
                pltpu.make_async_copy(dkv.at[h, 1], v_out.at[rows, cols], sems.at[j, 3]).start()

        @pl.when(local != j)
        def _():
            for t, dst in enumerate(outs):
                pltpu.make_async_copy(zero.at[:, pl.ds(0, dst.shape[1])], dst.at[rows], sems.at[j, t]).start()

    for j in range(count):
        for t, dst in enumerate(outs):
            view = dst.at[pl.ds(j * block, block)]
            pltpu.make_async_copy(view, view, sems.at[j, t]).wait()
    w_copy.wait()


def kernel(
    n, dn, scale,
    chosen, q_hbm, k_hbm, v_hbm, g_hbm, proj,
    dq_r, dkv_r, w_out, mix_r,
    picked, qkv_in, g_in, qkv, g, kpos, qkv_r, g_r, proj_r, agp_s, agp_r, ag_s, ag_r,
    attn_s, attn_r, attn_y, attn_d, attn_e, attn_t,
    p_s, k_t, v_t, dq_s, dkv_s, dk_acc, dv_acc, w_s, w_x, w_m, w_p, mix_s,
    ss, rs, proj_rs, g_rs, agp_rs, ag_rs, ad_rs, ae_rs, loc,
):
    me = lax.axis_index("ctx")
    md = lax.axis_index("dp")
    bf16 = jnp.bfloat16
    block, dh = qkv.shape[2], qkv.shape[3]
    dc = proj.shape[1]
    slots = n * block
    width = 2 * block
    rows = n // 2
    half = rows // 2
    s_proj, s_g, s_qkv, s_agp, s_ag, s_gp, s_attn, s_dq, s_dkv, s_ad, s_ap, s_ae, s_w, s_mix, s_pass, s_pp = (
        ss.at[k] for k in range(16))
    r_pp, r_qkv, r_gp, r_attn0, r_attn1, r_dq, r_dkv, r_ap, r_wx, r_wm, r_wp, r_mix = (rs.at[k] for k in range(12))

    def ctx_copy(src, dst, send, recv, peer):
        return pltpu.make_async_remote_copy(
            src_ref=src, dst_ref=dst, send_sem=send, recv_sem=recv,
            device_id={"ctx": peer}, device_id_type=pl.DeviceIdType.MESH)

    def dp_copy(src, dst, send, recv, peer):
        return pltpu.make_async_remote_copy(
            src_ref=src, dst_ref=dst, send_sem=send, recv_sem=recv,
            device_id={"dp": peer}, device_id_type=pl.DeviceIdType.MESH)

    ctx_peers = [lax.rem(me + s, n) for s in range(1, n)]
    dp_peers = [lax.rem(md + s, dn) for s in range(1, dn)]

    barrier = pltpu.get_barrier_semaphore()
    for peer in ctx_peers:
        pl.semaphore_signal(barrier, inc=1, device_id={"ctx": peer}, device_id_type=pl.DeviceIdType.MESH)
    for peer in dp_peers:
        pl.semaphore_signal(barrier, inc=1, device_id={"dp": peer}, device_id_type=pl.DeviceIdType.MESH)

    row = me // 2
    side = lax.rem(me, 2)
    other = 1 - side
    pair = me + 1 - 2 * side
    own_base = (row // half) * half
    far_base = half - own_base

    def near(s):
        return own_base + lax.rem(row + s, half)

    def across(s):
        return far_base + lax.rem(row + s, half)

    mates = [near(s) for s in range(1, half)]
    partner = across(0)
    mate_partners = [across(s) for s in range(1, half)]

    pick = pltpu.make_async_copy(chosen, picked, loc.at[10])
    pick.start()
    own_proj = pltpu.make_async_copy(proj, proj_r.at[side, row], loc.at[0])
    g_load = pltpu.make_async_copy(g_hbm, g_in, loc.at[1])
    g_load.start()
    for t, src in enumerate((q_hbm, k_hbm, v_hbm)):
        pltpu.make_async_copy(src, qkv_in.at[t], loc.at[2]).start()
    own_proj.start()
    pick.wait()
    marks = block_marks(picked, me, qkv_in.shape[1] // block)

    def chosen_rows(load):
        total = None
        for j, mark in enumerate(marks):
            term = load(slice(j * block, (j + 1) * block)).astype(jnp.float32) * mark
            total = term if total is None else total + term
        return total.astype(bf16)

    def arrived(view, recv):
        ctx_copy(view, view, s_proj, recv, pair).wait_recv()

    def sent(view, send):
        ctx_copy(view, view, send, r_pp, pair).wait_send()

    with scope("A_load"):
        g_load.wait()
        for j in range(dn):
            g[j] = chosen_rows(lambda r: g_in[r, j * dc:(j + 1) * dc])
        g_r[side, md] = g[md]
        pltpu.make_async_copy(qkv_in, qkv_in, loc.at[2]).wait()
        for t in range(3):
            for h in range(n):
                qkv[h, t] = chosen_rows(lambda r: qkv_in[t, r, h * dh:(h + 1) * dh])
        qkv_r[me] = qkv[me]
    with scope("B_barrier"):
        pl.semaphore_wait(barrier, n - 1 + dn - 1)

    twin = md + 1 - 2 * lax.rem(md, 2)
    dp_far = [lax.rem(md + 2 * s, dn) for s in range(1, dn // 2)]
    dp_cross = [lax.rem(twin + 2 * s, dn) for s in range(1, dn // 2)]

    own_block = proj_r.at[side, row]
    for a in [partner] + mates:
        ctx_copy(proj, own_block, s_proj, proj_rs.at[row], 2 * a + side).start()
    for peer in dp_far + dp_cross + [twin]:
        dp_copy(g.at[peer], g_r.at[side, md], s_g, g_rs.at[md], peer).start()
    ctx_copy(g.at[md], g_r.at[side, md], s_gp, r_gp, pair).start()

    def send_qkv(peers):
        for peer in peers:
            ctx_copy(qkv.at[peer], qkv_r.at[me], s_qkv, r_qkv, peer).start()

    send_qkv([2 * a + side for a in [partner] + mate_partners])

    down = lax.broadcasted_iota(jnp.int32, (block, block), 0)
    for j in range(n):
        entry = picked[0, j]
        kpos[j * block:(j + 1) * block] = down + jnp.where(entry >= 0, entry * block, FAR)

    def proj_arrived(a):
        arrived(proj_r.at[side, a], proj_rs.at[a])

    with scope("C_waitg"):
        for peer in [twin] + dp_far + dp_cross:
            view = g_r.at[side, peer]
            arrived(view, g_rs.at[peer])
            ctx_copy(view, view, s_gp, r_gp, pair).start()
    with scope("D_waitpartner"):
        proj_arrived(partner)
        view = proj_r.at[side, partner]
        for a in mates:
            ctx_copy(view, view, s_pass, proj_rs.at[partner], 2 * a + side).start()
    send_qkv([2 * a + other for a in [partner] + mate_partners])
    send_qkv([2 * a + s for a in mates for s in (side, other)] + [pair])
    own_proj.wait()

    def part(a, b):
        k = 2 * a + b
        out = dot_nt(g_r[b].reshape(dn * block, dc), proj_r[side, a]).astype(bf16)
        agp_s[k] = out.reshape(dn, block, dh)
        for peer in dp_far + dp_cross + [twin]:
            dp_copy(agp_s.at[k, peer], agp_r.at[k, md], s_agp, agp_rs.at[k], peer).start()

    def finish(a, b):
        k = 2 * a + b
        arrived(agp_r.at[k, pl.ds(0, dn - 1)], agp_rs.at[k])
        total = agp_s[k, md].astype(jnp.float32)
        for peer in dp_peers:
            total = total + agp_r[k, peer].astype(jnp.float32)
        if a is row:
            ag_r[2 * row + b] = total.astype(bf16)
        else:
            ag_s[k] = total.astype(bf16)
            ctx_copy(ag_s.at[k], ag_r.at[2 * row + b], s_ag, ag_rs.at[row], 2 * a + side).start()

    def parts(names, b, waiting, lag):
        for a in names:
            with scope("G_part"):
                part(a, b)
            waiting.append((a, b))
            if len(waiting) > lag:
                with scope("H_finish"):
                    finish(*waiting.pop(0))

    waiting = []
    with scope("E_waitmate"):
        for a in mates:
            proj_arrived(a)
    parts([partner] + mates + [row], side, waiting, n)
    with scope("F_waitsecond"):
        for a in mate_partners:
            proj_arrived(a)
    parts(mate_partners, side, waiting, n)
    with scope("F_waitpairg"):
        arrived(g_r.at[other], r_gp)
    parts([partner] + mate_partners + mates + [row], other, waiting, rows)
    with scope("H_finish"):
        for a, b in waiting:
            finish(a, b)
    ctx_copy(proj_r.at[side], proj_r.at[side], s_pp, r_pp, pair).start()

    with scope("I_waitqkv"):
        arrived(qkv_r.at[pl.ds(0, n - 1)], r_qkv)
    k_t[...] = transposed(qkv_r[:, 1].reshape(slots, dh))
    v_t[...] = transposed(qkv_r[:, 2].reshape(slots, dh))

    def ordered(k):
        late = k // half
        return far_base * (1 - late) + own_base * late + lax.rem(row + k + late, half)

    def forward(k, carry):
        i = ordered(k)
        q = qkv_r[pl.ds(2 * i, 2), 0].reshape(width, dh)
        keys = qkv_r[:, 1].reshape(slots, dh)
        scores = dot_nt(keys, q) * scale
        key_pos = kpos[...]
        key_pos = jnp.concatenate([key_pos, key_pos], axis=1)
        same = lax.broadcasted_iota(jnp.int32, (slots, width), 0) == (
            lax.broadcasted_iota(jnp.int32, (slots, width), 1) + i * width)
        lane = lax.broadcasted_iota(jnp.int32, (1, width), 1)
        one, two = picked[0, 2 * i], picked[0, 2 * i + 1]
        one = jnp.where(one >= 0, one * block, -FAR)
        two = jnp.where(two >= 0, (two - 1) * block, -FAR)
        query_pos = lane + jnp.where(lane < block, one, two)
        scores = jnp.where((key_pos <= query_pos) | same, scores, -1e30)
        e = jnp.exp(scores - jnp.max(scores, axis=0, keepdims=True))
        p = (e * (1.0 / jnp.sum(e, axis=0, keepdims=True))).astype(bf16)
        p_s[i] = p
        a_t = dot_nn(v_t[...], p)
        attn_t[i] = a_t.astype(bf16)
        attn_s[i] = a_t.T.astype(bf16)

        @pl.when(k < half)
        def _():
            ctx_copy(attn_s.at[i], attn_r.at[row], s_attn, r_attn0, 2 * i + side).start()

        @pl.when((k >= half) & (k < rows - 1))
        def _():
            ctx_copy(attn_s.at[i], attn_r.at[row], s_attn, r_attn1, 2 * i + side).start()

        @pl.when(k == rows - 1)
        def _():
            pltpu.make_async_copy(attn_s.at[i], attn_r.at[i], loc.at[3]).start()

        return carry

    with scope("J_forward"):
        lax.fori_loop(0, rows, forward, 0)

    dk_acc[...] = jnp.zeros_like(dk_acc)
    dv_acc[...] = jnp.zeros_like(dv_acc)

    def backward(k, carry):
        i = ordered(k)
        with scope("K_waitag"):
            @pl.when(k < rows - 1)
            def _():
                arrived(ag_r.at[pl.ds(2 * i, 2)], ag_rs.at[i])

        q = qkv_r[pl.ds(2 * i, 2), 0].reshape(width, dh)
        v = qkv_r[:, 2].reshape(slots, dh)
        da = ag_r[pl.ds(2 * i, 2)].reshape(width, dh)
        delta = jnp.sum(da.astype(jnp.float32).T * attn_t[i].astype(jnp.float32), axis=0, keepdims=True)
        p = p_s[i]
        ds = (p.astype(jnp.float32) * (dot_nt(v, da) - delta)).astype(bf16)
        dq_t = dot_nn(k_t[...], ds) * scale
        dq_s[pl.ds(2 * i, 2)] = dq_t.T.astype(bf16).reshape(2, block, dh)
        for t in range(2):
            peer = 2 * i + t

            @pl.when(peer != me)
            def _():
                ctx_copy(dq_s.at[peer], dq_r.at[me], s_dq, r_dq, peer).start()

            @pl.when(peer == me)
            def _():
                pltpu.make_async_copy(dq_s.at[peer], dq_r.at[peer], loc.at[4]).start()

        dk_acc[...] += dot_nn(ds, q)
        dv_acc[...] += dot_nn(p, da)
        return carry

    with scope("L_backward"):
        lax.fori_loop(0, rows, backward, 0)

    dkv_s[:, 0] = (dk_acc[...] * scale).astype(bf16).reshape(n, block, dh)
    dkv_s[:, 1] = dv_acc[...].astype(bf16).reshape(n, block, dh)

    def send_dkv(peers):
        for peer in peers:
            ctx_copy(dkv_s.at[peer], dkv_r.at[me], s_dkv, r_dkv, peer).start()

    send_dkv([2 * a + side for a in [partner] + mate_partners + mates])
    own_dkv = pltpu.make_async_copy(dkv_s.at[me], dkv_r.at[me], loc.at[5])
    own_dkv.start()

    def spread(src, dst_of, send, recv, own_sem):
        for s, peer in enumerate(dp_far):
            dp_copy(src, dst_of(md), send, recv.at[1 + s], peer).start()
        dp_copy(src, dst_of(md), send, recv.at[0], twin).start()
        copy = pltpu.make_async_copy(src, dst_of(md), own_sem)
        copy.start()
        return copy

    def hand_over(dst_of, send, recv):
        for s in range(1, dn // 2):
            peer = lax.rem(md + dn - 2 * s, dn)
            arrived(dst_of(peer), recv.at[s])
            dp_copy(dst_of(peer), dst_of(peer), send, recv.at[0], twin).start()

    groups = [pl.ds(far_base, half), pl.ds(own_base, half)]
    with scope("M_waitattn"):
        arrived(attn_r.at[groups[0]], r_attn0)
    own_far = spread(attn_r.at[groups[0]], lambda d: attn_d.at[0, d, pl.ds(0, half)], s_ad, ad_rs.at[0], loc.at[6])
    with scope("M_waitattn"):
        if half > 1:
            arrived(attn_r.at[pl.ds(0, half - 1)], r_attn1)
        pltpu.make_async_copy(attn_s.at[row], attn_r.at[row], loc.at[3]).wait()
    own_near = spread(attn_r.at[groups[1]], lambda d: attn_d.at[1, d, pl.ds(0, half)], s_ad, ad_rs.at[1], loc.at[7])
    ctx_copy(attn_r.at[:, pl.ds(pl.multiple_of(other * block, block), block)], attn_y, s_ap, r_ap, pair).start()
    send_dkv([2 * a + other for a in [partner] + mate_partners + mates] + [pair])
    with scope("N_handover0"):
        hand_over(lambda d: attn_d.at[0, d, pl.ds(0, half)], s_ad, ad_rs.at[0])
    with scope("N_waitpair"):
        arrived(attn_y, r_ap)
    own_ae = spread(attn_y, lambda d: attn_e.at[d], s_ae, ae_rs, loc.at[8])
    with scope("N_handover1"):
        hand_over(lambda d: attn_d.at[1, d, pl.ds(0, half)], s_ad, ad_rs.at[1])
    with scope("N_waitspread"):
        own_far.wait()
        own_near.wait()
        for t in range(2):
            arrived(attn_d.at[t, pl.ds(0, dn // 2)], ad_rs.at[t, 0])

    def weight(t, a):
        total = None
        for b in range(2):
            heads_of = attn_d[t, :, lax.rem(a, half), b * block:(b + 1) * block].reshape(dn * block, dh)
            term = dot_nn(transposed(heads_of), g_r[b].reshape(dn * block, dc))
            total = term if total is None else total + term
        return total

    def send_w(slot, value, dst, recv, peer_row):
        w_s[slot] = value.astype(bf16)
        ctx_copy(w_s.at[slot], dst, s_w, recv, 2 * peer_row + side).start()

    with scope("P_weight"):
        for k, a in enumerate(mate_partners):
            send_w(k, weight(0, a), w_x.at[row], r_wx, mates[k])
        crossing = weight(0, partner)
        for k, a in enumerate(mates):
            send_w(half - 1 + k, weight(1, a), w_m.at[row], r_wm, a)
        w_out[...] = weight(1, row)


    def cross_sum(total):
        if mates:
            arrived(w_x.at[pl.ds(0, half - 1)], r_wx)
        for a in mates:
            total = total + w_x[a].astype(jnp.float32)
        send_w(rows - 2, total, w_p, r_wp, partner)

    with scope("O_handover"):
        hand_over(lambda d: attn_e.at[d], s_ae, ae_rs)
    with scope("S_waitcross"):
        cross_sum(crossing)
    with scope("O_waitrows"):
        arrived(proj_r.at[other], r_pp)
        own_ae.wait()
        arrived(attn_e.at[pl.ds(0, dn // 2)], ae_rs.at[0])

    mine = pl.ds(pl.multiple_of(side * block, block), block)

    def mix_step(j, carry):
        def two(ref, *at):
            return ref[at].reshape(width, dh)

        d = pl.ds(2 * j, 2)
        t_of = [row // half if a // half else 1 - row // half for a in range(rows)]
        here = jnp.concatenate([two(attn_d, t_of[a], d, a % half, mine) for a in range(rows)], axis=1)
        there = jnp.concatenate([two(attn_e, d, a) for a in range(rows)], axis=1)
        out = dot_nn(here, proj_r[side].reshape(rows * dh, dc)) + dot_nn(there, proj_r[other].reshape(rows * dh, dc))
        mix_s[d] = out.astype(bf16).reshape(2, block, dc)
        return carry

    with scope("Q_mix"):
        lax.fori_loop(0, dn // 2, mix_step, 0)
    for peer in dp_peers:
        dp_copy(mix_s.at[peer], mix_r.at[md], s_mix, r_mix, peer).start()
    own_mix = pltpu.make_async_copy(mix_s.at[md], mix_r.at[md], loc.at[9])
    own_mix.start()

    with scope("T_waitdq"):
        pltpu.make_async_copy(dq_s.at[me], dq_r.at[me], loc.at[4]).wait()
        arrived(dq_r.at[pl.ds(0, n - 1)], r_dq)
    with scope("U_waitdkv"):
        own_dkv.wait()
        arrived(dkv_r.at[pl.ds(0, n - 1)], r_dkv)
    with scope("W_waitmates"):
        if mates:
            arrived(w_m.at[pl.ds(0, half - 1)], r_wm)
        for a in mates:
            w_out[...] += w_m[a].astype(jnp.float32)
    with scope("X_waitpartner"):
        arrived(w_p, r_wp)
        w_out[...] += w_p[...].astype(jnp.float32)
    with scope("V_waitmix"):
        own_mix.wait()
        arrived(mix_r.at[pl.ds(0, dn - 1)], r_mix)

    with scope("Y_waitsend"):
        blocks = pl.ds(0, n - 1)
        others = pl.ds(0, dn - 1)
        sent(qkv_r.at[pl.ds(0, n - 1)], s_qkv)
        sent(proj_r.at[0, pl.ds(0, half)], s_proj)
        if mates:
            sent(proj_r.at[0, pl.ds(0, half - 1)], s_pass)
        sent(proj_r.at[0], s_pp)
        sent(g.at[others], s_g)
        sent(agp_s.at[:, others], s_agp)
        sent(ag_s.at[pl.ds(0, n - 2)], s_ag)
        sent(g_r.at[0], s_gp)
        sent(attn_s.at[pl.ds(0, rows - 1)], s_attn)
        sent(dq_s.at[blocks], s_dq)
        sent(dkv_s.at[blocks], s_dkv)
        sent(attn_d.at[:, others], s_ad)
        sent(attn_y, s_ap)
        sent(attn_e.at[others], s_ae)
        sent(w_s.at[pl.ds(0, rows - 1)], s_w)
        sent(mix_s.at[others], s_mix)


def shards(queries, keys, values, out_grad, chosen, proj):
    n = lax.axis_size("ctx")
    dn = lax.axis_size("dp")
    tokens = queries.shape[1]
    hd = queries.shape[2]
    dh = hd // n
    dc = proj.shape[1]
    slots = n * BLOCK
    width = 2 * BLOCK
    rows = n // 2
    half = rows // 2
    bf16, f32 = jnp.bfloat16, jnp.float32
    sem = pltpu.SemaphoreType.DMA
    blocks = (n, BLOCK, dh)
    pairs = (rows, width, dh)
    sheets = (rows, dh, dc)
    buffers = [
        ((3, tokens, hd), bf16), ((tokens, dn * dc), bf16), ((n, 3, BLOCK, dh), bf16), ((dn, BLOCK, dc), bf16),
        ((slots, BLOCK), jnp.int32), ((n, 3, BLOCK, dh), bf16), ((2, dn, BLOCK, dc), bf16), ((2,) + sheets, bf16),
        ((n, dn, BLOCK, dh), bf16), ((n, dn, BLOCK, dh), bf16), (blocks, bf16), (blocks, bf16),
        (pairs, bf16), (pairs, bf16), ((rows, BLOCK, dh), bf16), ((2, dn, half, width, dh), bf16),
        ((dn, rows, BLOCK, dh), bf16), ((rows, dh, width), bf16),
        ((rows, slots, width), bf16), ((dh, slots), bf16), ((dh, slots), bf16),
        (blocks, bf16), ((n, 2, BLOCK, dh), bf16), ((slots, dh), f32), ((slots, dh), f32),
        (sheets, bf16), (sheets, bf16), (sheets, bf16), ((dh, dc), bf16), ((dn, BLOCK, dc), bf16),
    ]
    held = sum(math.prod(shape) * jnp.dtype(kind).itemsize for shape, kind in buffers)
    sems = [sem((16,)), sem((12,)), sem((rows,)), sem((dn,)), sem((n,)), sem((rows,)), sem((2, dn // 2)), sem((dn // 2,)), sem((11,))]
    vmem = pl.BlockSpec(memory_space=pltpu.VMEM)
    picks = pltpu.SMEM(chosen.shape, chosen.dtype)
    free = pl.BlockSpec(memory_space=pl.ANY)
    hbm = pl.BlockSpec(memory_space=pltpu.HBM)

    def kept(x):
        return pltpu.with_memory_space_constraint(x, pltpu.HBM)

    chosen = kept(chosen)
    dq, dkv, weight_grad, mixed = pl.pallas_call(
        functools.partial(kernel, n, dn, 1.0 / math.sqrt(dh)),
        out_shape=(
            jax.ShapeDtypeStruct(blocks, bf16),
            jax.ShapeDtypeStruct((n, 2, BLOCK, dh), bf16),
            jax.ShapeDtypeStruct((dh, dc), f32),
            jax.ShapeDtypeStruct((dn, BLOCK, dc), bf16),
        ),
        in_specs=[hbm] * 6,
        out_specs=[free, free, vmem, free],
        scratch_shapes=[picks] + [pltpu.VMEM(shape, kind) for shape, kind in buffers] + sems,
        compiler_params=pltpu.CompilerParams(
            collective_id=0, has_side_effects=True, vmem_limit_bytes=min(held + SPARE, 60 * MIB)),
    )(chosen, *[kept(x) for x in (queries[0], keys[0], values[0], out_grad[0], proj)])

    wide = (tokens, dn * dc)
    thin = (tokens, hd)
    count = tokens // BLOCK
    out, q_grad, k_grad, v_grad, proj_grad = pl.pallas_call(
        functools.partial(place_kernel, n, dn, count),
        out_shape=(
            jax.ShapeDtypeStruct(wide, bf16), jax.ShapeDtypeStruct(thin, bf16), jax.ShapeDtypeStruct(thin, bf16),
            jax.ShapeDtypeStruct(thin, bf16), jax.ShapeDtypeStruct((dh, dc), f32)),
        in_specs=[hbm] + [free] * 4,
        out_specs=[hbm] * 5,
        scratch_shapes=[picks, pltpu.VMEM((BLOCK, max(dn * dc, hd)), bf16), sem((count, 4)), sem((2,))],
        compiler_params=pltpu.CompilerParams(vmem_limit_bytes=8 * MIB),
    )(chosen, mixed, dq, dkv, weight_grad)
    return out[None], q_grad[None], k_grad[None], v_grad[None], proj_grad


def solution(mesh):
    rows = P("dp", "ctx", None)
    return jax.shard_map(
        shards,
        mesh=mesh,
        in_specs=(rows, rows, rows, rows, P("dp", None), P("ctx", "dp")),
        out_specs=(rows, rows, rows, rows, P("ctx", "dp")),
        check_vma=False,
    )
```

```python
import functools
import math

import jax
import jax.numpy as jnp
from jax import lax
from jax.experimental import pallas as pl
from jax.experimental.pallas import tpu as pltpu
from jax.sharding import PartitionSpec as P

BLOCK = 128
FAR = 1 << 30
MIB = 1024 * 1024
LOG2E = math.log2(math.e)
SPARE = 8 * MIB

scope = jax.named_scope


def dot_nt(a, b):
    return lax.dot_general(a, b, (((1,), (1,)), ((), ())), preferred_element_type=jnp.float32)


def dot_nn(a, b):
    return lax.dot_general(a, b, (((1,), (0,)), ((), ())), preferred_element_type=jnp.float32)


def transposed(a):
    return a.astype(jnp.float32).T.astype(a.dtype)


def local_block(picked, me, count):
    entry = picked[0, me]
    spans = count // 2
    index = jnp.maximum(entry, 0)
    local = jnp.where(index // spans == me, index % spans, spans + index % spans)
    return entry, local


def block_marks(picked, me, count):
    entry, local = local_block(picked, me, count)
    local = jnp.where(entry >= 0, local, -1)
    return [jnp.where(local == j, 1.0, 0.0) for j in range(count)]


def place_kernel(n, dn, count, chosen, mix, dq, dkv, w, out, q_out, k_out, v_out, w_out, picked, zero, sems, w_sem):
    block, dh, dc = dq.shape[1], dq.shape[2], mix.shape[2]
    pick = pltpu.make_async_copy(chosen, picked, w_sem.at[1])
    pick.start()
    w_copy = pltpu.make_async_copy(w, w_out, w_sem.at[0])
    w_copy.start()
    zero[...] = jnp.zeros_like(zero)
    pick.wait()
    entry, local = local_block(picked, lax.axis_index("ctx"), count)
    local = jnp.where(entry >= 0, local, -1)
    outs = (out, q_out, k_out, v_out)
    for j in range(count):
        rows = pl.ds(j * block, block)

        @pl.when(local == j)
        def _():
            for d in range(dn):
                pltpu.make_async_copy(mix.at[d], out.at[rows, pl.ds(d * dc, dc)], sems.at[j, 0]).start()
            for h in range(n):
                cols = pl.ds(h * dh, dh)
                pltpu.make_async_copy(dq.at[h], q_out.at[rows, cols], sems.at[j, 1]).start()
                pltpu.make_async_copy(dkv.at[h, 0], k_out.at[rows, cols], sems.at[j, 2]).start()
                pltpu.make_async_copy(dkv.at[h, 1], v_out.at[rows, cols], sems.at[j, 3]).start()

        @pl.when(local != j)
        def _():
            for t, dst in enumerate(outs):
                pltpu.make_async_copy(zero.at[:, pl.ds(0, dst.shape[1])], dst.at[rows], sems.at[j, t]).start()

    for j in range(count):
        for t, dst in enumerate(outs):
            view = dst.at[pl.ds(j * block, block)]
            pltpu.make_async_copy(view, view, sems.at[j, t]).wait()
    w_copy.wait()


def kernel(
    n, dn, scale,
    chosen, q_hbm, k_hbm, v_hbm, g_hbm, proj,
    dq_r, dkv_r, w_out, mix_r, kept_out,
    picked, qkv_in, g_in, qkv, g, kpos, qkv_r, g_r, proj_r, agp_s, agp_r, ag_s, ag_r,
    attn_s, attn_r, attn_y, attn_d, attn_e, attn_t,
    p_s, k_t, v_t, dq_s, dkv_s, dk_acc, dv_acc, w_c, w_s, w_x, w_m, w_p, mix_s,
    ss, rs, proj_rs, g_rs, agp_rs, ag_rs, ad_rs, ae_rs, loc,
):
    me = lax.axis_index("ctx")
    md = lax.axis_index("dp")
    bf16 = jnp.bfloat16
    block, dh = qkv.shape[2], qkv.shape[3]
    dc = proj.shape[1]
    slots = n * block
    width = 2 * block
    rows = n // 2
    half = rows // 2
    s_proj, s_g, s_qkv, s_agp, s_ag, s_gp, s_attn, s_dq, s_dkv, s_ad, s_ap, s_ae, s_w, s_mix, s_pass, s_pp = (
        ss.at[k] for k in range(16))
    r_pp, r_qkv, r_gp, r_attn0, r_attn1, r_dq, r_dkv, r_ap, r_wx, r_wm, r_wp, r_mix = (rs.at[k] for k in range(12))

    def ctx_copy(src, dst, send, recv, peer):
        return pltpu.make_async_remote_copy(
            src_ref=src, dst_ref=dst, send_sem=send, recv_sem=recv,
            device_id={"ctx": peer}, device_id_type=pl.DeviceIdType.MESH)

    def dp_copy(src, dst, send, recv, peer):
        return pltpu.make_async_remote_copy(
            src_ref=src, dst_ref=dst, send_sem=send, recv_sem=recv,
            device_id={"dp": peer}, device_id_type=pl.DeviceIdType.MESH)

    ctx_peers = [lax.rem(me + s, n) for s in range(1, n)]
    dp_peers = [lax.rem(md + s, dn) for s in range(1, dn)]

    barrier = pltpu.get_barrier_semaphore()
    for peer in ctx_peers:
        pl.semaphore_signal(barrier, inc=1, device_id={"ctx": peer}, device_id_type=pl.DeviceIdType.MESH)
    for peer in dp_peers:
        pl.semaphore_signal(barrier, inc=1, device_id={"dp": peer}, device_id_type=pl.DeviceIdType.MESH)

    row = me // 2
    side = lax.rem(me, 2)
    other = 1 - side
    pair = me + 1 - 2 * side
    own_base = (row // half) * half
    far_base = half - own_base

    def near(s):
        return own_base + lax.rem(row + s, half)

    def across(s):
        return far_base + lax.rem(row + s, half)

    mates = [near(s) for s in range(1, half)]
    partner = across(0)
    mate_partners = [across(s) for s in range(1, half)]

    pick = pltpu.make_async_copy(chosen, picked, loc.at[10])
    pick.start()
    own_proj = pltpu.make_async_copy(proj, proj_r.at[side, row], loc.at[0])
    g_load = pltpu.make_async_copy(g_hbm, g_in, loc.at[1])
    g_load.start()
    for t, src in enumerate((q_hbm, k_hbm, v_hbm)):
        pltpu.make_async_copy(src, qkv_in.at[t], loc.at[2]).start()
    own_proj.start()
    pltpu.make_async_copy(chosen, kept_out, loc.at[11]).start()
    pick.wait()
    marks = block_marks(picked, me, qkv_in.shape[1] // block)

    def chosen_rows(load):
        total = None
        for j, mark in enumerate(marks):
            term = load(slice(j * block, (j + 1) * block)).astype(jnp.float32) * mark
            total = term if total is None else total + term
        return total.astype(bf16)

    def arrived(view, recv):
        ctx_copy(view, view, s_proj, recv, pair).wait_recv()

    def sent(view, send):
        ctx_copy(view, view, send, r_pp, pair).wait_send()

    with scope("B_barrier"):
        pl.semaphore_wait(barrier, n - 1 + dn - 1)

    own_block = proj_r.at[side, row]
    for a in [partner] + mates:
        ctx_copy(proj, own_block, s_proj, proj_rs.at[row], 2 * a + side).start()

    with scope("A_loadg"):
        g_load.wait()
        for j in range(dn):
            g[j] = chosen_rows(lambda r: g_in[r, j * dc:(j + 1) * dc])
        g_r[side, md] = g[md]
    twin = md + 1 - 2 * lax.rem(md, 2)
    dp_far = [lax.rem(md + 2 * s, dn) for s in range(1, dn // 2)]
    dp_cross = [lax.rem(twin + 2 * s, dn) for s in range(1, dn // 2)]

    for peer in dp_far + dp_cross + [twin]:
        dp_copy(g.at[peer], g_r.at[side, md], s_g, g_rs.at[md], peer).start()
    ctx_copy(g.at[md], g_r.at[side, md], s_gp, r_gp, pair).start()
    with scope("A_loadqkv"):
        pltpu.make_async_copy(qkv_in, qkv_in, loc.at[2]).wait()
        for t in range(3):
            for h in range(n):
                qkv[h, t] = chosen_rows(lambda r: qkv_in[t, r, h * dh:(h + 1) * dh])
        qkv_r[me] = qkv[me]

    def send_qkv(peers):
        for peer in peers:
            ctx_copy(qkv.at[peer], qkv_r.at[me], s_qkv, r_qkv, peer).start()

    send_qkv([2 * a + side for a in [partner] + mate_partners])

    down = lax.broadcasted_iota(jnp.int32, (block, block), 0)
    for j in range(n):
        entry = picked[0, j]
        kpos[j * block:(j + 1) * block] = down + jnp.where(entry >= 0, entry * block, FAR)

    def proj_arrived(a):
        arrived(proj_r.at[side, a], proj_rs.at[a])

    with scope("C_waitg"):
        for peer in [twin] + dp_far + dp_cross:
            view = g_r.at[side, peer]
            arrived(view, g_rs.at[peer])
            ctx_copy(view, view, s_gp, r_gp, pair).start()
    with scope("D_waitpartner"):
        proj_arrived(partner)
        view = proj_r.at[side, partner]
        for a in mates:
            ctx_copy(view, view, s_pass, proj_rs.at[partner], 2 * a + side).start()
    send_qkv([2 * a + other for a in [partner] + mate_partners])
    send_qkv([2 * a + s for a in mates for s in (side, other)] + [pair])
    own_proj.wait()

    def part(a, b):
        k = 2 * a + b
        out = dot_nt(g_r[b].reshape(dn * block, dc), proj_r[side, a]).astype(bf16)
        agp_s[k] = out.reshape(dn, block, dh)
        for peer in dp_far + dp_cross + [twin]:
            dp_copy(agp_s.at[k, peer], agp_r.at[k, md], s_agp, agp_rs.at[k], peer).start()

    def finish(a, b):
        k = 2 * a + b
        arrived(agp_r.at[k, pl.ds(0, dn - 1)], agp_rs.at[k])
        total = agp_s[k, md].astype(jnp.float32)
        for peer in dp_peers:
            total = total + agp_r[k, peer].astype(jnp.float32)
        if a is row:
            ag_r[2 * row + b] = total.astype(bf16)
        else:
            ag_s[k] = total.astype(bf16)
            ctx_copy(ag_s.at[k], ag_r.at[2 * row + b], s_ag, ag_rs.at[row], 2 * a + side).start()

    def parts(names, b, waiting, lag):
        for a in names:
            with scope("G_part"):
                part(a, b)
            waiting.append((a, b))
            if len(waiting) > lag:
                with scope("H_finish"):
                    finish(*waiting.pop(0))

    waiting = []
    with scope("E_waitmate"):
        for a in mates:
            proj_arrived(a)
    parts([partner] + mates + [row], side, waiting, n)
    with scope("F_waitsecond"):
        for a in mate_partners:
            proj_arrived(a)
    parts(mate_partners, side, waiting, n)
    with scope("F_waitpairg"):
        arrived(g_r.at[other], r_gp)
    parts([partner] + mate_partners + mates + [row], other, waiting, rows)
    with scope("H_finish"):
        for a, b in waiting:
            finish(a, b)
    ctx_copy(proj_r.at[side], proj_r.at[side], s_pp, r_pp, pair).start()

    with scope("I_waitqkv"):
        arrived(qkv_r.at[pl.ds(0, n - 1)], r_qkv)
    k_t[...] = transposed(qkv_r[:, 1].reshape(slots, dh))
    v_t[...] = transposed(qkv_r[:, 2].reshape(slots, dh))

    def ordered(k):
        late = k // half
        return far_base * (1 - late) + own_base * late + lax.rem(row + k + late, half)

    def forward(k, carry):
        i = ordered(k)
        q = qkv_r[pl.ds(2 * i, 2), 0].reshape(width, dh)
        keys = qkv_r[:, 1].reshape(slots, dh)
        scores = dot_nt(keys, q)
        key_pos = kpos[...]
        key_pos = jnp.concatenate([key_pos, key_pos], axis=1)
        lane = lax.broadcasted_iota(jnp.int32, (1, width), 1)
        one, two = picked[0, 2 * i], picked[0, 2 * i + 1]
        one = jnp.where(one >= 0, one * block, -FAR)
        two = jnp.where(two >= 0, (two - 1) * block, -FAR)
        query_pos = lane + jnp.where(lane < block, one, two)
        scores = jnp.where(key_pos <= query_pos, scores * (scale * LOG2E), -1e30)
        e = jnp.exp2(scores - jnp.max(scores, axis=0, keepdims=True))
        p = (e * (1.0 / jnp.sum(e, axis=0, keepdims=True))).astype(bf16)
        p_s[i] = p
        a_t = dot_nn(v_t[...], p)
        attn_t[i] = a_t.astype(bf16)
        attn_s[i] = a_t.T.astype(bf16)

        @pl.when(k < half)
        def _():
            ctx_copy(attn_s.at[i], attn_r.at[row], s_attn, r_attn0, 2 * i + side).start()

        @pl.when((k >= half) & (k < rows - 1))
        def _():
            ctx_copy(attn_s.at[i], attn_r.at[row], s_attn, r_attn1, 2 * i + side).start()

        @pl.when(k == rows - 1)
        def _():
            pltpu.make_async_copy(attn_s.at[i], attn_r.at[i], loc.at[3]).start()

        return carry

    with scope("J_forward"):
        lax.fori_loop(0, rows, forward, 0)

    dk_acc[...] = jnp.zeros_like(dk_acc)
    dv_acc[...] = jnp.zeros_like(dv_acc)

    def backward(k, carry):
        i = ordered(k)
        with scope("K_waitag"):
            @pl.when(k < rows - 1)
            def _():
                arrived(ag_r.at[pl.ds(2 * i, 2)], ag_rs.at[i])

        q = qkv_r[pl.ds(2 * i, 2), 0].reshape(width, dh)
        v = qkv_r[:, 2].reshape(slots, dh)
        da = ag_r[pl.ds(2 * i, 2)].reshape(width, dh)
        delta = jnp.sum(da.astype(jnp.float32).T * attn_t[i].astype(jnp.float32), axis=0, keepdims=True)
        p = p_s[i]
        ds = (p.astype(jnp.float32) * (dot_nt(v, da) - delta)).astype(bf16)
        dq_t = dot_nn(k_t[...], ds) * scale
        dq_s[pl.ds(2 * i, 2)] = dq_t.T.astype(bf16).reshape(2, block, dh)
        for t in range(2):
            peer = 2 * i + t

            @pl.when(peer != me)
            def _():
                ctx_copy(dq_s.at[peer], dq_r.at[me], s_dq, r_dq, peer).start()

            @pl.when(peer == me)
            def _():
                pltpu.make_async_copy(dq_s.at[peer], dq_r.at[peer], loc.at[4]).start()

        dk_acc[...] += dot_nn(ds, q)
        dv_acc[...] += dot_nn(p, da)
        return carry

    with scope("L_backward"):
        lax.fori_loop(0, rows, backward, 0)

    dkv_s[:, 0] = (dk_acc[...] * scale).astype(bf16).reshape(n, block, dh)
    dkv_s[:, 1] = dv_acc[...].astype(bf16).reshape(n, block, dh)

    def send_dkv(peers):
        for peer in peers:
            ctx_copy(dkv_s.at[peer], dkv_r.at[me], s_dkv, r_dkv, peer).start()

    send_dkv([2 * a + side for a in [partner] + mate_partners + mates])
    own_dkv = pltpu.make_async_copy(dkv_s.at[me], dkv_r.at[me], loc.at[5])
    own_dkv.start()

    def spread(src, dst_of, send, recv, own_sem):
        for s, peer in enumerate(dp_far):
            dp_copy(src, dst_of(md), send, recv.at[1 + s], peer).start()
        dp_copy(src, dst_of(md), send, recv.at[0], twin).start()
        copy = pltpu.make_async_copy(src, dst_of(md), own_sem)
        copy.start()
        return copy

    def hand_over(dst_of, send, recv):
        for s in range(1, dn // 2):
            peer = lax.rem(md + dn - 2 * s, dn)
            arrived(dst_of(peer), recv.at[s])
            dp_copy(dst_of(peer), dst_of(peer), send, recv.at[0], twin).start()

    groups = [pl.ds(far_base, half), pl.ds(own_base, half)]
    with scope("M_waitattn"):
        arrived(attn_r.at[groups[0]], r_attn0)
    own_far = spread(attn_r.at[groups[0]], lambda d: attn_d.at[0, d, pl.ds(0, half)], s_ad, ad_rs.at[0], loc.at[6])
    with scope("M_waitattn"):
        if half > 1:
            arrived(attn_r.at[pl.ds(0, half - 1)], r_attn1)
        pltpu.make_async_copy(attn_s.at[row], attn_r.at[row], loc.at[3]).wait()
    own_near = spread(attn_r.at[groups[1]], lambda d: attn_d.at[1, d, pl.ds(0, half)], s_ad, ad_rs.at[1], loc.at[7])
    ctx_copy(attn_r.at[:, pl.ds(pl.multiple_of(other * block, block), block)], attn_y, s_ap, r_ap, pair).start()
    send_dkv([2 * a + other for a in [partner] + mate_partners + mates] + [pair])
    def weight(t, a):
        total = None
        for b in range(2):
            heads_of = attn_d[t, :, lax.rem(a, half), b * block:(b + 1) * block].reshape(dn * block, dh)
            term = dot_nn(transposed(heads_of), g_r[b].reshape(dn * block, dc))
            total = term if total is None else total + term
        return total

    def send_w(slot, value, dst, recv, peer_row):
        w_s[slot] = value.astype(bf16)
        ctx_copy(w_s.at[slot], dst, s_w, recv, 2 * peer_row + side).start()

    def spread_done(t, own):
        own.wait()
        arrived(attn_d.at[t, pl.ds(0, dn // 2)], ad_rs.at[t, 0])

    with scope("N_handover0"):
        hand_over(lambda d: attn_d.at[0, d, pl.ds(0, half)], s_ad, ad_rs.at[0])
    with scope("N_waitspread0"):
        spread_done(0, own_far)
    with scope("P_weight"):
        for k, a in enumerate(mate_partners):
            send_w(k, weight(0, a), w_x.at[row], r_wx, mates[k])
    with scope("N_waitpair"):
        arrived(attn_y, r_ap)
    own_ae = spread(attn_y, lambda d: attn_e.at[d], s_ae, ae_rs, loc.at[8])
    with scope("N_handover1"):
        hand_over(lambda d: attn_d.at[1, d, pl.ds(0, half)], s_ad, ad_rs.at[1])
    with scope("P_weight"):
        w_c[...] = weight(0, partner)
    with scope("N_waitspread1"):
        spread_done(1, own_near)
    with scope("P_weight"):
        for k, a in enumerate(mates):
            send_w(half - 1 + k, weight(1, a), w_m.at[row], r_wm, a)
        w_out[...] = weight(1, row)
    inner = lax.rem(row, half) == (half - 1) * (1 - row // half)

    def cross_sum():
        if mates:
            arrived(w_x.at[pl.ds(0, half - 1)], r_wx)
        total = w_c[...]
        for a in mates:
            total = total + w_x[a].astype(jnp.float32)
        send_w(rows - 2, total, w_p, r_wp, partner)

    with scope("S_waitinner"):
        pl.when(inner)(cross_sum)
    with scope("O_handover"):
        hand_over(lambda d: attn_e.at[d], s_ae, ae_rs)
    with scope("O_waitrows"):
        arrived(proj_r.at[other], r_pp)
        own_ae.wait()
        arrived(attn_e.at[pl.ds(0, dn // 2)], ae_rs.at[0])

    mine = pl.ds(pl.multiple_of(side * block, block), block)

    def mix_step(j, carry):
        def two(ref, *at):
            return ref[at].reshape(width, dh)

        d = pl.ds(2 * j, 2)
        t_of = [row // half if a // half else 1 - row // half for a in range(rows)]
        here = jnp.concatenate([two(attn_d, t_of[a], d, a % half, mine) for a in range(rows)], axis=1)
        there = jnp.concatenate([two(attn_e, d, a) for a in range(rows)], axis=1)
        out = dot_nn(here, proj_r[side].reshape(rows * dh, dc)) + dot_nn(there, proj_r[other].reshape(rows * dh, dc))
        mix_s[d] = out.astype(bf16).reshape(2, block, dc)
        return carry

    with scope("Q_mix"):
        lax.fori_loop(0, dn // 2, mix_step, 0)
    for peer in dp_peers:
        dp_copy(mix_s.at[peer], mix_r.at[md], s_mix, r_mix, peer).start()
    own_mix = pltpu.make_async_copy(mix_s.at[md], mix_r.at[md], loc.at[9])
    own_mix.start()

    with scope("S_waitcross"):
        pl.when(jnp.logical_not(inner))(cross_sum)

    with scope("T_waitdq"):
        pltpu.make_async_copy(dq_s.at[me], dq_r.at[me], loc.at[4]).wait()
        arrived(dq_r.at[pl.ds(0, n - 1)], r_dq)
    with scope("U_waitdkv"):
        own_dkv.wait()
        arrived(dkv_r.at[pl.ds(0, n - 1)], r_dkv)
    with scope("W_waitmates"):
        if mates:
            arrived(w_m.at[pl.ds(0, half - 1)], r_wm)
        for a in mates:
            w_out[...] += w_m[a].astype(jnp.float32)
    with scope("X_waitpartner"):
        arrived(w_p, r_wp)
        w_out[...] += w_p[...].astype(jnp.float32)
    with scope("V_waitmix"):
        own_mix.wait()
        arrived(mix_r.at[pl.ds(0, dn - 1)], r_mix)

    pltpu.make_async_copy(chosen, kept_out, loc.at[11]).wait()
    with scope("Y_waitsend"):
        blocks = pl.ds(0, n - 1)
        others = pl.ds(0, dn - 1)
        sent(qkv_r.at[pl.ds(0, n - 1)], s_qkv)
        sent(proj_r.at[0, pl.ds(0, half)], s_proj)
        if mates:
            sent(proj_r.at[0, pl.ds(0, half - 1)], s_pass)
        sent(proj_r.at[0], s_pp)
        sent(g.at[others], s_g)
        sent(agp_s.at[:, others], s_agp)
        sent(ag_s.at[pl.ds(0, n - 2)], s_ag)
        sent(g_r.at[0], s_gp)
        sent(attn_s.at[pl.ds(0, rows - 1)], s_attn)
        sent(dq_s.at[blocks], s_dq)
        sent(dkv_s.at[blocks], s_dkv)
        sent(attn_d.at[:, others], s_ad)
        sent(attn_y, s_ap)
        sent(attn_e.at[others], s_ae)
        sent(w_s.at[pl.ds(0, rows - 1)], s_w)
        sent(mix_s.at[others], s_mix)


def shards(queries, keys, values, out_grad, chosen, proj):
    n = lax.axis_size("ctx")
    dn = lax.axis_size("dp")
    tokens = queries.shape[1]
    hd = queries.shape[2]
    dh = hd // n
    dc = proj.shape[1]
    slots = n * BLOCK
    width = 2 * BLOCK
    rows = n // 2
    half = rows // 2
    bf16, f32 = jnp.bfloat16, jnp.float32
    sem = pltpu.SemaphoreType.DMA
    blocks = (n, BLOCK, dh)
    pairs = (rows, width, dh)
    sheets = (rows, dh, dc)
    buffers = [
        ((3, tokens, hd), bf16), ((tokens, dn * dc), bf16), ((n, 3, BLOCK, dh), bf16), ((dn, BLOCK, dc), bf16),
        ((slots, BLOCK), jnp.int32), ((n, 3, BLOCK, dh), bf16), ((2, dn, BLOCK, dc), bf16), ((2,) + sheets, bf16),
        ((n, dn, BLOCK, dh), bf16), ((n, dn, BLOCK, dh), bf16), (blocks, bf16), (blocks, bf16),
        (pairs, bf16), (pairs, bf16), ((rows, BLOCK, dh), bf16), ((2, dn, half, width, dh), bf16),
        ((dn, rows, BLOCK, dh), bf16), ((rows, dh, width), bf16),
        ((rows, slots, width), bf16), ((dh, slots), bf16), ((dh, slots), bf16),
        (blocks, bf16), ((n, 2, BLOCK, dh), bf16), ((slots, dh), f32), ((slots, dh), f32),
        ((dh, dc), f32), (sheets, bf16), (sheets, bf16), (sheets, bf16), ((dh, dc), bf16), ((dn, BLOCK, dc), bf16),
    ]
    held = sum(math.prod(shape) * jnp.dtype(kind).itemsize for shape, kind in buffers)
    sems = [sem((16,)), sem((12,)), sem((rows,)), sem((dn,)), sem((n,)), sem((rows,)), sem((2, dn // 2)), sem((dn // 2,)), sem((12,))]
    vmem = pl.BlockSpec(memory_space=pltpu.VMEM)
    picks = pltpu.SMEM(chosen.shape, chosen.dtype)
    free = pl.BlockSpec(memory_space=pl.ANY)
    hbm = pl.BlockSpec(memory_space=pltpu.HBM)

    def kept(x):
        return pltpu.with_memory_space_constraint(x, pltpu.HBM)

    chosen = kept(chosen)
    dq, dkv, weight_grad, mixed, placed = pl.pallas_call(
        functools.partial(kernel, n, dn, 1.0 / math.sqrt(dh)),
        out_shape=(
            jax.ShapeDtypeStruct(blocks, bf16),
            jax.ShapeDtypeStruct((n, 2, BLOCK, dh), bf16),
            jax.ShapeDtypeStruct((dh, dc), f32),
            jax.ShapeDtypeStruct((dn, BLOCK, dc), bf16),
            jax.ShapeDtypeStruct(chosen.shape, chosen.dtype),
        ),
        in_specs=[hbm] * 6,
        out_specs=[free, free, vmem, free, free],
        scratch_shapes=[picks] + [pltpu.VMEM(shape, kind) for shape, kind in buffers] + sems,
        compiler_params=pltpu.CompilerParams(
            collective_id=0, has_side_effects=True, vmem_limit_bytes=min(held + SPARE, 60 * MIB)),
    )(chosen, *[kept(x) for x in (queries[0], keys[0], values[0], out_grad[0], proj)])

    wide = (tokens, dn * dc)
    thin = (tokens, hd)
    count = tokens // BLOCK
    out, q_grad, k_grad, v_grad, proj_grad = pl.pallas_call(
        functools.partial(place_kernel, n, dn, count),
        out_shape=(
            jax.ShapeDtypeStruct(wide, bf16), jax.ShapeDtypeStruct(thin, bf16), jax.ShapeDtypeStruct(thin, bf16),
            jax.ShapeDtypeStruct(thin, bf16), jax.ShapeDtypeStruct((dh, dc), f32)),
        in_specs=[free] * 5,
        out_specs=[hbm] * 5,
        scratch_shapes=[picks, pltpu.VMEM((BLOCK, max(dn * dc, hd)), bf16), sem((count, 4)), sem((2,))],
        compiler_params=pltpu.CompilerParams(vmem_limit_bytes=8 * MIB),
    )(placed, mixed, dq, dkv, weight_grad)
    return out[None], q_grad[None], k_grad[None], v_grad[None], proj_grad


def solution(mesh):
    rows = P("dp", "ctx", None)
    return jax.shard_map(
        shards,
        mesh=mesh,
        in_specs=(rows, rows, rows, rows, P("dp", None), P("ctx", "dp")),
        out_specs=(rows, rows, rows, rows, P("ctx", "dp")),
        check_vma=False,
    )
```

```python
import functools
import math

import jax
import jax.numpy as jnp
from jax import lax
from jax.experimental import pallas as pl
from jax.experimental.pallas import tpu as pltpu
from jax.sharding import PartitionSpec as P

BLOCK = 128
FAR = 1 << 30
MIB = 1024 * 1024
LOG2E = math.log2(math.e)
SPARE = 8 * MIB

scope = jax.named_scope


def dot_nt(a, b):
    return lax.dot_general(a, b, (((1,), (1,)), ((), ())), preferred_element_type=jnp.float32)


def dot_nn(a, b):
    return lax.dot_general(a, b, (((1,), (0,)), ((), ())), preferred_element_type=jnp.float32)


def transposed(a):
    return a.astype(jnp.float32).T.astype(a.dtype)


def local_block(entry, me, count):
    spans = count // 2
    index = jnp.maximum(entry, 0)
    return jnp.where(index // spans == me, index % spans, spans + index % spans)


def block_marks(picked, me, count):
    entry = picked[0, me]
    local = jnp.where(entry >= 0, local_block(entry, me, count), -1)
    return [jnp.where(local == j, 1.0, 0.0) for j in range(count)]


def place_kernel(count, chosen, mix, dq, dkv, w, out, q_out, k_out, v_out, w_out, zero, sems, w_sem):
    block = dq.shape[0]
    w_copy = pltpu.make_async_copy(w, w_out, w_sem.at[0])
    w_copy.start()
    zero[...] = jnp.zeros_like(zero)
    me = lax.axis_index("ctx")
    with scope("a_pick"):
        lane = lax.broadcasted_iota(jnp.int32, chosen.shape, 1)
        entry = jnp.max(jnp.where(lane == me, chosen[...], -1))
        local = jnp.where(entry >= 0, local_block(entry, me, count), -1)
    outs = ((mix, out), (dq, q_out), (dkv.at[0], k_out), (dkv.at[1], v_out))
    with scope("b_issue"):
        for j in range(count):
            for t, (src, dst) in enumerate(outs):
                rows = dst.at[pl.ds(j * block, block)]

                @pl.when(local == j)
                def _():
                    pltpu.make_async_copy(src, rows, sems.at[j, t]).start()

                @pl.when(local != j)
                def _():
                    pltpu.make_async_copy(zero.at[:, pl.ds(0, dst.shape[1])], rows, sems.at[j, t]).start()

    with scope("c_wait"):
        for j in range(count):
            for t, (_, dst) in enumerate(outs):
                view = dst.at[pl.ds(j * block, block)]
                pltpu.make_async_copy(view, view, sems.at[j, t]).wait()
        w_copy.wait()


def kernel(
    n, dn, scale,
    chosen, q_hbm, k_hbm, v_hbm, g_hbm, proj,
    dq_r, dkv_r, w_out, mix_r, kept_out,
    picked, qkv_in, g_in, qkv, g, kpos, qkv_r, g_r, proj_r, agp_s, agp_r, ag_s, ag_r,
    attn_s, attn_r, attn_y, attn_d, attn_e, attn_t,
    p_s, k_t, v_t, dq_s, dkv_s, dk_acc, dv_acc, w_c, w_s, w_x, w_m, w_p, mix_s,
    ss, rs, proj_rs, g_rs, agp_rs, ag_rs, ad_rs, ae_rs, loc,
):
    me = lax.axis_index("ctx")
    md = lax.axis_index("dp")
    bf16 = jnp.bfloat16
    block, dh = qkv.shape[2], qkv.shape[3]
    dc = proj.shape[1]
    slots = n * block
    width = 2 * block
    rows = n // 2
    half = rows // 2
    s_proj, s_g, s_qkv, s_agp, s_ag, s_gp, s_attn, s_dq, s_dkv, s_ad, s_ap, s_ae, s_w, s_mix, s_pass, s_pp = (
        ss.at[k] for k in range(16))
    r_pp, r_qkv, r_gp, r_attn0, r_attn1, r_dq, r_dkv, r_ap, r_wx, r_wm, r_wp, r_mix = (rs.at[k] for k in range(12))

    def ctx_copy(src, dst, send, recv, peer):
        return pltpu.make_async_remote_copy(
            src_ref=src, dst_ref=dst, send_sem=send, recv_sem=recv,
            device_id={"ctx": peer}, device_id_type=pl.DeviceIdType.MESH)

    def dp_copy(src, dst, send, recv, peer):
        return pltpu.make_async_remote_copy(
            src_ref=src, dst_ref=dst, send_sem=send, recv_sem=recv,
            device_id={"dp": peer}, device_id_type=pl.DeviceIdType.MESH)

    ctx_peers = [lax.rem(me + s, n) for s in range(1, n)]
    dp_peers = [lax.rem(md + s, dn) for s in range(1, dn)]

    barrier = pltpu.get_barrier_semaphore()
    for peer in ctx_peers:
        pl.semaphore_signal(barrier, inc=1, device_id={"ctx": peer}, device_id_type=pl.DeviceIdType.MESH)
    for peer in dp_peers:
        pl.semaphore_signal(barrier, inc=1, device_id={"dp": peer}, device_id_type=pl.DeviceIdType.MESH)

    row = me // 2
    side = lax.rem(me, 2)
    other = 1 - side
    pair = me + 1 - 2 * side
    own_base = (row // half) * half
    far_base = half - own_base

    def near(s):
        return own_base + lax.rem(row + s, half)

    def across(s):
        return far_base + lax.rem(row + s, half)

    mates = [near(s) for s in range(1, half)]
    partner = across(0)
    mate_partners = [across(s) for s in range(1, half)]

    pick = pltpu.make_async_copy(chosen, picked, loc.at[10])
    pick.start()
    own_proj = pltpu.make_async_copy(proj, proj_r.at[side, row], loc.at[0])
    g_load = pltpu.make_async_copy(g_hbm, g_in, loc.at[1])
    g_load.start()
    for t, src in enumerate((q_hbm, k_hbm, v_hbm)):
        pltpu.make_async_copy(src, qkv_in.at[t], loc.at[2]).start()
    own_proj.start()
    pltpu.make_async_copy(chosen, kept_out, loc.at[11]).start()

    def chosen_rows(load):
        total = None
        for j, mark in enumerate(marks):
            term = load(slice(j * block, (j + 1) * block)).astype(jnp.float32) * mark
            total = term if total is None else total + term
        return total.astype(bf16)

    def arrived(view, recv):
        ctx_copy(view, view, s_proj, recv, pair).wait_recv()

    def sent(view, send):
        ctx_copy(view, view, send, r_pp, pair).wait_send()

    with scope("B_barrier"):
        pl.semaphore_wait(barrier, n - 1 + dn - 1)

    own_block = proj_r.at[side, row]
    for a in [partner] + mates:
        ctx_copy(proj, own_block, s_proj, proj_rs.at[row], 2 * a + side).start()

    with scope("A_loadg"):
        pick.wait()
        marks = block_marks(picked, me, qkv_in.shape[1] // block)
        g_load.wait()
        for j in range(dn):
            g[j] = chosen_rows(lambda r: g_in[r, j * dc:(j + 1) * dc])
        g_r[side, md] = g[md]
    twin = md + 1 - 2 * lax.rem(md, 2)
    dp_far = [lax.rem(md + 2 * s, dn) for s in range(1, dn // 2)]
    dp_cross = [lax.rem(twin + 2 * s, dn) for s in range(1, dn // 2)]

    for peer in dp_far + dp_cross + [twin]:
        dp_copy(g.at[peer], g_r.at[side, md], s_g, g_rs.at[md], peer).start()
    ctx_copy(g.at[md], g_r.at[side, md], s_gp, r_gp, pair).start()
    with scope("A_loadqkv"):
        pltpu.make_async_copy(qkv_in, qkv_in, loc.at[2]).wait()
        for t in range(3):
            for h in range(n):
                qkv[h, t] = chosen_rows(lambda r: qkv_in[t, r, h * dh:(h + 1) * dh])
        qkv_r[me] = qkv[me]

    def send_qkv(peers):
        for peer in peers:
            ctx_copy(qkv.at[peer], qkv_r.at[me], s_qkv, r_qkv, peer).start()

    send_qkv([2 * a + side for a in [partner] + mate_partners])

    down = lax.broadcasted_iota(jnp.int32, (block, block), 0)
    for j in range(n):
        entry = picked[0, j]
        kpos[j * block:(j + 1) * block] = down + jnp.where(entry >= 0, entry * block, FAR)

    def proj_arrived(a):
        arrived(proj_r.at[side, a], proj_rs.at[a])

    with scope("C_waitg"):
        for peer in [twin] + dp_far + dp_cross:
            view = g_r.at[side, peer]
            arrived(view, g_rs.at[peer])
            ctx_copy(view, view, s_gp, r_gp, pair).start()
    with scope("D_waitpartner"):
        proj_arrived(partner)
        view = proj_r.at[side, partner]
        for a in mates:
            ctx_copy(view, view, s_pass, proj_rs.at[partner], 2 * a + side).start()
    send_qkv([2 * a + other for a in [partner] + mate_partners])
    send_qkv([2 * a + s for a in mates for s in (side, other)] + [pair])
    own_proj.wait()

    def part(a, b):
        k = 2 * a + b
        out = dot_nt(g_r[b].reshape(dn * block, dc), proj_r[side, a]).astype(bf16)
        agp_s[k] = out.reshape(dn, block, dh)
        for peer in dp_far + dp_cross + [twin]:
            dp_copy(agp_s.at[k, peer], agp_r.at[k, md], s_agp, agp_rs.at[k], peer).start()

    def finish(a, b):
        k = 2 * a + b
        arrived(agp_r.at[k, pl.ds(0, dn - 1)], agp_rs.at[k])
        total = agp_s[k, md].astype(jnp.float32)
        for peer in dp_peers:
            total = total + agp_r[k, peer].astype(jnp.float32)
        if a is row:
            ag_r[2 * row + b] = total.astype(bf16)
        else:
            ag_s[k] = total.astype(bf16)
            ctx_copy(ag_s.at[k], ag_r.at[2 * row + b], s_ag, ag_rs.at[row], 2 * a + side).start()

    def parts(names, b, waiting, lag):
        for a in names:
            with scope("G_part"):
                part(a, b)
            waiting.append((a, b))
            if len(waiting) > lag:
                with scope("H_finish"):
                    finish(*waiting.pop(0))

    waiting = []
    with scope("E_waitmate"):
        for a in mates:
            proj_arrived(a)
    parts([partner] + mates + [row], side, waiting, n)
    with scope("F_waitpairg"):
        arrived(g_r.at[other], r_gp)
    parts([partner] + mates + [row], other, waiting, n)
    with scope("F_waitsecond"):
        for a in mate_partners:
            proj_arrived(a)
    for b in (side, other):
        parts(mate_partners, b, waiting, rows)
    with scope("H_finish"):
        for a, b in waiting:
            finish(a, b)
    ctx_copy(proj_r.at[side], proj_r.at[side], s_pp, r_pp, pair).start()

    with scope("I_waitqkv"):
        arrived(qkv_r.at[pl.ds(0, n - 1)], r_qkv)
    k_t[...] = transposed(qkv_r[:, 1].reshape(slots, dh))
    v_t[...] = transposed(qkv_r[:, 2].reshape(slots, dh))

    def ordered(k):
        late = k // half
        return far_base * (1 - late) + own_base * late + lax.rem(row + k + late, half)

    def forward(k, carry):
        i = ordered(k)
        q = qkv_r[pl.ds(2 * i, 2), 0].reshape(width, dh)
        keys = qkv_r[:, 1].reshape(slots, dh)
        scores = dot_nt(keys, q)
        key_pos = kpos[...]
        key_pos = jnp.concatenate([key_pos, key_pos], axis=1)
        lane = lax.broadcasted_iota(jnp.int32, (1, width), 1)
        one, two = picked[0, 2 * i], picked[0, 2 * i + 1]
        one = jnp.where(one >= 0, one * block, -FAR)
        two = jnp.where(two >= 0, (two - 1) * block, -FAR)
        query_pos = lane + jnp.where(lane < block, one, two)
        scores = jnp.where(key_pos <= query_pos, scores * (scale * LOG2E), -1e30)
        e = jnp.exp2(scores - jnp.max(scores, axis=0, keepdims=True))
        p = (e * (1.0 / jnp.sum(e, axis=0, keepdims=True))).astype(bf16)
        p_s[i] = p
        a_t = dot_nn(v_t[...], p)
        attn_t[i] = a_t.astype(bf16)
        attn_s[i] = a_t.T.astype(bf16)

        @pl.when(k < half)
        def _():
            ctx_copy(attn_s.at[i], attn_r.at[row], s_attn, r_attn0, 2 * i + side).start()

        @pl.when((k >= half) & (k < rows - 1))
        def _():
            ctx_copy(attn_s.at[i], attn_r.at[row], s_attn, r_attn1, 2 * i + side).start()

        @pl.when(k == rows - 1)
        def _():
            pltpu.make_async_copy(attn_s.at[i], attn_r.at[i], loc.at[3]).start()

        return carry

    with scope("J_forward"):
        lax.fori_loop(0, rows, forward, 0)

    dk_acc[...] = jnp.zeros_like(dk_acc)
    dv_acc[...] = jnp.zeros_like(dv_acc)

    def heads_of_me(ref):
        return ref.at[:, pl.ds(pl.multiple_of(me * dh, dh), dh)]

    def backward(k, carry):
        i = ordered(k)
        with scope("K_waitag"):
            @pl.when(k < rows - 1)
            def _():
                arrived(ag_r.at[pl.ds(2 * i, 2)], ag_rs.at[i])

        q = qkv_r[pl.ds(2 * i, 2), 0].reshape(width, dh)
        v = qkv_r[:, 2].reshape(slots, dh)
        da = ag_r[pl.ds(2 * i, 2)].reshape(width, dh)
        delta = jnp.sum(da.astype(jnp.float32).T * attn_t[i].astype(jnp.float32), axis=0, keepdims=True)
        p = p_s[i]
        ds = (p.astype(jnp.float32) * (dot_nt(v, da) - delta)).astype(bf16)
        dq_t = dot_nn(k_t[...], ds) * scale
        dq_s[pl.ds(2 * i, 2)] = dq_t.T.astype(bf16).reshape(2, block, dh)
        for t in range(2):
            peer = 2 * i + t

            @pl.when(peer != me)
            def _():
                ctx_copy(dq_s.at[peer], heads_of_me(dq_r), s_dq, r_dq, peer).start()

            @pl.when(peer == me)
            def _():
                pltpu.make_async_copy(dq_s.at[peer], heads_of_me(dq_r), loc.at[4]).start()

        dk_acc[...] += dot_nn(ds, q)
        dv_acc[...] += dot_nn(p, da)
        return carry

    with scope("L_backward"):
        lax.fori_loop(0, rows, backward, 0)

    dkv_s[:, 0] = (dk_acc[...] * scale).astype(bf16).reshape(n, block, dh)
    dkv_s[:, 1] = dv_acc[...].astype(bf16).reshape(n, block, dh)

    my_dkv = dkv_r.at[:, :, pl.ds(pl.multiple_of(me * dh, dh), dh)]

    def send_dkv(peers):
        for peer in peers:
            ctx_copy(dkv_s.at[peer], my_dkv, s_dkv, r_dkv, peer).start()

    send_dkv([2 * a + side for a in [partner] + mate_partners + mates])
    own_dkv = pltpu.make_async_copy(dkv_s.at[me], my_dkv, loc.at[5])
    own_dkv.start()

    def spread(src, dst_of, send, recv, own_sem):
        for s, peer in enumerate(dp_far):
            dp_copy(src, dst_of(md), send, recv.at[1 + s], peer).start()
        dp_copy(src, dst_of(md), send, recv.at[0], twin).start()
        copy = pltpu.make_async_copy(src, dst_of(md), own_sem)
        copy.start()
        return copy

    def hand_over(dst_of, send, recv):
        for s in range(1, dn // 2):
            peer = lax.rem(md + dn - 2 * s, dn)
            arrived(dst_of(peer), recv.at[s])
            dp_copy(dst_of(peer), dst_of(peer), send, recv.at[0], twin).start()

    groups = [pl.ds(far_base, half), pl.ds(own_base, half)]
    with scope("M_waitattn"):
        arrived(attn_r.at[groups[0]], r_attn0)
    own_far = spread(attn_r.at[groups[0]], lambda d: attn_d.at[0, d, pl.ds(0, half)], s_ad, ad_rs.at[0], loc.at[6])
    with scope("M_waitattn"):
        if half > 1:
            arrived(attn_r.at[pl.ds(0, half - 1)], r_attn1)
        pltpu.make_async_copy(attn_s.at[row], attn_r.at[row], loc.at[3]).wait()
    own_near = spread(attn_r.at[groups[1]], lambda d: attn_d.at[1, d, pl.ds(0, half)], s_ad, ad_rs.at[1], loc.at[7])
    ctx_copy(attn_r.at[:, pl.ds(pl.multiple_of(other * block, block), block)], attn_y, s_ap, r_ap, pair).start()
    send_dkv([2 * a + other for a in [partner] + mate_partners + mates] + [pair])
    def weight(t, a):
        total = None
        for b in range(2):
            heads_of = attn_d[t, :, lax.rem(a, half), b * block:(b + 1) * block].reshape(dn * block, dh)
            term = dot_nn(transposed(heads_of), g_r[b].reshape(dn * block, dc))
            total = term if total is None else total + term
        return total

    def send_w(slot, value, dst, recv, peer_row):
        w_s[slot] = value.astype(bf16)
        ctx_copy(w_s.at[slot], dst, s_w, recv, 2 * peer_row + side).start()

    def spread_done(t, own):
        own.wait()
        arrived(attn_d.at[t, pl.ds(0, dn // 2)], ad_rs.at[t, 0])

    with scope("N_handover0"):
        hand_over(lambda d: attn_d.at[0, d, pl.ds(0, half)], s_ad, ad_rs.at[0])
    with scope("N_waitspread0"):
        spread_done(0, own_far)
    with scope("P_weight"):
        for k, a in enumerate(mate_partners):
            send_w(k, weight(0, a), w_x.at[row], r_wx, mates[k])
    with scope("N_waitpair"):
        arrived(attn_y, r_ap)
    own_ae = spread(attn_y, lambda d: attn_e.at[d], s_ae, ae_rs, loc.at[8])
    with scope("N_handover1"):
        hand_over(lambda d: attn_d.at[1, d, pl.ds(0, half)], s_ad, ad_rs.at[1])
    with scope("P_weight"):
        w_c[...] = weight(0, partner)
    with scope("N_waitspread1"):
        spread_done(1, own_near)
    with scope("P_weight"):
        for k, a in enumerate(mates):
            send_w(half - 1 + k, weight(1, a), w_m.at[row], r_wm, a)
        w_out[...] = weight(1, row)
    inner = lax.rem(row, half) == (half - 1) * (1 - row // half)

    def cross_sum():
        if mates:
            arrived(w_x.at[pl.ds(0, half - 1)], r_wx)
        total = w_c[...]
        for a in mates:
            total = total + w_x[a].astype(jnp.float32)
        send_w(rows - 2, total, w_p, r_wp, partner)

    with scope("S_waitinner"):
        pl.when(inner)(cross_sum)
    with scope("O_handover"):
        hand_over(lambda d: attn_e.at[d], s_ae, ae_rs)
    with scope("O_waitrows"):
        arrived(proj_r.at[other], r_pp)
        own_ae.wait()
        arrived(attn_e.at[pl.ds(0, dn // 2)], ae_rs.at[0])

    mine = pl.ds(pl.multiple_of(side * block, block), block)

    def mix_step(j, carry):
        def two(ref, *at):
            return ref[at].reshape(width, dh)

        d = pl.ds(2 * j, 2)
        t_of = [row // half if a // half else 1 - row // half for a in range(rows)]
        here = jnp.concatenate([two(attn_d, t_of[a], d, a % half, mine) for a in range(rows)], axis=1)
        there = jnp.concatenate([two(attn_e, d, a) for a in range(rows)], axis=1)
        out = dot_nn(here, proj_r[side].reshape(rows * dh, dc)) + dot_nn(there, proj_r[other].reshape(rows * dh, dc))
        mix_s[d] = out.astype(bf16).reshape(2, block, dc)
        return carry

    my_columns = mix_r.at[:, pl.ds(pl.multiple_of(md * dc, dc), dc)]
    with scope("Q_mix"):
        lax.fori_loop(0, dn // 2, mix_step, 0)
    for peer in dp_peers:
        dp_copy(mix_s.at[peer], my_columns, s_mix, r_mix, peer).start()
    own_mix = pltpu.make_async_copy(mix_s.at[md], my_columns, loc.at[9])
    own_mix.start()

    with scope("S_waitcross"):
        pl.when(jnp.logical_not(inner))(cross_sum)

    with scope("T_waitdq"):
        pltpu.make_async_copy(dq_s.at[me], heads_of_me(dq_r), loc.at[4]).wait()
        arrived(dq_r.at[:, pl.ds(0, (n - 1) * dh)], r_dq)
    with scope("U_waitdkv"):
        own_dkv.wait()
        arrived(dkv_r.at[:, :, pl.ds(0, (n - 1) * dh)], r_dkv)
    with scope("W_waitmates"):
        if mates:
            arrived(w_m.at[pl.ds(0, half - 1)], r_wm)
        for a in mates:
            w_out[...] += w_m[a].astype(jnp.float32)
    with scope("X_waitpartner"):
        arrived(w_p, r_wp)
        w_out[...] += w_p[...].astype(jnp.float32)
    with scope("V_waitmix"):
        own_mix.wait()
        arrived(mix_r.at[:, pl.ds(0, (dn - 1) * dc)], r_mix)

    pltpu.make_async_copy(chosen, kept_out, loc.at[11]).wait()
    with scope("Y_waitsend"):
        blocks = pl.ds(0, n - 1)
        others = pl.ds(0, dn - 1)
        sent(qkv_r.at[pl.ds(0, n - 1)], s_qkv)
        sent(proj_r.at[0, pl.ds(0, half)], s_proj)
        if mates:
            sent(proj_r.at[0, pl.ds(0, half - 1)], s_pass)
        sent(proj_r.at[0], s_pp)
        sent(g.at[others], s_g)
        sent(agp_s.at[:, others], s_agp)
        sent(ag_s.at[pl.ds(0, n - 2)], s_ag)
        sent(g_r.at[0], s_gp)
        sent(attn_s.at[pl.ds(0, rows - 1)], s_attn)
        sent(dq_s.at[blocks], s_dq)
        sent(dkv_s.at[blocks], s_dkv)
        sent(attn_d.at[:, others], s_ad)
        sent(attn_y, s_ap)
        sent(attn_e.at[others], s_ae)
        sent(w_s.at[pl.ds(0, rows - 1)], s_w)
        sent(mix_s.at[others], s_mix)


def shards(queries, keys, values, out_grad, chosen, proj):
    n = lax.axis_size("ctx")
    dn = lax.axis_size("dp")
    tokens = queries.shape[1]
    hd = queries.shape[2]
    dh = hd // n
    dc = proj.shape[1]
    slots = n * BLOCK
    width = 2 * BLOCK
    rows = n // 2
    half = rows // 2
    bf16, f32 = jnp.bfloat16, jnp.float32
    sem = pltpu.SemaphoreType.DMA
    blocks = (n, BLOCK, dh)
    pairs = (rows, width, dh)
    sheets = (rows, dh, dc)
    buffers = [
        ((3, tokens, hd), bf16), ((tokens, dn * dc), bf16), ((n, 3, BLOCK, dh), bf16), ((dn, BLOCK, dc), bf16),
        ((slots, BLOCK), jnp.int32), ((n, 3, BLOCK, dh), bf16), ((2, dn, BLOCK, dc), bf16), ((2,) + sheets, bf16),
        ((n, dn, BLOCK, dh), bf16), ((n, dn, BLOCK, dh), bf16), (blocks, bf16), (blocks, bf16),
        (pairs, bf16), (pairs, bf16), ((rows, BLOCK, dh), bf16), ((2, dn, half, width, dh), bf16),
        ((dn, rows, BLOCK, dh), bf16), ((rows, dh, width), bf16),
        ((rows, slots, width), bf16), ((dh, slots), bf16), ((dh, slots), bf16),
        (blocks, bf16), ((n, 2, BLOCK, dh), bf16), ((slots, dh), f32), ((slots, dh), f32),
        ((dh, dc), f32), (sheets, bf16), (sheets, bf16), (sheets, bf16), ((dh, dc), bf16), ((dn, BLOCK, dc), bf16),
    ]
    held = sum(math.prod(shape) * jnp.dtype(kind).itemsize for shape, kind in buffers)
    sems = [sem((16,)), sem((12,)), sem((rows,)), sem((dn,)), sem((n,)), sem((rows,)), sem((2, dn // 2)), sem((dn // 2,)), sem((12,))]
    vmem = pl.BlockSpec(memory_space=pltpu.VMEM)
    picks = pltpu.SMEM(chosen.shape, chosen.dtype)
    free = pl.BlockSpec(memory_space=pl.ANY)
    hbm = pl.BlockSpec(memory_space=pltpu.HBM)

    def kept(x):
        return pltpu.with_memory_space_constraint(x, pltpu.HBM)

    chosen = kept(chosen)
    dq, dkv, weight_grad, mixed, placed = pl.pallas_call(
        functools.partial(kernel, n, dn, 1.0 / math.sqrt(dh)),
        out_shape=(
            jax.ShapeDtypeStruct((BLOCK, hd), bf16),
            jax.ShapeDtypeStruct((2, BLOCK, hd), bf16),
            jax.ShapeDtypeStruct((dh, dc), f32),
            jax.ShapeDtypeStruct((BLOCK, dn * dc), bf16),
            jax.ShapeDtypeStruct(chosen.shape, chosen.dtype),
        ),
        in_specs=[hbm] * 6,
        out_specs=[free, free, vmem, free, free],
        scratch_shapes=[picks] + [pltpu.VMEM(shape, kind) for shape, kind in buffers] + sems,
        compiler_params=pltpu.CompilerParams(
            collective_id=0, has_side_effects=True, vmem_limit_bytes=min(held + SPARE, 60 * MIB)),
    )(chosen, *[kept(x) for x in (queries[0], keys[0], values[0], out_grad[0], proj)])

    wide = (tokens, dn * dc)
    thin = (tokens, hd)
    count = tokens // BLOCK
    out, q_grad, k_grad, v_grad, proj_grad = pl.pallas_call(
        functools.partial(place_kernel, count),
        out_shape=(
            jax.ShapeDtypeStruct(wide, bf16), jax.ShapeDtypeStruct(thin, bf16), jax.ShapeDtypeStruct(thin, bf16),
            jax.ShapeDtypeStruct(thin, bf16), jax.ShapeDtypeStruct((dh, dc), f32)),
        in_specs=[vmem] + [free] * 4,
        out_specs=[hbm] * 5,
        scratch_shapes=[pltpu.VMEM((BLOCK, max(dn * dc, hd)), bf16), sem((count, 4)), sem((1,))],
        compiler_params=pltpu.CompilerParams(vmem_limit_bytes=8 * MIB),
    )(placed, mixed, dq, dkv, weight_grad)
    return out[None], q_grad[None], k_grad[None], v_grad[None], proj_grad


def solution(mesh):
    rows = P("dp", "ctx", None)
    return jax.shard_map(
        shards,
        mesh=mesh,
        in_specs=(rows, rows, rows, rows, P("dp", None), P("ctx", "dp")),
        out_specs=(rows, rows, rows, rows, P("ctx", "dp")),
        check_vma=False,
    )
```

```python
import functools
import math

import jax
import jax.numpy as jnp
from jax import lax
from jax.experimental import pallas as pl
from jax.experimental.pallas import tpu as pltpu
from jax.sharding import PartitionSpec as P

BLOCK = 128
FAR = 1 << 30
MIB = 1024 * 1024
LOG2E = math.log2(math.e)
SPARE = 8 * MIB

scope = jax.named_scope


def dot_nt(a, b):
    return lax.dot_general(a, b, (((1,), (1,)), ((), ())), preferred_element_type=jnp.float32)


def dot_nn(a, b):
    return lax.dot_general(a, b, (((1,), (0,)), ((), ())), preferred_element_type=jnp.float32)


def transposed(a):
    return a.astype(jnp.float32).T.astype(a.dtype)


def local_block(entry, me, count):
    spans = count // 2
    index = jnp.maximum(entry, 0)
    return jnp.where(index // spans == me, index % spans, spans + index % spans)


def block_marks(picked, me, count):
    entry = picked[0, me]
    local = jnp.where(entry >= 0, local_block(entry, me, count), -1)
    return [jnp.where(local == j, 1.0, 0.0) for j in range(count)]


def place_kernel(count, chosen, mix, dq, dkv, w, out, q_out, k_out, v_out, w_out, zero, sems, w_sem):
    block = dq.shape[0]
    w_copy = pltpu.make_async_copy(w, w_out, w_sem.at[0])
    w_copy.start()
    zero[...] = jnp.zeros_like(zero)
    me = lax.axis_index("ctx")
    with scope("a_pick"):
        lane = lax.broadcasted_iota(jnp.int32, chosen.shape, 1)
        entry = jnp.max(jnp.where(lane == me, chosen[...], -1))
        local = jnp.where(entry >= 0, local_block(entry, me, count), -1)
    outs = ((mix, out), (dq, q_out), (dkv.at[0], k_out), (dkv.at[1], v_out))
    with scope("b_issue"):
        for j in range(count):
            for t, (src, dst) in enumerate(outs):
                rows = dst.at[pl.ds(j * block, block)]

                @pl.when(local == j)
                def _():
                    pltpu.make_async_copy(src, rows, sems.at[j, t]).start()

                @pl.when(local != j)
                def _():
                    pltpu.make_async_copy(zero.at[:, pl.ds(0, dst.shape[1])], rows, sems.at[j, t]).start()

    with scope("c_wait"):
        for j in range(count):
            for t, (_, dst) in enumerate(outs):
                view = dst.at[pl.ds(j * block, block)]
                pltpu.make_async_copy(view, view, sems.at[j, t]).wait()
        w_copy.wait()


def kernel(
    n, dn, scale,
    chosen, q_hbm, k_hbm, v_hbm, g_hbm, proj,
    dq_r, dkv_r, w_out, mix_r, kept_out,
    picked, qkv_in, g_in, qkv, g, kpos, qkv_r, g_r, proj_r, agp_s, agp_r, ag_s, ag_r,
    attn_s, attn_r, attn_y, attn_d, attn_e, attn_t,
    p_s, k_t, v_t, dq_s, dkv_s, dk_acc, dv_acc, w_c, w_s, w_x, w_m, w_p, mix_s,
    ss, rs, proj_rs, g_rs, agp_rs, ag_rs, ad_rs, ae_rs, loc,
):
    me = lax.axis_index("ctx")
    md = lax.axis_index("dp")
    bf16 = jnp.bfloat16
    block, dh = qkv.shape[2], qkv.shape[3]
    dc = proj.shape[1]
    slots = n * block
    width = 2 * block
    rows = n // 2
    half = rows // 2
    s_proj, s_g, s_qkv, s_agp, s_ag, s_gp, s_attn, s_dq, s_dkv, s_ad, s_ap, s_ae, s_w, s_mix, s_pass, s_pp = (
        ss.at[k] for k in range(16))
    r_pp, r_qkv, r_gp, r_attn0, r_attn1, r_dq, r_dkv, r_ap, r_wx, r_wm, r_wp, r_mix = (rs.at[k] for k in range(12))

    def ctx_copy(src, dst, send, recv, peer):
        return pltpu.make_async_remote_copy(
            src_ref=src, dst_ref=dst, send_sem=send, recv_sem=recv,
            device_id={"ctx": peer}, device_id_type=pl.DeviceIdType.MESH)

    def dp_copy(src, dst, send, recv, peer):
        return pltpu.make_async_remote_copy(
            src_ref=src, dst_ref=dst, send_sem=send, recv_sem=recv,
            device_id={"dp": peer}, device_id_type=pl.DeviceIdType.MESH)

    ctx_peers = [lax.rem(me + s, n) for s in range(1, n)]
    dp_peers = [lax.rem(md + s, dn) for s in range(1, dn)]

    barrier = pltpu.get_barrier_semaphore()
    for peer in ctx_peers:
        pl.semaphore_signal(barrier, inc=1, device_id={"ctx": peer}, device_id_type=pl.DeviceIdType.MESH)
    for peer in dp_peers:
        pl.semaphore_signal(barrier, inc=1, device_id={"dp": peer}, device_id_type=pl.DeviceIdType.MESH)

    row = me // 2
    side = lax.rem(me, 2)
    other = 1 - side
    pair = me + 1 - 2 * side
    own_base = (row // half) * half
    far_base = half - own_base

    def near(s):
        return own_base + lax.rem(row + s, half)

    def across(s):
        return far_base + lax.rem(row + s, half)

    mates = [near(s) for s in range(1, half)]
    partner = across(0)
    mate_partners = [across(s) for s in range(1, half)]

    pick = pltpu.make_async_copy(chosen, picked, loc.at[10])
    pick.start()
    own_proj = pltpu.make_async_copy(proj, proj_r.at[side, row], loc.at[0])
    g_load = pltpu.make_async_copy(g_hbm, g_in, loc.at[1])
    g_load.start()
    for t, src in enumerate((q_hbm, k_hbm, v_hbm)):
        pltpu.make_async_copy(src, qkv_in.at[t], loc.at[2]).start()
    own_proj.start()
    pltpu.make_async_copy(chosen, kept_out, loc.at[11]).start()

    def chosen_rows(load):
        total = None
        for j, mark in enumerate(marks):
            term = load(slice(j * block, (j + 1) * block)).astype(jnp.float32) * mark
            total = term if total is None else total + term
        return total.astype(bf16)

    def arrived(view, recv):
        ctx_copy(view, view, s_proj, recv, pair).wait_recv()

    def sent(view, send):
        ctx_copy(view, view, send, r_pp, pair).wait_send()

    with scope("B_barrier"):
        pl.semaphore_wait(barrier, n - 1 + dn - 1)

    own_block = proj_r.at[side, row]
    for a in [partner] + mates:
        ctx_copy(proj, own_block, s_proj, proj_rs.at[row], 2 * a + side).start()

    with scope("A_loadg"):
        pick.wait()
        marks = block_marks(picked, me, qkv_in.shape[1] // block)
        g_load.wait()
        for j in range(dn):
            g[j] = chosen_rows(lambda r: g_in[r, j * dc:(j + 1) * dc])
        g_r[side, md] = g[md]
    twin = md + 1 - 2 * lax.rem(md, 2)
    dp_far = [lax.rem(md + 2 * s, dn) for s in range(1, dn // 2)]
    dp_cross = [lax.rem(twin + 2 * s, dn) for s in range(1, dn // 2)]

    for peer in dp_far + dp_cross + [twin]:
        dp_copy(g.at[peer], g_r.at[side, md], s_g, g_rs.at[md], peer).start()
    ctx_copy(g.at[md], g_r.at[side, md], s_gp, r_gp, pair).start()
    with scope("A_loadqkv"):
        pltpu.make_async_copy(qkv_in, qkv_in, loc.at[2]).wait()
        for t in range(3):
            for h in range(n):
                qkv[h, t] = chosen_rows(lambda r: qkv_in[t, r, h * dh:(h + 1) * dh])
        qkv_r[me] = qkv[me]

    def send_qkv(peers):
        for peer in peers:
            ctx_copy(qkv.at[peer], qkv_r.at[me], s_qkv, r_qkv, peer).start()

    send_qkv([2 * a + side for a in [partner] + mate_partners])

    down = lax.broadcasted_iota(jnp.int32, (block, block), 0)
    for j in range(n):
        entry = picked[0, j]
        kpos[j * block:(j + 1) * block] = down + jnp.where(entry >= 0, entry * block, FAR)

    def proj_arrived(a):
        arrived(proj_r.at[side, a], proj_rs.at[a])

    with scope("C_waitg"):
        for peer in [twin] + dp_far + dp_cross:
            view = g_r.at[side, peer]
            arrived(view, g_rs.at[peer])
            ctx_copy(view, view, s_gp, r_gp, pair).start()
    with scope("D_waitpartner"):
        proj_arrived(partner)
        view = proj_r.at[side, partner]
        for a in mates:
            ctx_copy(view, view, s_pass, proj_rs.at[partner], 2 * a + side).start()
    send_qkv([2 * a + other for a in [partner] + mate_partners])
    send_qkv([2 * a + s for a in mates for s in (side, other)] + [pair])
    own_proj.wait()

    def part(a, b):
        k = 2 * a + b
        out = dot_nt(g_r[b].reshape(dn * block, dc), proj_r[side, a]).astype(bf16)
        agp_s[k] = out.reshape(dn, block, dh)
        for peer in dp_far + dp_cross + [twin]:
            dp_copy(agp_s.at[k, peer], agp_r.at[k, md], s_agp, agp_rs.at[k], peer).start()

    def finish(a, b):
        k = 2 * a + b
        arrived(agp_r.at[k, pl.ds(0, dn - 1)], agp_rs.at[k])
        total = agp_s[k, md].astype(jnp.float32)
        for peer in dp_peers:
            total = total + agp_r[k, peer].astype(jnp.float32)
        if a is row:
            ag_r[2 * row + b] = total.astype(bf16)
        else:
            ag_s[k] = total.astype(bf16)
            ctx_copy(ag_s.at[k], ag_r.at[2 * row + b], s_ag, ag_rs.at[row], 2 * a + side).start()

    def parts(names, b, waiting, lag):
        for a in names:
            with scope("G_part"):
                part(a, b)
            waiting.append((a, b))
            if len(waiting) > lag:
                with scope("H_finish"):
                    finish(*waiting.pop(0))

    waiting = []
    with scope("E_waitmate"):
        for a in mates:
            proj_arrived(a)
    parts([partner] + mates + [row], side, waiting, n)
    with scope("F_waitpairg"):
        arrived(g_r.at[other], r_gp)
    parts([partner] + mates + [row], other, waiting, n)
    with scope("F_waitsecond"):
        for a in mate_partners:
            proj_arrived(a)
    for b in (side, other):
        parts(mate_partners, b, waiting, rows)
    with scope("H_finish"):
        for a, b in waiting:
            finish(a, b)
    ctx_copy(proj_r.at[side], proj_r.at[side], s_pp, r_pp, pair).start()

    with scope("I_waitqkv"):
        arrived(qkv_r.at[pl.ds(0, n - 1)], r_qkv)
    k_t[...] = transposed(qkv_r[:, 1].reshape(slots, dh))
    v_t[...] = transposed(qkv_r[:, 2].reshape(slots, dh))

    def ordered(k):
        late = k // half
        return far_base * (1 - late) + own_base * late + lax.rem(row + k + late, half)

    def forward(k, carry):
        i = ordered(k)
        q = qkv_r[pl.ds(2 * i, 2), 0].reshape(width, dh)
        keys = qkv_r[:, 1].reshape(slots, dh)
        scores = dot_nt(keys, q)
        key_pos = kpos[...]
        key_pos = jnp.concatenate([key_pos, key_pos], axis=1)
        lane = lax.broadcasted_iota(jnp.int32, (1, width), 1)
        one, two = picked[0, 2 * i], picked[0, 2 * i + 1]
        one = jnp.where(one >= 0, one * block, -FAR)
        two = jnp.where(two >= 0, (two - 1) * block, -FAR)
        query_pos = lane + jnp.where(lane < block, one, two)
        scores = jnp.where(key_pos <= query_pos, scores * (scale * LOG2E), -1e30)
        e = jnp.exp2(scores - jnp.max(scores, axis=0, keepdims=True))
        p = (e * (1.0 / jnp.sum(e, axis=0, keepdims=True))).astype(bf16)
        p_s[i] = p
        a_t = dot_nn(v_t[...], p)
        attn_t[i] = a_t.astype(bf16)
        attn_s[i] = a_t.T.astype(bf16)

        @pl.when(k < half)
        def _():
            ctx_copy(attn_s.at[i], attn_r.at[row], s_attn, r_attn0, 2 * i + side).start()

        @pl.when((k >= half) & (k < rows - 1))
        def _():
            ctx_copy(attn_s.at[i], attn_r.at[row], s_attn, r_attn1, 2 * i + side).start()

        @pl.when(k == rows - 1)
        def _():
            pltpu.make_async_copy(attn_s.at[i], attn_r.at[i], loc.at[3]).start()

        return carry

    with scope("J_forward"):
        lax.fori_loop(0, rows, forward, 0)

    dk_acc[...] = jnp.zeros_like(dk_acc)
    dv_acc[...] = jnp.zeros_like(dv_acc)

    def heads_of_me(ref):
        return ref.at[:, pl.ds(pl.multiple_of(me * dh, dh), dh)]

    def backward(k, carry):
        i = ordered(k)
        with scope("K_waitag"):
            @pl.when(k < rows - 1)
            def _():
                arrived(ag_r.at[pl.ds(2 * i, 2)], ag_rs.at[i])

        q = qkv_r[pl.ds(2 * i, 2), 0].reshape(width, dh)
        v = qkv_r[:, 2].reshape(slots, dh)
        da = ag_r[pl.ds(2 * i, 2)].reshape(width, dh)
        delta = jnp.sum(da.astype(jnp.float32).T * attn_t[i].astype(jnp.float32), axis=0, keepdims=True)
        p = p_s[i]
        ds = (p.astype(jnp.float32) * (dot_nt(v, da) - delta)).astype(bf16)
        dq_t = dot_nn(k_t[...], ds) * scale
        dq_s[pl.ds(2 * i, 2)] = dq_t.T.astype(bf16).reshape(2, block, dh)
        for t in range(2):
            peer = 2 * i + t

            @pl.when(peer != me)
            def _():
                ctx_copy(dq_s.at[peer], heads_of_me(dq_r), s_dq, r_dq, peer).start()

            @pl.when(peer == me)
            def _():
                pltpu.make_async_copy(dq_s.at[peer], heads_of_me(dq_r), loc.at[4]).start()

        dk_acc[...] += dot_nn(ds, q)
        dv_acc[...] += dot_nn(p, da)
        return carry

    with scope("L_backward"):
        lax.fori_loop(0, rows, backward, 0)

    dkv_s[:, 0] = (dk_acc[...] * scale).astype(bf16).reshape(n, block, dh)
    dkv_s[:, 1] = dv_acc[...].astype(bf16).reshape(n, block, dh)

    my_dkv = dkv_r.at[:, :, pl.ds(pl.multiple_of(me * dh, dh), dh)]

    def send_dkv(peers):
        for peer in peers:
            ctx_copy(dkv_s.at[peer], my_dkv, s_dkv, r_dkv, peer).start()

    far_rows = [k + (rows - 1 - 2 * k) * (1 - row // half) for k in range(half)]
    send_dkv([2 * a + side for a in far_rows + mates])
    own_dkv = pltpu.make_async_copy(dkv_s.at[me], my_dkv, loc.at[5])
    own_dkv.start()

    def spread(src, dst_of, send, recv, own_sem):
        for s, peer in enumerate(dp_far):
            dp_copy(src, dst_of(md), send, recv.at[1 + s], peer).start()
        dp_copy(src, dst_of(md), send, recv.at[0], twin).start()
        copy = pltpu.make_async_copy(src, dst_of(md), own_sem)
        copy.start()
        return copy

    def hand_over(dst_of, send, recv):
        for s in range(1, dn // 2):
            peer = lax.rem(md + dn - 2 * s, dn)
            arrived(dst_of(peer), recv.at[s])
            dp_copy(dst_of(peer), dst_of(peer), send, recv.at[0], twin).start()

    groups = [pl.ds(far_base, half), pl.ds(own_base, half)]
    with scope("M_waitattn"):
        arrived(attn_r.at[groups[0]], r_attn0)
    own_far = spread(attn_r.at[groups[0]], lambda d: attn_d.at[0, d, pl.ds(0, half)], s_ad, ad_rs.at[0], loc.at[6])
    with scope("M_waitattn"):
        if half > 1:
            arrived(attn_r.at[pl.ds(0, half - 1)], r_attn1)
        pltpu.make_async_copy(attn_s.at[row], attn_r.at[row], loc.at[3]).wait()
    own_near = spread(attn_r.at[groups[1]], lambda d: attn_d.at[1, d, pl.ds(0, half)], s_ad, ad_rs.at[1], loc.at[7])
    ctx_copy(attn_r.at[:, pl.ds(pl.multiple_of(other * block, block), block)], attn_y, s_ap, r_ap, pair).start()

    inner = lax.rem(row, half) == (half - 1) * (1 - row // half)

    send_dkv([2 * a + other for a in far_rows + mates] + [pair])
    def weight(t, a):
        total = None
        for b in range(2):
            heads_of = attn_d[t, :, lax.rem(a, half), b * block:(b + 1) * block].reshape(dn * block, dh)
            term = dot_nn(transposed(heads_of), g_r[b].reshape(dn * block, dc))
            total = term if total is None else total + term
        return total

    def send_w(slot, value, dst, recv, peer_row):
        w_s[slot] = value.astype(bf16)
        ctx_copy(w_s.at[slot], dst, s_w, recv, 2 * peer_row + side).start()

    def spread_done(t, own):
        own.wait()
        arrived(attn_d.at[t, pl.ds(0, dn // 2)], ad_rs.at[t, 0])

    with scope("N_handover0"):
        hand_over(lambda d: attn_d.at[0, d, pl.ds(0, half)], s_ad, ad_rs.at[0])
    with scope("N_waitpair"):
        arrived(attn_y, r_ap)
    own_ae = spread(attn_y, lambda d: attn_e.at[d], s_ae, ae_rs, loc.at[8])
    with scope("N_handover1"):
        hand_over(lambda d: attn_d.at[1, d, pl.ds(0, half)], s_ad, ad_rs.at[1])
    with scope("N_waitspread0"):
        spread_done(0, own_far)
    with scope("P_weight"):
        for k, a in enumerate(far_rows):
            w_c[k] = weight(0, a)

        @pl.when(jnp.logical_not(inner))
        def _():
            for k in range(half):
                send_w(k, w_c[k], w_x.at[lax.rem(row, half), k], r_wx, own_base + (half - 1) * (1 - row // half))
    with scope("N_waitspread1"):
        spread_done(1, own_near)
    with scope("P_weight"):
        for k, a in enumerate(mates):
            send_w(half + k, weight(1, a), w_m.at[row], r_wm, a)
        w_out[...] = weight(1, row)
    def cross_sum():
        if mates:
            arrived(w_x.at[pl.ds(0, half - 1)], r_wx)
        for k, a in enumerate(far_rows):
            total = w_c[k]
            for mate in mates:
                total = total + w_x[lax.rem(mate, half), k].astype(jnp.float32)
            send_w(k, total, w_p, r_wp, a)

    with scope("O_handover"):
        hand_over(lambda d: attn_e.at[d], s_ae, ae_rs)
    with scope("S_waitinner"):
        pl.when(inner)(cross_sum)
    with scope("O_waitrows"):
        arrived(proj_r.at[other], r_pp)
        own_ae.wait()
        arrived(attn_e.at[pl.ds(0, dn // 2)], ae_rs.at[0])

    mine = pl.ds(pl.multiple_of(side * block, block), block)

    def mix_step(k, carry):
        j = lax.rem(md // 2 + 1 + k, dn // 2)

        def two(ref, *at):
            return ref[at].reshape(width, dh)

        d = pl.ds(2 * j, 2)
        t_of = [row // half if a // half else 1 - row // half for a in range(rows)]
        here = jnp.concatenate([two(attn_d, t_of[a], d, a % half, mine) for a in range(rows)], axis=1)
        there = jnp.concatenate([two(attn_e, d, a) for a in range(rows)], axis=1)
        out = dot_nn(here, proj_r[side].reshape(rows * dh, dc)) + dot_nn(there, proj_r[other].reshape(rows * dh, dc))
        mix_s[d] = out.astype(bf16).reshape(2, block, dc)
        for t in range(2):
            peer = 2 * j + t

            @pl.when(peer != md)
            def _():
                dp_copy(mix_s.at[peer], my_columns, s_mix, r_mix, peer).start()

            @pl.when(peer == md)
            def _():
                pltpu.make_async_copy(mix_s.at[peer], my_columns, loc.at[9]).start()

        return carry

    my_columns = mix_r.at[:, pl.ds(pl.multiple_of(md * dc, dc), dc)]
    with scope("Q_mix"):
        lax.fori_loop(0, dn // 2, mix_step, 0)

    with scope("T_waitdq"):
        pltpu.make_async_copy(dq_s.at[me], heads_of_me(dq_r), loc.at[4]).wait()
        arrived(dq_r.at[:, pl.ds(0, (n - 1) * dh)], r_dq)
    with scope("U_waitdkv"):
        own_dkv.wait()
        arrived(dkv_r.at[:, :, pl.ds(0, (n - 1) * dh)], r_dkv)
    with scope("W_waitmates"):
        if mates:
            arrived(w_m.at[pl.ds(0, half - 1)], r_wm)
        for a in mates:
            w_out[...] += w_m[a].astype(jnp.float32)
    with scope("X_waitpartner"):
        arrived(w_p, r_wp)
        w_out[...] += w_p[...].astype(jnp.float32)
    with scope("V_waitmix"):
        pltpu.make_async_copy(mix_s.at[md], my_columns, loc.at[9]).wait()
        arrived(mix_r.at[:, pl.ds(0, (dn - 1) * dc)], r_mix)

    pltpu.make_async_copy(chosen, kept_out, loc.at[11]).wait()
    with scope("Y_waitsend"):
        blocks = pl.ds(0, n - 1)
        others = pl.ds(0, dn - 1)
        sent(qkv_r.at[pl.ds(0, n - 1)], s_qkv)
        sent(proj_r.at[0, pl.ds(0, half)], s_proj)
        if mates:
            sent(proj_r.at[0, pl.ds(0, half - 1)], s_pass)
        sent(proj_r.at[0], s_pp)
        sent(g.at[others], s_g)
        sent(agp_s.at[:, others], s_agp)
        sent(ag_s.at[pl.ds(0, n - 2)], s_ag)
        sent(g_r.at[0], s_gp)
        sent(attn_s.at[pl.ds(0, rows - 1)], s_attn)
        sent(dq_s.at[blocks], s_dq)
        sent(dkv_s.at[blocks], s_dkv)
        sent(attn_d.at[:, others], s_ad)
        sent(attn_y, s_ap)
        sent(attn_e.at[others], s_ae)
        sent(w_s.at[pl.ds(0, rows - 1)], s_w)
        sent(mix_s.at[others], s_mix)


def shards(queries, keys, values, out_grad, chosen, proj):
    n = lax.axis_size("ctx")
    dn = lax.axis_size("dp")
    tokens = queries.shape[1]
    hd = queries.shape[2]
    dh = hd // n
    dc = proj.shape[1]
    slots = n * BLOCK
    width = 2 * BLOCK
    rows = n // 2
    half = rows // 2
    bf16, f32 = jnp.bfloat16, jnp.float32
    sem = pltpu.SemaphoreType.DMA
    blocks = (n, BLOCK, dh)
    pairs = (rows, width, dh)
    sheets = (rows, dh, dc)
    buffers = [
        ((3, tokens, hd), bf16), ((tokens, dn * dc), bf16), ((n, 3, BLOCK, dh), bf16), ((dn, BLOCK, dc), bf16),
        ((slots, BLOCK), jnp.int32), ((n, 3, BLOCK, dh), bf16), ((2, dn, BLOCK, dc), bf16), ((2,) + sheets, bf16),
        ((n, dn, BLOCK, dh), bf16), ((n, dn, BLOCK, dh), bf16), (blocks, bf16), (blocks, bf16),
        (pairs, bf16), (pairs, bf16), ((rows, BLOCK, dh), bf16), ((2, dn, half, width, dh), bf16),
        ((dn, rows, BLOCK, dh), bf16), ((rows, dh, width), bf16),
        ((rows, slots, width), bf16), ((dh, slots), bf16), ((dh, slots), bf16),
        (blocks, bf16), ((n, 2, BLOCK, dh), bf16), ((slots, dh), f32), ((slots, dh), f32),
        ((half, dh, dc), f32), (sheets, bf16), ((half, half, dh, dc), bf16), (sheets, bf16), ((dh, dc), bf16), ((dn, BLOCK, dc), bf16),
    ]
    held = sum(math.prod(shape) * jnp.dtype(kind).itemsize for shape, kind in buffers)
    sems = [sem((16,)), sem((12,)), sem((rows,)), sem((dn,)), sem((n,)), sem((rows,)), sem((2, dn // 2)), sem((dn // 2,)), sem((12,))]
    vmem = pl.BlockSpec(memory_space=pltpu.VMEM)
    picks = pltpu.SMEM(chosen.shape, chosen.dtype)
    free = pl.BlockSpec(memory_space=pl.ANY)
    hbm = pl.BlockSpec(memory_space=pltpu.HBM)

    def kept(x):
        return pltpu.with_memory_space_constraint(x, pltpu.HBM)

    chosen = kept(chosen)
    dq, dkv, weight_grad, mixed, placed = pl.pallas_call(
        functools.partial(kernel, n, dn, 1.0 / math.sqrt(dh)),
        out_shape=(
            jax.ShapeDtypeStruct((BLOCK, hd), bf16),
            jax.ShapeDtypeStruct((2, BLOCK, hd), bf16),
            jax.ShapeDtypeStruct((dh, dc), f32),
            jax.ShapeDtypeStruct((BLOCK, dn * dc), bf16),
            jax.ShapeDtypeStruct(chosen.shape, chosen.dtype),
        ),
        in_specs=[hbm] * 6,
        out_specs=[free, free, vmem, free, free],
        scratch_shapes=[picks] + [pltpu.VMEM(shape, kind) for shape, kind in buffers] + sems,
        compiler_params=pltpu.CompilerParams(
            collective_id=0, has_side_effects=True, vmem_limit_bytes=min(held + SPARE, 60 * MIB)),
    )(chosen, *[kept(x) for x in (queries[0], keys[0], values[0], out_grad[0], proj)])

    wide = (tokens, dn * dc)
    thin = (tokens, hd)
    count = tokens // BLOCK
    out, q_grad, k_grad, v_grad, proj_grad = pl.pallas_call(
        functools.partial(place_kernel, count),
        out_shape=(
            jax.ShapeDtypeStruct(wide, bf16), jax.ShapeDtypeStruct(thin, bf16), jax.ShapeDtypeStruct(thin, bf16),
            jax.ShapeDtypeStruct(thin, bf16), jax.ShapeDtypeStruct((dh, dc), f32)),
        in_specs=[vmem] + [free] * 4,
        out_specs=[hbm] * 5,
        scratch_shapes=[pltpu.VMEM((BLOCK, max(dn * dc, hd)), bf16), sem((count, 4)), sem((1,))],
        compiler_params=pltpu.CompilerParams(vmem_limit_bytes=8 * MIB),
    )(placed, mixed, dq, dkv, weight_grad)
    return out[None], q_grad[None], k_grad[None], v_grad[None], proj_grad


def solution(mesh):
    rows = P("dp", "ctx", None)
    return jax.shard_map(
        shards,
        mesh=mesh,
        in_specs=(rows, rows, rows, rows, P("dp", None), P("ctx", "dp")),
        out_specs=(rows, rows, rows, rows, P("ctx", "dp")),
        check_vma=False,
    )
```

```python
import functools
import math

import jax
import jax.numpy as jnp
from jax import lax
from jax.experimental import pallas as pl
from jax.experimental.pallas import tpu as pltpu
from jax.sharding import PartitionSpec as P

BLOCK = 128
FAR = 1 << 30
MIB = 1024 * 1024
LOG2E = math.log2(math.e)
SPARE = 8 * MIB

scope = jax.named_scope


def dot_nt(a, b):
    return lax.dot_general(a, b, (((1,), (1,)), ((), ())), preferred_element_type=jnp.float32)


def dot_nn(a, b):
    return lax.dot_general(a, b, (((1,), (0,)), ((), ())), preferred_element_type=jnp.float32)


def transposed(a):
    return a.astype(jnp.float32).T.astype(a.dtype)


def local_block(entry, me, count):
    spans = count // 2
    index = jnp.maximum(entry, 0)
    return jnp.where(index // spans == me, index % spans, spans + index % spans)


def block_marks(picked, me, count):
    entry = picked[0, me]
    local = jnp.where(entry >= 0, local_block(entry, me, count), -1)
    return [jnp.where(local == j, 1.0, 0.0) for j in range(count)]


def place_kernel(count, chosen, mix, dq, dkv, w, out, q_out, k_out, v_out, w_out, zero, sems, w_sem):
    block = dq.shape[0]
    w_copy = pltpu.make_async_copy(w, w_out, w_sem.at[0])
    w_copy.start()
    zero[...] = jnp.zeros_like(zero)
    me = lax.axis_index("ctx")
    with scope("a_pick"):
        lane = lax.broadcasted_iota(jnp.int32, chosen.shape, 1)
        entry = jnp.max(jnp.where(lane == me, chosen[...], -1))
        local = jnp.where(entry >= 0, local_block(entry, me, count), -1)
    outs = ((mix, out), (dq, q_out), (dkv.at[0], k_out), (dkv.at[1], v_out))
    with scope("b_issue"):
        for j in range(count):
            for t, (src, dst) in enumerate(outs):
                rows = dst.at[pl.ds(j * block, block)]

                @pl.when(local == j)
                def _():
                    pltpu.make_async_copy(src, rows, sems.at[j, t]).start()

                @pl.when(local != j)
                def _():
                    pltpu.make_async_copy(zero.at[:, pl.ds(0, dst.shape[1])], rows, sems.at[j, t]).start()

    with scope("c_wait"):
        for j in range(count):
            for t, (_, dst) in enumerate(outs):
                view = dst.at[pl.ds(j * block, block)]
                pltpu.make_async_copy(view, view, sems.at[j, t]).wait()
        w_copy.wait()


def kernel(
    n, dn, scale,
    chosen, q_hbm, k_hbm, v_hbm, g_hbm, proj,
    dq_r, dkv_r, w_out, mix_r, kept_out,
    picked, qkv_in, g_in, qkv, g, kpos, qkv_r, g_r, proj_r, agp_s, agp_r, ag_s, ag_r,
    attn_s, attn_r, attn_y, attn_d, attn_e, attn_t,
    p_s, k_t, v_t, dq_s, dkv_s, dk_acc, dv_acc, w_c, w_s, w_x, w_m, w_p, mix_s,
    ss, rs, proj_rs, g_rs, agp_rs, ag_rs, ad_rs, ae_rs, loc,
):
    me = lax.axis_index("ctx")
    md = lax.axis_index("dp")
    bf16 = jnp.bfloat16
    block, dh = qkv.shape[2], qkv.shape[3]
    dc = proj.shape[1]
    slots = n * block
    width = 2 * block
    rows = n // 2
    half = rows // 2
    s_proj, s_g, s_qkv, s_agp, s_ag, s_gp, s_attn, s_dq, s_dkv, s_ad, s_ap, s_ae, s_w, s_mix, s_pass, s_pp = (
        ss.at[k] for k in range(16))
    r_pp, r_qkv, r_gp, r_attn0, r_attn1, r_dq, r_dkv, r_ap, r_wx, r_wm, r_wp, r_mix = (rs.at[k] for k in range(12))

    def ctx_copy(src, dst, send, recv, peer):
        return pltpu.make_async_remote_copy(
            src_ref=src, dst_ref=dst, send_sem=send, recv_sem=recv,
            device_id={"ctx": peer}, device_id_type=pl.DeviceIdType.MESH)

    def dp_copy(src, dst, send, recv, peer):
        return pltpu.make_async_remote_copy(
            src_ref=src, dst_ref=dst, send_sem=send, recv_sem=recv,
            device_id={"dp": peer}, device_id_type=pl.DeviceIdType.MESH)

    ctx_peers = [lax.rem(me + s, n) for s in range(1, n)]
    dp_peers = [lax.rem(md + s, dn) for s in range(1, dn)]

    barrier = pltpu.get_barrier_semaphore()
    for peer in ctx_peers:
        pl.semaphore_signal(barrier, inc=1, device_id={"ctx": peer}, device_id_type=pl.DeviceIdType.MESH)
    for peer in dp_peers:
        pl.semaphore_signal(barrier, inc=1, device_id={"dp": peer}, device_id_type=pl.DeviceIdType.MESH)

    row = me // 2
    side = lax.rem(me, 2)
    other = 1 - side
    pair = me + 1 - 2 * side
    own_base = (row // half) * half
    far_base = half - own_base

    def near(s):
        return own_base + lax.rem(row + s, half)

    def across(s):
        return far_base + lax.rem(row + s, half)

    mates = [near(s) for s in range(1, half)]
    partner = across(0)
    mate_partners = [across(s) for s in range(1, half)]

    pick = pltpu.make_async_copy(chosen, picked, loc.at[10])
    pick.start()
    own_proj = pltpu.make_async_copy(proj, proj_r.at[side, row], loc.at[0])
    g_load = pltpu.make_async_copy(g_hbm, g_in, loc.at[1])
    g_load.start()
    for t, src in enumerate((q_hbm, k_hbm, v_hbm)):
        pltpu.make_async_copy(src, qkv_in.at[t], loc.at[2]).start()
    own_proj.start()
    pltpu.make_async_copy(chosen, kept_out, loc.at[11]).start()

    def chosen_rows(load):
        total = None
        for j, mark in enumerate(marks):
            term = load(slice(j * block, (j + 1) * block)).astype(jnp.float32) * mark
            total = term if total is None else total + term
        return total.astype(bf16)

    def arrived(view, recv):
        ctx_copy(view, view, s_proj, recv, pair).wait_recv()

    def sent(view, send):
        ctx_copy(view, view, send, r_pp, pair).wait_send()

    with scope("B_barrier"):
        pl.semaphore_wait(barrier, n - 1 + dn - 1)

    own_block = proj_r.at[side, row]
    for a in [partner] + mates:
        ctx_copy(proj, own_block, s_proj, proj_rs.at[row], 2 * a + side).start()

    with scope("A_loadg"):
        pick.wait()
        marks = block_marks(picked, me, qkv_in.shape[1] // block)
        g_load.wait()
        for j in range(dn):
            g[j] = chosen_rows(lambda r: g_in[r, j * dc:(j + 1) * dc])
        g_r[side, md] = g[md]
    twin = md + 1 - 2 * lax.rem(md, 2)
    dp_far = [lax.rem(md + 2 * s, dn) for s in range(1, dn // 2)]
    dp_cross = [lax.rem(twin + 2 * s, dn) for s in range(1, dn // 2)]

    for peer in dp_far + dp_cross + [twin]:
        dp_copy(g.at[peer], g_r.at[side, md], s_g, g_rs.at[md], peer).start()
    ctx_copy(g.at[md], g_r.at[side, md], s_gp, r_gp, pair).start()
    with scope("A_loadqkv"):
        pltpu.make_async_copy(qkv_in, qkv_in, loc.at[2]).wait()
        for t in range(3):
            for h in range(n):
                qkv[h, t] = chosen_rows(lambda r: qkv_in[t, r, h * dh:(h + 1) * dh])
        qkv_r[me] = qkv[me]

    def send_qkv(peers):
        for peer in peers:
            ctx_copy(qkv.at[peer], qkv_r.at[me], s_qkv, r_qkv, peer).start()

    send_qkv([2 * a + side for a in [partner] + mate_partners])

    down = lax.broadcasted_iota(jnp.int32, (block, block), 0)
    for j in range(n):
        entry = picked[0, j]
        kpos[j * block:(j + 1) * block] = down + jnp.where(entry >= 0, entry * block, FAR)

    def proj_arrived(a):
        arrived(proj_r.at[side, a], proj_rs.at[a])

    with scope("C_waitg"):
        for peer in [twin] + dp_far + dp_cross:
            view = g_r.at[side, peer]
            arrived(view, g_rs.at[peer])
            ctx_copy(view, view, s_gp, r_gp, pair).start()
    with scope("D_waitpartner"):
        proj_arrived(partner)
        view = proj_r.at[side, partner]
        for a in mates:
            ctx_copy(view, view, s_pass, proj_rs.at[partner], 2 * a + side).start()
    send_qkv([2 * a + other for a in [partner] + mate_partners])
    send_qkv([2 * a + s for a in mates for s in (side, other)] + [pair])
    own_proj.wait()

    def part(a, b):
        k = 2 * a + b
        out = dot_nt(g_r[b].reshape(dn * block, dc), proj_r[side, a]).astype(bf16)
        agp_s[k] = out.reshape(dn, block, dh)
        for peer in dp_far + dp_cross + [twin]:
            dp_copy(agp_s.at[k, peer], agp_r.at[k, md], s_agp, agp_rs.at[k], peer).start()

    def finish(a, b):
        k = 2 * a + b
        arrived(agp_r.at[k, pl.ds(0, dn - 1)], agp_rs.at[k])
        total = agp_s[k, md].astype(jnp.float32)
        for peer in dp_peers:
            total = total + agp_r[k, peer].astype(jnp.float32)
        if a is row:
            ag_r[2 * row + b] = total.astype(bf16)
        else:
            ag_s[k] = total.astype(bf16)
            ctx_copy(ag_s.at[k], ag_r.at[2 * row + b], s_ag, ag_rs.at[row], 2 * a + side).start()

    def parts(names, b, waiting, lag):
        for a in names:
            with scope("G_part"):
                part(a, b)
            waiting.append((a, b))
            if len(waiting) > lag:
                with scope("H_finish"):
                    finish(*waiting.pop(0))

    waiting = []
    with scope("E_waitmate"):
        for a in mates:
            proj_arrived(a)
    parts([partner] + mates + [row], side, waiting, n)
    with scope("F_waitpairg"):
        arrived(g_r.at[other], r_gp)
    parts([partner] + mates + [row], other, waiting, n)
    with scope("F_waitsecond"):
        for a in mate_partners:
            proj_arrived(a)
    for b in (side, other):
        parts(mate_partners, b, waiting, rows)
    with scope("H_finish"):
        for a, b in waiting:
            finish(a, b)
    ctx_copy(proj_r.at[side], proj_r.at[side], s_pp, r_pp, pair).start()

    with scope("I_waitqkv"):
        arrived(qkv_r.at[pl.ds(0, n - 1)], r_qkv)
    k_t[...] = transposed(qkv_r[:, 1].reshape(slots, dh))
    v_t[...] = transposed(qkv_r[:, 2].reshape(slots, dh))

    def ordered(k):
        late = k // half
        return far_base * (1 - late) + own_base * late + lax.rem(row + k + late, half)

    def forward(k, carry):
        i = ordered(k)
        q = qkv_r[pl.ds(2 * i, 2), 0].reshape(width, dh)
        keys = qkv_r[:, 1].reshape(slots, dh)
        scores = dot_nt(keys, q)
        key_pos = kpos[...]
        key_pos = jnp.concatenate([key_pos, key_pos], axis=1)
        lane = lax.broadcasted_iota(jnp.int32, (1, width), 1)
        one, two = picked[0, 2 * i], picked[0, 2 * i + 1]
        one = jnp.where(one >= 0, one * block, -FAR)
        two = jnp.where(two >= 0, (two - 1) * block, -FAR)
        query_pos = lane + jnp.where(lane < block, one, two)
        scores = jnp.where(key_pos <= query_pos, scores * (scale * LOG2E), -1e30)
        e = jnp.exp2(scores - jnp.max(scores, axis=0, keepdims=True))
        p = (e * (1.0 / jnp.sum(e, axis=0, keepdims=True))).astype(bf16)
        p_s[i] = p
        a_t = dot_nn(v_t[...], p)
        attn_t[i] = a_t.astype(bf16)
        attn_s[i] = a_t.T.astype(bf16)

        @pl.when(k < half)
        def _():
            ctx_copy(attn_s.at[i], attn_r.at[row], s_attn, r_attn0, 2 * i + side).start()

        @pl.when((k >= half) & (k < rows - 1))
        def _():
            ctx_copy(attn_s.at[i], attn_r.at[row], s_attn, r_attn1, 2 * i + side).start()

        @pl.when(k == rows - 1)
        def _():
            pltpu.make_async_copy(attn_s.at[i], attn_r.at[i], loc.at[3]).start()

        return carry

    with scope("J_forward"):
        lax.fori_loop(0, rows, forward, 0)

    dk_acc[...] = jnp.zeros_like(dk_acc)
    dv_acc[...] = jnp.zeros_like(dv_acc)

    def heads_of_me(ref):
        return ref.at[:, pl.ds(pl.multiple_of(me * dh, dh), dh)]

    def backward(k, carry):
        i = ordered(k)
        with scope("K_waitag"):
            @pl.when(k < rows - 1)
            def _():
                arrived(ag_r.at[pl.ds(2 * i, 2)], ag_rs.at[i])

        q = qkv_r[pl.ds(2 * i, 2), 0].reshape(width, dh)
        v = qkv_r[:, 2].reshape(slots, dh)
        da = ag_r[pl.ds(2 * i, 2)].reshape(width, dh)
        delta = jnp.sum(da.astype(jnp.float32).T * attn_t[i].astype(jnp.float32), axis=0, keepdims=True)
        p = p_s[i]
        ds = (p.astype(jnp.float32) * (dot_nt(v, da) - delta)).astype(bf16)
        dq_t = dot_nn(k_t[...], ds) * scale
        dq_s[pl.ds(2 * i, 2)] = dq_t.T.astype(bf16).reshape(2, block, dh)
        for t in range(2):
            peer = 2 * i + t

            @pl.when(peer != me)
            def _():
                ctx_copy(dq_s.at[peer], heads_of_me(dq_r), s_dq, r_dq, peer).start()

            @pl.when(peer == me)
            def _():
                pltpu.make_async_copy(dq_s.at[peer], heads_of_me(dq_r), loc.at[4]).start()

        dk_acc[...] += dot_nn(ds, q)
        dv_acc[...] += dot_nn(p, da)
        return carry

    with scope("L_backward"):
        lax.fori_loop(0, rows, backward, 0)

    dkv_s[:, 0] = (dk_acc[...] * scale).astype(bf16).reshape(n, block, dh)
    dkv_s[:, 1] = dv_acc[...].astype(bf16).reshape(n, block, dh)

    my_dkv = dkv_r.at[:, :, pl.ds(pl.multiple_of(me * dh, dh), dh)]

    def send_dkv(peers):
        for peer in peers:
            ctx_copy(dkv_s.at[peer], my_dkv, s_dkv, r_dkv, peer).start()

    far_rows = [k + (rows - 1 - 2 * k) * (1 - row // half) for k in range(half)]
    own_dkv = pltpu.make_async_copy(dkv_s.at[me], my_dkv, loc.at[5])
    own_dkv.start()

    def spread(src, dst_of, send, recv, own_sem):
        for s, peer in enumerate(dp_far):
            dp_copy(src, dst_of(md), send, recv.at[1 + s], peer).start()
        dp_copy(src, dst_of(md), send, recv.at[0], twin).start()
        copy = pltpu.make_async_copy(src, dst_of(md), own_sem)
        copy.start()
        return copy

    def hand_over(dst_of, send, recv):
        for s in range(1, dn // 2):
            peer = lax.rem(md + dn - 2 * s, dn)
            arrived(dst_of(peer), recv.at[s])
            dp_copy(dst_of(peer), dst_of(peer), send, recv.at[0], twin).start()

    groups = [pl.ds(far_base, half), pl.ds(own_base, half)]
    with scope("M_waitattn"):
        arrived(attn_r.at[groups[0]], r_attn0)
    own_far = spread(attn_r.at[groups[0]], lambda d: attn_d.at[0, d, pl.ds(0, half)], s_ad, ad_rs.at[0], loc.at[6])
    with scope("M_waitattn"):
        if half > 1:
            arrived(attn_r.at[pl.ds(0, half - 1)], r_attn1)
        pltpu.make_async_copy(attn_s.at[row], attn_r.at[row], loc.at[3]).wait()
    own_near = spread(attn_r.at[groups[1]], lambda d: attn_d.at[1, d, pl.ds(0, half)], s_ad, ad_rs.at[1], loc.at[7])
    ctx_copy(attn_r.at[:, pl.ds(pl.multiple_of(other * block, block), block)], attn_y, s_ap, r_ap, pair).start()

    inner = lax.rem(row, half) == (half - 1) * (1 - row // half)

    send_dkv([2 * a + s for s in (side, other) for a in far_rows + mates] + [pair])
    def weight(t, a):
        total = None
        for b in range(2):
            heads_of = attn_d[t, :, lax.rem(a, half), b * block:(b + 1) * block].reshape(dn * block, dh)
            term = dot_nn(transposed(heads_of), g_r[b].reshape(dn * block, dc))
            total = term if total is None else total + term
        return total

    def send_w(slot, value, dst, recv, peer_row):
        w_s[slot] = value.astype(bf16)
        ctx_copy(w_s.at[slot], dst, s_w, recv, 2 * peer_row + side).start()

    def spread_done(t, own):
        own.wait()
        arrived(attn_d.at[t, pl.ds(0, dn // 2)], ad_rs.at[t, 0])

    with scope("N_handover0"):
        hand_over(lambda d: attn_d.at[0, d, pl.ds(0, half)], s_ad, ad_rs.at[0])
    with scope("N_waitpair"):
        arrived(attn_y, r_ap)
    own_ae = spread(attn_y, lambda d: attn_e.at[d], s_ae, ae_rs, loc.at[8])
    with scope("N_handover1"):
        hand_over(lambda d: attn_d.at[1, d, pl.ds(0, half)], s_ad, ad_rs.at[1])
    with scope("N_waitspread0"):
        spread_done(0, own_far)
    with scope("P_weight"):
        for k, a in enumerate(far_rows):
            w_c[k] = weight(0, a)

        @pl.when(jnp.logical_not(inner))
        def _():
            for k in range(half):
                send_w(k, w_c[k], w_x.at[lax.rem(row, half), k], r_wx, own_base + (half - 1) * (1 - row // half))
    with scope("N_waitspread1"):
        spread_done(1, own_near)
    with scope("P_weight"):
        for k, a in enumerate(mates):
            send_w(half + k, weight(1, a), w_m.at[row], r_wm, a)
        w_out[...] = weight(1, row)
    def cross_sum():
        if mates:
            arrived(w_x.at[pl.ds(0, half - 1)], r_wx)
        for k, a in enumerate(far_rows):
            total = w_c[k]
            for mate in mates:
                total = total + w_x[lax.rem(mate, half), k].astype(jnp.float32)
            send_w(k, total, w_p, r_wp, a)

    with scope("O_handover"):
        hand_over(lambda d: attn_e.at[d], s_ae, ae_rs)
    with scope("S_waitinner"):
        pl.when(inner)(cross_sum)
    with scope("O_waitrows"):
        arrived(proj_r.at[other], r_pp)
        own_ae.wait()
        arrived(attn_e.at[pl.ds(0, dn // 2)], ae_rs.at[0])

    mine = pl.ds(pl.multiple_of(side * block, block), block)

    def mix_step(k, carry):
        j = lax.rem(md // 2 + 1 + k, dn // 2)

        def two(ref, *at):
            return ref[at].reshape(width, dh)

        d = pl.ds(2 * j, 2)
        t_of = [row // half if a // half else 1 - row // half for a in range(rows)]
        here = jnp.concatenate([two(attn_d, t_of[a], d, a % half, mine) for a in range(rows)], axis=1)
        there = jnp.concatenate([two(attn_e, d, a) for a in range(rows)], axis=1)
        out = dot_nn(here, proj_r[side].reshape(rows * dh, dc)) + dot_nn(there, proj_r[other].reshape(rows * dh, dc))
        mix_s[d] = out.astype(bf16).reshape(2, block, dc)
        for t in range(2):
            peer = 2 * j + t

            @pl.when(peer != md)
            def _():
                dp_copy(mix_s.at[peer], my_columns, s_mix, r_mix, peer).start()

            @pl.when(peer == md)
            def _():
                pltpu.make_async_copy(mix_s.at[peer], my_columns, loc.at[9]).start()

        return carry

    my_columns = mix_r.at[:, pl.ds(pl.multiple_of(md * dc, dc), dc)]
    with scope("Q_mix"):
        lax.fori_loop(0, dn // 2, mix_step, 0)

    with scope("T_waitdq"):
        pltpu.make_async_copy(dq_s.at[me], heads_of_me(dq_r), loc.at[4]).wait()
        arrived(dq_r.at[:, pl.ds(0, (n - 1) * dh)], r_dq)
    with scope("U_waitdkv"):
        own_dkv.wait()
        arrived(dkv_r.at[:, :, pl.ds(0, (n - 1) * dh)], r_dkv)
    with scope("W_waitmates"):
        if mates:
            arrived(w_m.at[pl.ds(0, half - 1)], r_wm)
        for a in mates:
            w_out[...] += w_m[a].astype(jnp.float32)
    with scope("X_waitpartner"):
        arrived(w_p, r_wp)
        w_out[...] += w_p[...].astype(jnp.float32)
    with scope("V_waitmix"):
        pltpu.make_async_copy(mix_s.at[md], my_columns, loc.at[9]).wait()
        arrived(mix_r.at[:, pl.ds(0, (dn - 1) * dc)], r_mix)

    pltpu.make_async_copy(chosen, kept_out, loc.at[11]).wait()
    with scope("Y_waitsend"):
        blocks = pl.ds(0, n - 1)
        others = pl.ds(0, dn - 1)
        sent(qkv_r.at[pl.ds(0, n - 1)], s_qkv)
        sent(proj_r.at[0, pl.ds(0, half)], s_proj)
        if mates:
            sent(proj_r.at[0, pl.ds(0, half - 1)], s_pass)
        sent(proj_r.at[0], s_pp)
        sent(g.at[others], s_g)
        sent(agp_s.at[:, others], s_agp)
        sent(ag_s.at[pl.ds(0, n - 2)], s_ag)
        sent(g_r.at[0], s_gp)
        sent(attn_s.at[pl.ds(0, rows - 1)], s_attn)
        sent(dq_s.at[blocks], s_dq)
        sent(dkv_s.at[blocks], s_dkv)
        sent(attn_d.at[:, others], s_ad)
        sent(attn_y, s_ap)
        sent(attn_e.at[others], s_ae)
        sent(w_s.at[pl.ds(0, rows - 1)], s_w)
        sent(mix_s.at[others], s_mix)


def shards(queries, keys, values, out_grad, chosen, proj):
    n = lax.axis_size("ctx")
    dn = lax.axis_size("dp")
    tokens = queries.shape[1]
    hd = queries.shape[2]
    dh = hd // n
    dc = proj.shape[1]
    slots = n * BLOCK
    width = 2 * BLOCK
    rows = n // 2
    half = rows // 2
    bf16, f32 = jnp.bfloat16, jnp.float32
    sem = pltpu.SemaphoreType.DMA
    blocks = (n, BLOCK, dh)
    pairs = (rows, width, dh)
    sheets = (rows, dh, dc)
    buffers = [
        ((3, tokens, hd), bf16), ((tokens, dn * dc), bf16), ((n, 3, BLOCK, dh), bf16), ((dn, BLOCK, dc), bf16),
        ((slots, BLOCK), jnp.int32), ((n, 3, BLOCK, dh), bf16), ((2, dn, BLOCK, dc), bf16), ((2,) + sheets, bf16),
        ((n, dn, BLOCK, dh), bf16), ((n, dn, BLOCK, dh), bf16), (blocks, bf16), (blocks, bf16),
        (pairs, bf16), (pairs, bf16), ((rows, BLOCK, dh), bf16), ((2, dn, half, width, dh), bf16),
        ((dn, rows, BLOCK, dh), bf16), ((rows, dh, width), bf16),
        ((rows, slots, width), bf16), ((dh, slots), bf16), ((dh, slots), bf16),
        (blocks, bf16), ((n, 2, BLOCK, dh), bf16), ((slots, dh), f32), ((slots, dh), f32),
        ((half, dh, dc), f32), (sheets, bf16), ((half, half, dh, dc), bf16), (sheets, bf16), ((dh, dc), bf16), ((dn, BLOCK, dc), bf16),
    ]
    held = sum(math.prod(shape) * jnp.dtype(kind).itemsize for shape, kind in buffers)
    sems = [sem((16,)), sem((12,)), sem((rows,)), sem((dn,)), sem((n,)), sem((rows,)), sem((2, dn // 2)), sem((dn // 2,)), sem((12,))]
    vmem = pl.BlockSpec(memory_space=pltpu.VMEM)
    picks = pltpu.SMEM(chosen.shape, chosen.dtype)
    free = pl.BlockSpec(memory_space=pl.ANY)
    hbm = pl.BlockSpec(memory_space=pltpu.HBM)

    def kept(x):
        return pltpu.with_memory_space_constraint(x, pltpu.HBM)

    chosen = kept(chosen)
    dq, dkv, weight_grad, mixed, placed = pl.pallas_call(
        functools.partial(kernel, n, dn, 1.0 / math.sqrt(dh)),
        out_shape=(
            jax.ShapeDtypeStruct((BLOCK, hd), bf16),
            jax.ShapeDtypeStruct((2, BLOCK, hd), bf16),
            jax.ShapeDtypeStruct((dh, dc), f32),
            jax.ShapeDtypeStruct((BLOCK, dn * dc), bf16),
            jax.ShapeDtypeStruct(chosen.shape, chosen.dtype),
        ),
        in_specs=[hbm] * 6,
        out_specs=[free, free, vmem, free, free],
        scratch_shapes=[picks] + [pltpu.VMEM(shape, kind) for shape, kind in buffers] + sems,
        compiler_params=pltpu.CompilerParams(
            collective_id=0, has_side_effects=True, vmem_limit_bytes=min(held + SPARE, 60 * MIB)),
    )(chosen, *[kept(x) for x in (queries[0], keys[0], values[0], out_grad[0], proj)])

    wide = (tokens, dn * dc)
    thin = (tokens, hd)
    count = tokens // BLOCK
    out, q_grad, k_grad, v_grad, proj_grad = pl.pallas_call(
        functools.partial(place_kernel, count),
        out_shape=(
            jax.ShapeDtypeStruct(wide, bf16), jax.ShapeDtypeStruct(thin, bf16), jax.ShapeDtypeStruct(thin, bf16),
            jax.ShapeDtypeStruct(thin, bf16), jax.ShapeDtypeStruct((dh, dc), f32)),
        in_specs=[vmem] + [free] * 4,
        out_specs=[hbm] * 5,
        scratch_shapes=[pltpu.VMEM((BLOCK, max(dn * dc, hd)), bf16), sem((count, 4)), sem((1,))],
        compiler_params=pltpu.CompilerParams(vmem_limit_bytes=8 * MIB),
    )(placed, mixed, dq, dkv, weight_grad)
    return out[None], q_grad[None], k_grad[None], v_grad[None], proj_grad


def solution(mesh):
    rows = P("dp", "ctx", None)
    return jax.shard_map(
        shards,
        mesh=mesh,
        in_specs=(rows, rows, rows, rows, P("dp", None), P("ctx", "dp")),
        out_specs=(rows, rows, rows, rows, P("ctx", "dp")),
        check_vma=False,
    )
```

```python
import functools
import math

import jax
import jax.numpy as jnp
from jax import lax
from jax.experimental import pallas as pl
from jax.experimental.pallas import tpu as pltpu
from jax.sharding import PartitionSpec as P

BLOCK = 128
FAR = 1 << 30
MIB = 1024 * 1024
LOG2E = math.log2(math.e)
SPARE = 8 * MIB

scope = jax.named_scope


def dot_nt(a, b):
    return lax.dot_general(a, b, (((1,), (1,)), ((), ())), preferred_element_type=jnp.float32)


def dot_nn(a, b):
    return lax.dot_general(a, b, (((1,), (0,)), ((), ())), preferred_element_type=jnp.float32)


def transposed(a):
    return a.astype(jnp.float32).T.astype(a.dtype)


def local_block(entry, me, count):
    spans = count // 2
    index = jnp.maximum(entry, 0)
    return jnp.where(index // spans == me, index % spans, spans + index % spans)


def block_marks(picked, me, count):
    entry = picked[0, me]
    local = jnp.where(entry >= 0, local_block(entry, me, count), -1)
    return [jnp.where(local == j, 1.0, 0.0) for j in range(count)]


def place_kernel(count, chosen, mix, dq, dkv, w, out, q_out, k_out, v_out, w_out, zero, sems, w_sem):
    block = dq.shape[0]
    w_copy = pltpu.make_async_copy(w, w_out, w_sem.at[0])
    w_copy.start()
    zero[...] = jnp.zeros_like(zero)
    me = lax.axis_index("ctx")
    with scope("a_pick"):
        lane = lax.broadcasted_iota(jnp.int32, chosen.shape, 1)
        entry = jnp.max(jnp.where(lane == me, chosen[...], -1))
        local = jnp.where(entry >= 0, local_block(entry, me, count), -1)
    outs = ((mix, out), (dq, q_out), (dkv.at[0], k_out), (dkv.at[1], v_out))
    with scope("b_issue"):
        for j in range(count):
            for t, (src, dst) in enumerate(outs):
                rows = dst.at[pl.ds(j * block, block)]

                @pl.when(local == j)
                def _():
                    pltpu.make_async_copy(src, rows, sems.at[j, t]).start()

                @pl.when(local != j)
                def _():
                    pltpu.make_async_copy(zero.at[:, pl.ds(0, dst.shape[1])], rows, sems.at[j, t]).start()

    with scope("c_wait"):
        for j in range(count):
            for t, (_, dst) in enumerate(outs):
                view = dst.at[pl.ds(j * block, block)]
                pltpu.make_async_copy(view, view, sems.at[j, t]).wait()
        w_copy.wait()


def kernel(
    n, dn, scale,
    chosen, q_hbm, k_hbm, v_hbm, g_hbm, proj,
    dq_r, dkv_r, w_out, mix_r, kept_out,
    picked, qkv_in, g_in, qkv, g, kpos, qkv_r, g_r, proj_r, agp_s, agp_r, ag_s, ag_r,
    attn_s, attn_r, attn_y, attn_d, attn_e, attn_t,
    p_s, k_t, v_t, dq_s, dkv_s, dk_acc, dv_acc, w_c, w_s, w_x, w_m, w_p, mix_s, mix_acc,
    ss, rs, proj_rs, g_rs, agp_rs, ag_rs, ad_rs, ae_rs, loc,
):
    me = lax.axis_index("ctx")
    md = lax.axis_index("dp")
    bf16 = jnp.bfloat16
    block, dh = qkv.shape[2], qkv.shape[3]
    dc = proj.shape[1]
    slots = n * block
    width = 2 * block
    rows = n // 2
    half = rows // 2
    s_proj, s_g, s_qkv, s_agp, s_ag, s_gp, s_attn, s_dq, s_dkv, s_ad, s_ap, s_ae, s_w, s_mix, s_pass, s_pp = (
        ss.at[k] for k in range(16))
    r_pp, r_qkv, r_gp, r_attn0, r_attn1, r_dq, r_dkv, r_ap, r_wx, r_wm, r_wp, r_mix = (rs.at[k] for k in range(12))

    def ctx_copy(src, dst, send, recv, peer):
        return pltpu.make_async_remote_copy(
            src_ref=src, dst_ref=dst, send_sem=send, recv_sem=recv,
            device_id={"ctx": peer}, device_id_type=pl.DeviceIdType.MESH)

    def dp_copy(src, dst, send, recv, peer):
        return pltpu.make_async_remote_copy(
            src_ref=src, dst_ref=dst, send_sem=send, recv_sem=recv,
            device_id={"dp": peer}, device_id_type=pl.DeviceIdType.MESH)

    ctx_peers = [lax.rem(me + s, n) for s in range(1, n)]
    dp_peers = [lax.rem(md + s, dn) for s in range(1, dn)]

    barrier = pltpu.get_barrier_semaphore()
    for peer in ctx_peers:
        pl.semaphore_signal(barrier, inc=1, device_id={"ctx": peer}, device_id_type=pl.DeviceIdType.MESH)
    for peer in dp_peers:
        pl.semaphore_signal(barrier, inc=1, device_id={"dp": peer}, device_id_type=pl.DeviceIdType.MESH)

    row = me // 2
    side = lax.rem(me, 2)
    other = 1 - side
    pair = me + 1 - 2 * side
    own_base = (row // half) * half
    far_base = half - own_base

    def near(s):
        return own_base + lax.rem(row + s, half)

    def across(s):
        return far_base + lax.rem(row + s, half)

    mates = [near(s) for s in range(1, half)]
    partner = across(0)
    mate_partners = [across(s) for s in range(1, half)]

    pick = pltpu.make_async_copy(chosen, picked, loc.at[10])
    pick.start()
    own_proj = pltpu.make_async_copy(proj, proj_r.at[side, row], loc.at[0])
    g_load = pltpu.make_async_copy(g_hbm, g_in, loc.at[1])
    g_load.start()
    for t, src in enumerate((q_hbm, k_hbm, v_hbm)):
        pltpu.make_async_copy(src, qkv_in.at[t], loc.at[2]).start()
    own_proj.start()
    pltpu.make_async_copy(chosen, kept_out, loc.at[11]).start()

    def chosen_rows(load):
        total = None
        for j, mark in enumerate(marks):
            term = load(slice(j * block, (j + 1) * block)).astype(jnp.float32) * mark
            total = term if total is None else total + term
        return total.astype(bf16)

    def arrived(view, recv):
        ctx_copy(view, view, s_proj, recv, pair).wait_recv()

    def sent(view, send):
        ctx_copy(view, view, send, r_pp, pair).wait_send()

    with scope("B_barrier"):
        pl.semaphore_wait(barrier, n - 1 + dn - 1)

    own_block = proj_r.at[side, row]
    for a in [partner] + mates:
        ctx_copy(proj, own_block, s_proj, proj_rs.at[row], 2 * a + side).start()

    with scope("A_loadg"):
        pick.wait()
        marks = block_marks(picked, me, qkv_in.shape[1] // block)
        g_load.wait()
        for j in range(dn):
            g[j] = chosen_rows(lambda r: g_in[r, j * dc:(j + 1) * dc])
        g_r[side, md] = g[md]
    twin = md + 1 - 2 * lax.rem(md, 2)
    dp_far = [lax.rem(md + 2 * s, dn) for s in range(1, dn // 2)]
    dp_cross = [lax.rem(twin + 2 * s, dn) for s in range(1, dn // 2)]

    for peer in dp_far + dp_cross + [twin]:
        dp_copy(g.at[peer], g_r.at[side, md], s_g, g_rs.at[md], peer).start()
    ctx_copy(g.at[md], g_r.at[side, md], s_gp, r_gp, pair).start()
    with scope("A_loadqkv"):
        pltpu.make_async_copy(qkv_in, qkv_in, loc.at[2]).wait()
        for t in range(3):
            for h in range(n):
                qkv[h, t] = chosen_rows(lambda r: qkv_in[t, r, h * dh:(h + 1) * dh])
        qkv_r[me] = qkv[me]

    def send_qkv(peers):
        for peer in peers:
            ctx_copy(qkv.at[peer], qkv_r.at[me], s_qkv, r_qkv, peer).start()

    send_qkv([2 * a + side for a in [partner] + mate_partners])

    down = lax.broadcasted_iota(jnp.int32, (block, block), 0)
    for j in range(n):
        entry = picked[0, j]
        kpos[j * block:(j + 1) * block] = down + jnp.where(entry >= 0, entry * block, FAR)

    def proj_arrived(a):
        arrived(proj_r.at[side, a], proj_rs.at[a])

    with scope("C_waitg"):
        for peer in [twin] + dp_far + dp_cross:
            view = g_r.at[side, peer]
            arrived(view, g_rs.at[peer])
            ctx_copy(view, view, s_gp, r_gp, pair).start()
    with scope("D_waitpartner"):
        proj_arrived(partner)
        view = proj_r.at[side, partner]
        for a in mates:
            ctx_copy(view, view, s_pass, proj_rs.at[partner], 2 * a + side).start()
    send_qkv([2 * a + other for a in [partner] + mate_partners])
    send_qkv([2 * a + s for a in mates for s in (side, other)] + [pair])
    own_proj.wait()

    def part(a, b):
        k = 2 * a + b
        out = dot_nt(g_r[b].reshape(dn * block, dc), proj_r[side, a]).astype(bf16)
        agp_s[k] = out.reshape(dn, block, dh)
        for peer in dp_far + dp_cross + [twin]:
            dp_copy(agp_s.at[k, peer], agp_r.at[k, md], s_agp, agp_rs.at[k], peer).start()

    def finish(a, b):
        k = 2 * a + b
        arrived(agp_r.at[k, pl.ds(0, dn - 1)], agp_rs.at[k])
        total = agp_s[k, md].astype(jnp.float32)
        for peer in dp_peers:
            total = total + agp_r[k, peer].astype(jnp.float32)
        if a is row:
            ag_r[2 * row + b] = total.astype(bf16)
        else:
            ag_s[k] = total.astype(bf16)
            ctx_copy(ag_s.at[k], ag_r.at[2 * row + b], s_ag, ag_rs.at[row], 2 * a + side).start()

    def parts(names, b, waiting, lag):
        for a in names:
            with scope("G_part"):
                part(a, b)
            waiting.append((a, b))
            if len(waiting) > lag:
                with scope("H_finish"):
                    finish(*waiting.pop(0))

    waiting = []
    with scope("E_waitmate"):
        for a in mates:
            proj_arrived(a)
    parts([partner] + mates + [row], side, waiting, n)
    with scope("F_waitpairg"):
        arrived(g_r.at[other], r_gp)
    parts([partner] + mates + [row], other, waiting, n)
    with scope("F_waitsecond"):
        for a in mate_partners:
            proj_arrived(a)
    for b in (side, other):
        parts(mate_partners, b, waiting, rows)
    with scope("H_finish"):
        for a, b in waiting:
            finish(a, b)
    ctx_copy(proj_r.at[side], proj_r.at[side], s_pp, r_pp, pair).start()

    with scope("I_waitqkv"):
        arrived(qkv_r.at[pl.ds(0, n - 1)], r_qkv)
    k_t[...] = transposed(qkv_r[:, 1].reshape(slots, dh))
    v_t[...] = transposed(qkv_r[:, 2].reshape(slots, dh))

    def ordered(k):
        late = k // half
        return far_base * (1 - late) + own_base * late + lax.rem(row + k + late, half)

    def forward(k, carry):
        i = ordered(k)
        q = qkv_r[pl.ds(2 * i, 2), 0].reshape(width, dh)
        keys = qkv_r[:, 1].reshape(slots, dh)
        scores = dot_nt(keys, q)
        key_pos = kpos[...]
        key_pos = jnp.concatenate([key_pos, key_pos], axis=1)
        lane = lax.broadcasted_iota(jnp.int32, (1, width), 1)
        one, two = picked[0, 2 * i], picked[0, 2 * i + 1]
        one = jnp.where(one >= 0, one * block, -FAR)
        two = jnp.where(two >= 0, (two - 1) * block, -FAR)
        query_pos = lane + jnp.where(lane < block, one, two)
        scores = jnp.where(key_pos <= query_pos, scores * (scale * LOG2E), -1e30)
        e = jnp.exp2(scores - jnp.max(scores, axis=0, keepdims=True))
        p = (e * (1.0 / jnp.sum(e, axis=0, keepdims=True))).astype(bf16)
        p_s[i] = p
        a_t = dot_nn(v_t[...], p)
        attn_t[i] = a_t.astype(bf16)
        attn_s[i] = a_t.T.astype(bf16)

        @pl.when(k < half)
        def _():
            ctx_copy(attn_s.at[i], attn_r.at[row], s_attn, r_attn0, 2 * i + side).start()

        @pl.when((k >= half) & (k < rows - 1))
        def _():
            ctx_copy(attn_s.at[i], attn_r.at[row], s_attn, r_attn1, 2 * i + side).start()

        @pl.when(k == rows - 1)
        def _():
            pltpu.make_async_copy(attn_s.at[i], attn_r.at[i], loc.at[3]).start()

        return carry

    with scope("J_forward"):
        lax.fori_loop(0, rows, forward, 0)

    dk_acc[...] = jnp.zeros_like(dk_acc)
    dv_acc[...] = jnp.zeros_like(dv_acc)

    def heads_of_me(ref):
        return ref.at[:, pl.ds(pl.multiple_of(me * dh, dh), dh)]

    def backward(k, carry):
        i = ordered(k)
        with scope("K_waitag"):
            @pl.when(k < rows - 1)
            def _():
                arrived(ag_r.at[pl.ds(2 * i, 2)], ag_rs.at[i])

        q = qkv_r[pl.ds(2 * i, 2), 0].reshape(width, dh)
        v = qkv_r[:, 2].reshape(slots, dh)
        da = ag_r[pl.ds(2 * i, 2)].reshape(width, dh)
        delta = jnp.sum(da.astype(jnp.float32).T * attn_t[i].astype(jnp.float32), axis=0, keepdims=True)
        p = p_s[i]
        ds = (p.astype(jnp.float32) * (dot_nt(v, da) - delta)).astype(bf16)
        dq_t = dot_nn(k_t[...], ds) * scale
        dq_s[pl.ds(2 * i, 2)] = dq_t.T.astype(bf16).reshape(2, block, dh)
        for t in range(2):
            peer = 2 * i + t

            @pl.when(peer != me)
            def _():
                ctx_copy(dq_s.at[peer], heads_of_me(dq_r), s_dq, r_dq, peer).start()

            @pl.when(peer == me)
            def _():
                pltpu.make_async_copy(dq_s.at[peer], heads_of_me(dq_r), loc.at[4]).start()

        dk_acc[...] += dot_nn(ds, q)
        dv_acc[...] += dot_nn(p, da)
        return carry

    with scope("L_backward"):
        lax.fori_loop(0, rows, backward, 0)

    dkv_s[:, 0] = (dk_acc[...] * scale).astype(bf16).reshape(n, block, dh)
    dkv_s[:, 1] = dv_acc[...].astype(bf16).reshape(n, block, dh)

    my_dkv = dkv_r.at[:, :, pl.ds(pl.multiple_of(me * dh, dh), dh)]

    def send_dkv(peers):
        for peer in peers:
            ctx_copy(dkv_s.at[peer], my_dkv, s_dkv, r_dkv, peer).start()

    far_rows = [k + (rows - 1 - 2 * k) * (1 - row // half) for k in range(half)]
    own_dkv = pltpu.make_async_copy(dkv_s.at[me], my_dkv, loc.at[5])
    own_dkv.start()

    def spread(src, dst_of, send, recv, own_sem):
        for s, peer in enumerate(dp_far):
            dp_copy(src, dst_of(md), send, recv.at[1 + s], peer).start()
        dp_copy(src, dst_of(md), send, recv.at[0], twin).start()
        copy = pltpu.make_async_copy(src, dst_of(md), own_sem)
        copy.start()
        return copy

    def hand_over(dst_of, send, recv):
        for s in range(1, dn // 2):
            peer = lax.rem(md + dn - 2 * s, dn)
            arrived(dst_of(peer), recv.at[s])
            dp_copy(dst_of(peer), dst_of(peer), send, recv.at[0], twin).start()

    groups = [pl.ds(far_base, half), pl.ds(own_base, half)]
    with scope("M_waitattn"):
        arrived(attn_r.at[groups[0]], r_attn0)
    own_far = spread(attn_r.at[groups[0]], lambda d: attn_d.at[0, d, pl.ds(0, half)], s_ad, ad_rs.at[0], loc.at[6])
    with scope("M_waitattn"):
        if half > 1:
            arrived(attn_r.at[pl.ds(0, half - 1)], r_attn1)
        pltpu.make_async_copy(attn_s.at[row], attn_r.at[row], loc.at[3]).wait()
    own_near = spread(attn_r.at[groups[1]], lambda d: attn_d.at[1, d, pl.ds(0, half)], s_ad, ad_rs.at[1], loc.at[7])
    ctx_copy(attn_r.at[:, pl.ds(pl.multiple_of(other * block, block), block)], attn_y, s_ap, r_ap, pair).start()

    inner = lax.rem(row, half) == (half - 1) * (1 - row // half)

    send_dkv([2 * a + s for s in (side, other) for a in far_rows + mates] + [pair])
    def weight(t, a):
        total = None
        for b in range(2):
            heads_of = attn_d[t, :, lax.rem(a, half), b * block:(b + 1) * block].reshape(dn * block, dh)
            term = dot_nn(transposed(heads_of), g_r[b].reshape(dn * block, dc))
            total = term if total is None else total + term
        return total

    def send_w(slot, value, dst, recv, peer_row):
        w_s[slot] = value.astype(bf16)
        ctx_copy(w_s.at[slot], dst, s_w, recv, 2 * peer_row + side).start()

    def spread_done(t, own):
        own.wait()
        arrived(attn_d.at[t, pl.ds(0, dn // 2)], ad_rs.at[t, 0])

    with scope("N_handover0"):
        hand_over(lambda d: attn_d.at[0, d, pl.ds(0, half)], s_ad, ad_rs.at[0])
    with scope("N_waitpair"):
        arrived(attn_y, r_ap)
    own_ae = spread(attn_y, lambda d: attn_e.at[d], s_ae, ae_rs, loc.at[8])
    with scope("N_handover1"):
        hand_over(lambda d: attn_d.at[1, d, pl.ds(0, half)], s_ad, ad_rs.at[1])
    with scope("N_waitspread0"):
        spread_done(0, own_far)
    with scope("P_weight"):
        for k, a in enumerate(far_rows):
            w_c[k] = weight(0, a)

        @pl.when(jnp.logical_not(inner))
        def _():
            for k in range(half):
                send_w(k, w_c[k], w_x.at[lax.rem(row, half), k], r_wx, own_base + (half - 1) * (1 - row // half))
    with scope("N_waitspread1"):
        spread_done(1, own_near)
    with scope("P_weight"):
        for k, a in enumerate(mates):
            send_w(half + k, weight(1, a), w_m.at[row], r_wm, a)
        w_out[...] = weight(1, row)
    def cross_sum():
        if mates:
            arrived(w_x.at[pl.ds(0, half - 1)], r_wx)
        for k, a in enumerate(far_rows):
            total = w_c[k]
            for mate in mates:
                total = total + w_x[lax.rem(mate, half), k].astype(jnp.float32)
            send_w(k, total, w_p, r_wp, a)

    with scope("O_handover"):
        hand_over(lambda d: attn_e.at[d], s_ae, ae_rs)
    with scope("S_waitinner"):
        pl.when(inner)(cross_sum)
    mine = pl.ds(pl.multiple_of(side * block, block), block)

    def two(ref, *at):
        return ref[at].reshape(width, dh)

    def mix_here(j, carry):
        d = pl.ds(2 * j, 2)
        t_of = [row // half if a // half else 1 - row // half for a in range(rows)]
        here = jnp.concatenate([two(attn_d, t_of[a], d, a % half, mine) for a in range(rows)], axis=1)
        mix_acc[j] = dot_nn(here, proj_r[side].reshape(rows * dh, dc))
        return carry

    with scope("Q_here"):
        lax.fori_loop(0, dn // 2, mix_here, 0)
    with scope("O_waitrows"):
        arrived(proj_r.at[other], r_pp)
        own_ae.wait()
        arrived(attn_e.at[pl.ds(0, dn // 2)], ae_rs.at[0])

    def mix_step(k, carry):
        j = lax.rem(md // 2 + 1 + k, dn // 2)

        d = pl.ds(2 * j, 2)
        there = jnp.concatenate([two(attn_e, d, a) for a in range(rows)], axis=1)
        out = mix_acc[j] + dot_nn(there, proj_r[other].reshape(rows * dh, dc))
        mix_s[d] = out.astype(bf16).reshape(2, block, dc)
        for t in range(2):
            peer = 2 * j + t

            @pl.when(peer != md)
            def _():
                dp_copy(mix_s.at[peer], my_columns, s_mix, r_mix, peer).start()

            @pl.when(peer == md)
            def _():
                pltpu.make_async_copy(mix_s.at[peer], my_columns, loc.at[9]).start()

        return carry

    my_columns = mix_r.at[:, pl.ds(pl.multiple_of(md * dc, dc), dc)]
    with scope("Q_mix"):
        lax.fori_loop(0, dn // 2, mix_step, 0)

    with scope("T_waitdq"):
        pltpu.make_async_copy(dq_s.at[me], heads_of_me(dq_r), loc.at[4]).wait()
        arrived(dq_r.at[:, pl.ds(0, (n - 1) * dh)], r_dq)
    with scope("U_waitdkv"):
        own_dkv.wait()
        arrived(dkv_r.at[:, :, pl.ds(0, (n - 1) * dh)], r_dkv)
    with scope("W_waitmates"):
        if mates:
            arrived(w_m.at[pl.ds(0, half - 1)], r_wm)
        for a in mates:
            w_out[...] += w_m[a].astype(jnp.float32)
    with scope("X_waitpartner"):
        arrived(w_p, r_wp)
        w_out[...] += w_p[...].astype(jnp.float32)
    with scope("V_waitmix"):
        pltpu.make_async_copy(mix_s.at[md], my_columns, loc.at[9]).wait()
        arrived(mix_r.at[:, pl.ds(0, (dn - 1) * dc)], r_mix)

    pltpu.make_async_copy(chosen, kept_out, loc.at[11]).wait()
    with scope("Y_waitsend"):
        blocks = pl.ds(0, n - 1)
        others = pl.ds(0, dn - 1)
        sent(qkv_r.at[pl.ds(0, n - 1)], s_qkv)
        sent(proj_r.at[0, pl.ds(0, half)], s_proj)
        if mates:
            sent(proj_r.at[0, pl.ds(0, half - 1)], s_pass)
        sent(proj_r.at[0], s_pp)
        sent(g.at[others], s_g)
        sent(agp_s.at[:, others], s_agp)
        sent(ag_s.at[pl.ds(0, n - 2)], s_ag)
        sent(g_r.at[0], s_gp)
        sent(attn_s.at[pl.ds(0, rows - 1)], s_attn)
        sent(dq_s.at[blocks], s_dq)
        sent(dkv_s.at[blocks], s_dkv)
        sent(attn_d.at[:, others], s_ad)
        sent(attn_y, s_ap)
        sent(attn_e.at[others], s_ae)
        sent(w_s.at[pl.ds(0, rows - 1)], s_w)
        sent(mix_s.at[others], s_mix)


def shards(queries, keys, values, out_grad, chosen, proj):
    n = lax.axis_size("ctx")
    dn = lax.axis_size("dp")
    tokens = queries.shape[1]
    hd = queries.shape[2]
    dh = hd // n
    dc = proj.shape[1]
    slots = n * BLOCK
    width = 2 * BLOCK
    rows = n // 2
    half = rows // 2
    bf16, f32 = jnp.bfloat16, jnp.float32
    sem = pltpu.SemaphoreType.DMA
    blocks = (n, BLOCK, dh)
    pairs = (rows, width, dh)
    sheets = (rows, dh, dc)
    buffers = [
        ((3, tokens, hd), bf16), ((tokens, dn * dc), bf16), ((n, 3, BLOCK, dh), bf16), ((dn, BLOCK, dc), bf16),
        ((slots, BLOCK), jnp.int32), ((n, 3, BLOCK, dh), bf16), ((2, dn, BLOCK, dc), bf16), ((2,) + sheets, bf16),
        ((n, dn, BLOCK, dh), bf16), ((n, dn, BLOCK, dh), bf16), (blocks, bf16), (blocks, bf16),
        (pairs, bf16), (pairs, bf16), ((rows, BLOCK, dh), bf16), ((2, dn, half, width, dh), bf16),
        ((dn, rows, BLOCK, dh), bf16), ((rows, dh, width), bf16),
        ((rows, slots, width), bf16), ((dh, slots), bf16), ((dh, slots), bf16),
        (blocks, bf16), ((n, 2, BLOCK, dh), bf16), ((slots, dh), f32), ((slots, dh), f32),
        ((half, dh, dc), f32), (sheets, bf16), ((half, half, dh, dc), bf16), (sheets, bf16), ((dh, dc), bf16), ((dn, BLOCK, dc), bf16),
        ((dn // 2, width, dc), f32),
    ]
    held = sum(math.prod(shape) * jnp.dtype(kind).itemsize for shape, kind in buffers)
    sems = [sem((16,)), sem((12,)), sem((rows,)), sem((dn,)), sem((n,)), sem((rows,)), sem((2, dn // 2)), sem((dn // 2,)), sem((12,))]
    vmem = pl.BlockSpec(memory_space=pltpu.VMEM)
    picks = pltpu.SMEM(chosen.shape, chosen.dtype)
    free = pl.BlockSpec(memory_space=pl.ANY)
    hbm = pl.BlockSpec(memory_space=pltpu.HBM)

    def kept(x):
        return pltpu.with_memory_space_constraint(x, pltpu.HBM)

    chosen = kept(chosen)
    dq, dkv, weight_grad, mixed, placed = pl.pallas_call(
        functools.partial(kernel, n, dn, 1.0 / math.sqrt(dh)),
        out_shape=(
            jax.ShapeDtypeStruct((BLOCK, hd), bf16),
            jax.ShapeDtypeStruct((2, BLOCK, hd), bf16),
            jax.ShapeDtypeStruct((dh, dc), f32),
            jax.ShapeDtypeStruct((BLOCK, dn * dc), bf16),
            jax.ShapeDtypeStruct(chosen.shape, chosen.dtype),
        ),
        in_specs=[hbm] * 6,
        out_specs=[free, free, vmem, free, free],
        scratch_shapes=[picks] + [pltpu.VMEM(shape, kind) for shape, kind in buffers] + sems,
        compiler_params=pltpu.CompilerParams(
            collective_id=0, has_side_effects=True, vmem_limit_bytes=min(held + SPARE, 60 * MIB)),
    )(chosen, *[kept(x) for x in (queries[0], keys[0], values[0], out_grad[0], proj)])

    wide = (tokens, dn * dc)
    thin = (tokens, hd)
    count = tokens // BLOCK
    out, q_grad, k_grad, v_grad, proj_grad = pl.pallas_call(
        functools.partial(place_kernel, count),
        out_shape=(
            jax.ShapeDtypeStruct(wide, bf16), jax.ShapeDtypeStruct(thin, bf16), jax.ShapeDtypeStruct(thin, bf16),
            jax.ShapeDtypeStruct(thin, bf16), jax.ShapeDtypeStruct((dh, dc), f32)),
        in_specs=[vmem] + [free] * 4,
        out_specs=[hbm] * 5,
        scratch_shapes=[pltpu.VMEM((BLOCK, max(dn * dc, hd)), bf16), sem((count, 4)), sem((1,))],
        compiler_params=pltpu.CompilerParams(vmem_limit_bytes=8 * MIB),
    )(placed, mixed, dq, dkv, weight_grad)
    return out[None], q_grad[None], k_grad[None], v_grad[None], proj_grad


def solution(mesh):
    rows = P("dp", "ctx", None)
    return jax.shard_map(
        shards,
        mesh=mesh,
        in_specs=(rows, rows, rows, rows, P("dp", None), P("ctx", "dp")),
        out_specs=(rows, rows, rows, rows, P("ctx", "dp")),
        check_vma=False,
    )
```
